32 devices in a mesh: dp: 16 (over z, x, core), tensor: 2 (over y).
Axes of the slice: x: 2, y: 2, z: 4, core: 2. Of those that a mesh axis runs over, the one named last changes fastest.
Arguments:
- tokens: bfloat16 [32, 512, 768], P('dp', 'tensor'), may hold values from -6 to 6
- cotangent: bfloat16 [32, 512, 768], P('dp', 'tensor'), may hold values from -6 to 6
- lengths: int32 [32], replicated, may hold values from 1 to 512, 10240 in all
- slot_order: int32 [32], replicated, may hold values from 0 to 31, each once
- query_weight: bfloat16 [768, 768], P('dp', 'tensor'), may hold values from -0.21875 to 0.21875
- key_weight: bfloat16 [768, 768], P('dp', 'tensor'), may hold values from -0.21875 to 0.21875
- value_weight: bfloat16 [768, 768], P('dp', 'tensor'), may hold values from -0.21875 to 0.21875
- out_weight: bfloat16 [768, 768], P('dp', 'tensor'), may hold values from -1.5 to 1.5
- up_weight: bfloat16 [768, 3072], P('dp', 'tensor'), may hold values from -0.21875 to 0.21875
- down_weight: bfloat16 [768, 3072], P('dp', 'tensor'), may hold values from -0.109375 to 0.109375
- query_bias: float32 [768], P('tensor'), may hold values from -3 to 3
- value_bias: float32 [768], P('tensor'), may hold values from -0.3 to 0.3
- out_bias: float32 [768], replicated, may hold values from -3 to 3
- up_bias: float32 [3072], P('tensor'), may hold values from -3 to 3
- down_bias: float32 [768], replicated, may hold values from -3 to 3
- first_gain: float32 [768], replicated, may hold values from 0.5 to 1.5
- first_offset: float32 [768], replicated, may hold values from -3 to 3
- second_gain: float32 [768], replicated, may hold values from 0.5 to 1.5
- second_offset: float32 [768], replicated, may hold values from -3 to 3
Outputs:
- layer_out: bfloat16 [32, 512, 768], P('dp', 'tensor')
- input_grad: bfloat16 [32, 512, 768], P('dp', 'tensor')
- query_weight_grad: float32 [768, 768], P('dp', 'tensor')
- key_weight_grad: float32 [768, 768], P('dp', 'tensor')
- value_weight_grad: float32 [768, 768], P('dp', 'tensor')
- out_weight_grad: float32 [768, 768], P('dp', 'tensor')
- up_weight_grad: float32 [768, 3072], P('dp', 'tensor')
- down_weight_grad: float32 [768, 3072], P('dp', 'tensor')
- query_bias_grad: float32 [768], P('tensor')
- value_bias_grad: float32 [768], P('tensor')
- out_bias_grad: float32 [768], replicated
- up_bias_grad: float32 [3072], P('tensor')
- down_bias_grad: float32 [768], replicated
- first_gain_grad: float32 [768], replicated
- first_offset_grad: float32 [768], replicated
- second_gain_grad: float32 [768], replicated
- second_offset_grad: float32 [768], replicated
The draws below stay inside these ranges and needn't reach their ends.
Inputs may be any that keep to these rules, and one draw needn't show every extreme that they name: The lengths of the 32 sequences sum to 10240, and the longest is exactly 512. `slot_order`: every sequence is held by exactly one slot.
All inputs are finite; a program needn't handle non-finite values.
Results may differ from the reference program's by a relative error of at most 0.017.
Values may be sent and summed in bfloat16 or wider, within the bound.
No kernel may reach another device: no remote copies, remote signals or barrier semaphores. Data moves between devices by JAX's collectives and lax.ppermute only.
A program may use at most 128 MiB of HBM per device.

```python
import math
import jax
import jax.numpy as jnp
import numpy as np
from jax import lax

D = 768
HEADS = 12
HEAD = 64
FF = 3072
SEQ_LEN = 512
SEQS = 32
TOTAL = 10240


def block_levels(own_key, shape, shards, least, top_value):
    def one(axis_at, shards_of):
        draws = jax.random.uniform(jax.random.fold_in(jax.random.fold_in(own_key, 6), axis_at), (shards_of,), jnp.float32, least / len(shards), top_value / len(shards))
        return jnp.repeat(jnp.exp(draws), shape[axis_at] // shards_of).reshape((-1,) + (1,) * (len(shape) - axis_at - 1))

    level = one(*shards[0])
    for cut in shards[1:]:
        level = level * one(*cut)
    return level


def length_profile(amount, total, bound, skew):
    portions = [(1 << 20) // math.isqrt(standing ** skew) + 1 for standing in range(2, amount + 1)]
    spare, given = total - bound - (amount - 1), [1] * (amount - 1)
    while spare > 0:
        free = [i for i in range(amount - 1) if given[i] < bound]
        pool, remaining = sum([portions[i] for i in free]), spare
        for i in free:
            extra = min(bound - given[i], max(1, remaining * portions[i] // pool), spare)
            given[i] = given[i] + extra
            spare = spare - extra
    return np.array([bound] + given)


def ragged_sizes(stream_key, count, total, bound, lean):
    if count == 2:
        one = jax.random.randint(stream_key, (), max(1, total - bound), min(bound, total - 1) + 1)
        return jnp.stack([one, total - one])
    tallies = jnp.asarray(length_profile(count, total, bound, lean), jnp.int32)
    pairs = (count - 1) // 2
    giver, taker = tallies[1:1 + 2 * pairs:2], tallies[2:2 + 2 * pairs:2]
    room = jnp.minimum(giver - 1, bound - taker)
    moved = jax.random.randint(jax.random.fold_in(stream_key, 1), (pairs,), 0, 1 << 20) % (room + 1)
    tallies = tallies.at[1:1 + 2 * pairs:2].set(giver - moved).at[2:2 + 2 * pairs:2].set(taker + moved)
    return tallies[jax.random.permutation(jax.random.fold_in(stream_key, 2), count)]


def bell_draw(key, extent, deviation, limit, pieces=(), kind=jnp.bfloat16):
    array = jax.random.normal(key, extent, jnp.float32) * deviation
    if len(pieces) > 0:
        array = block_levels(key, extent, pieces, -0.22, 0.18) * array
    return jnp.clip(array, min=-limit, max=limit).astype(kind)


def setup_inputs(seed: int = 0) -> dict:
    streams_of = jax.random.split(jax.random.key(seed), 20)
    tokens = bell_draw(streams_of[0], (SEQS, SEQ_LEN, D), 1.0, 6.0, ((0, 16), (1, 2)))
    cotangent = bell_draw(streams_of[1], (SEQS, SEQ_LEN, D), 1.0, 6.0, ((0, 16), (1, 2)))
    lengths = ragged_sizes(streams_of[2], SEQS, TOTAL, SEQ_LEN, 2).astype(jnp.int32)
    slot_order = jax.random.permutation(streams_of[3], SEQS).astype(jnp.int32)
    query_weight = bell_draw(streams_of[4], (D, D), D ** -0.5, 0.21875, ((0, 16), (1, 2)))
    key_weight = bell_draw(streams_of[5], (D, D), D ** -0.5, 0.21875, ((0, 16), (1, 2)))
    value_weight = bell_draw(streams_of[6], (D, D), D ** -0.5, 0.21875, ((0, 16), (1, 2)))
    out_weight = bell_draw(streams_of[7], (D, D), 16 ** -0.5, 1.5, ((0, 16), (1, 2)))
    up_weight = bell_draw(streams_of[8], (D, FF), D ** -0.5, 0.21875, ((0, 16), (1, 2)))
    down_weight = bell_draw(streams_of[9], (D, FF), FF ** -0.5, 0.109375, ((0, 16), (1, 2)))
    query_bias = bell_draw(streams_of[10], (D,), 0.5, 3.0, ((0, 2),), jnp.float32)
    value_bias = bell_draw(streams_of[11], (D,), 0.05, 0.3, ((0, 2),), jnp.float32)
    out_bias = bell_draw(streams_of[12], (D,), 0.5, 3.0, (), jnp.float32)
    up_bias = bell_draw(streams_of[13], (FF,), 0.5, 3.0, ((0, 2),), jnp.float32)
    down_bias = bell_draw(streams_of[14], (D,), 0.5, 3.0, (), jnp.float32)
    first_gain = jnp.clip(1.0 + 0.1 * jax.random.normal(streams_of[15], (D,), jnp.float32), 0.5, 1.5)
    first_offset = bell_draw(streams_of[16], (D,), 0.5, 3.0, (), jnp.float32)
    second_gain = jnp.clip(1.0 + 0.1 * jax.random.normal(streams_of[17], (D,), jnp.float32), 0.5, 1.5)
    second_offset = bell_draw(streams_of[18], (D,), 0.5, 3.0, (), jnp.float32)
    return dict(tokens=tokens, cotangent=cotangent, lengths=lengths, slot_order=slot_order, query_weight=query_weight, key_weight=key_weight, value_weight=value_weight, out_weight=out_weight, up_weight=up_weight, down_weight=down_weight, query_bias=query_bias, value_bias=value_bias, out_bias=out_bias, up_bias=up_bias, down_bias=down_bias, first_gain=first_gain, first_offset=first_offset, second_gain=second_gain, second_offset=second_offset)


EPSILON = 1e-05
PRECISE = lax.Precision.HIGHEST

@jax.custom_vjp
def low(v):
    return lax.optimization_barrier(v.astype(jnp.bfloat16)).astype(jnp.float32)

@jax.custom_vjp
def low_back(v):
    return v

def low_keep(v):
    return (low(v), None)

def low_pass(kept, grad):
    return (grad,)

def back_keep(v):
    return (v, None)

def back_low(kept, grad):
    return (low(grad),)
low.defvjp(low_keep, low_pass)
low_back.defvjp(back_keep, back_low)

def round_both(value_in):
    return low_back(low(value_in))

def norm_apply(inputs, norm_gain, offset):
    center = inputs - lax.optimization_barrier(jnp.mean(inputs, axis=-1, keepdims=True))
    rscale = lax.rsqrt(lax.optimization_barrier(jnp.mean(center * center, axis=-1, keepdims=True)) + EPSILON)
    return center * rscale * norm_gain + offset

def attend_one(operands):
    query_rows, key_rows, value_rows, key_live = operands
    scores = low_back(jnp.einsum('qhd,khd->hqk', query_rows, key_rows, precision=PRECISE)) * HEAD ** (-0.5)
    scores = jnp.where(key_live[None, None, :], scores, -1000000000.0)
    raised = jnp.exp(scores - lax.optimization_barrier(jnp.max(scores, axis=-1, keepdims=True)))
    attn_probs = raised / lax.optimization_barrier(jnp.sum(raised, axis=-1, keepdims=True))
    mixed = jnp.einsum('hqk,khd->qhd', low(attn_probs), value_rows, precision=PRECISE)
    return round_both(mixed.reshape(mixed.shape[0], HEADS * HEAD))

def project(left_side, weight):
    return jnp.einsum('gld,dx->glx', left_side, weight, precision=PRECISE)

def project_back(left_side, weight):
    return jnp.einsum('glx,dx->gld', left_side, weight, precision=PRECISE)

def layer_forward(params, seq_group, group_lens):
    query_weight, key_weight, value_weight, out_weight, up_weight, down_weight, query_bias, value_bias, out_bias, up_bias, down_bias, first_gain, first_offset, second_gain, second_offset = params
    group_size = seq_group.shape[0]
    positions = jnp.arange(SEQ_LEN, dtype=jnp.int32)
    key_live = positions[None, :] < group_lens[:, None]
    split_shape = (group_size, SEQ_LEN, HEADS, HEAD)
    queries = round_both(project(seq_group, query_weight) + query_bias)
    key_rows = round_both(project(seq_group, key_weight))
    values = round_both(project(seq_group, value_weight) + value_bias)
    attended = lax.map(jax.checkpoint(attend_one), (queries.reshape(split_shape), key_rows.reshape(split_shape), values.reshape(split_shape), key_live))
    attn_out = low_back(project_back(attended, out_weight) + out_bias)
    normed = norm_apply(seq_group + attn_out, first_gain, first_offset)
    hidden = low_back(project(low(normed), up_weight) + up_bias)
    ffn_out = low_back(project_back(low(jax.nn.gelu(hidden, approximate=False)), down_weight) + down_bias)
    final_norm = norm_apply(normed + ffn_out, second_gain, second_offset)
    return final_norm * key_live[:, :, None].astype(jnp.float32)

def reference(tokens, cotangent, lengths, slot_order, query_weight, key_weight, value_weight, out_weight, up_weight, down_weight, query_bias, value_bias, out_bias, up_bias, down_bias, first_gain, first_offset, second_gain, second_offset):
    params = tuple((item.astype(jnp.float32) for item in (query_weight, key_weight, value_weight, out_weight, up_weight, down_weight, query_bias, value_bias, out_bias, up_bias, down_bias, first_gain, first_offset, second_gain, second_offset)))
    group_count = SEQS // 4
    slot_tokens = jnp.take(tokens, slot_order, axis=0).astype(jnp.float32)
    slot_lens = jnp.take(lengths, slot_order)
    grouped = slot_tokens.reshape(group_count, 4, SEQ_LEN, D)
    cot_groups = cotangent.astype(jnp.float32).reshape(group_count, 4, SEQ_LEN, D)
    len_groups = slot_lens.reshape(group_count, 4)

    def visit(totals, operands):
        seq_group, cot_group, group_lens = operands

        def forward_group(param_set, group_rows):
            return layer_forward(param_set, group_rows, group_lens)
        result, pullback = jax.vjp(forward_group, params, seq_group)
        grad_params, grad_tokens = pullback(cot_group)
        totals = jax.tree.map(jnp.add, totals, grad_params)
        return (totals, (result.astype(jnp.bfloat16), grad_tokens))
    zero_grads = jax.tree.map(jnp.zeros_like, params)
    totals, (layer_out, slot_grads) = lax.scan(visit, zero_grads, (grouped, cot_groups, len_groups))
    layer_out = layer_out.reshape(SEQS, SEQ_LEN, D)
    slot_grads = slot_grads.reshape(SEQS, SEQ_LEN, D)
    input_grad = jnp.zeros_like(slot_grads).at[slot_order].set(slot_grads).astype(jnp.bfloat16)
    return (layer_out, input_grad, totals[0], totals[1], totals[2], totals[3], totals[4], totals[5], totals[6], totals[7], totals[8], totals[9], totals[10], totals[11], totals[12], totals[13], totals[14])
```

```python
import jax
import jax.numpy as jnp
from jax import lax
from jax.experimental import pallas as pl
from jax.experimental.pallas import tpu as pltpu
from jax.sharding import PartitionSpec as P

HEAD = 64
EPSILON = 1e-05
SQRT_HALF = 0.7071067811865476
INV_ROOT_TWO_PI = 0.3989422804014327
BOTH = ("dp", "tensor")
F32 = jnp.float32
BF16 = jnp.bfloat16


def norm_forward(inputs, gain, offset):
    center = inputs - jnp.mean(inputs, axis=-1, keepdims=True)
    rscale = lax.rsqrt(jnp.mean(center * center, axis=-1, keepdims=True) + EPSILON)
    normal = center * rscale
    return normal * gain + offset, normal, rscale


def norm_backward(incoming, normal, rscale, gain):
    scaled = incoming * gain
    inner = (
        scaled
        - jnp.mean(scaled, axis=-1, keepdims=True)
        - normal * jnp.mean(scaled * normal, axis=-1, keepdims=True)
    )
    return rscale * inner, jnp.sum(incoming * normal, axis=0), jnp.sum(incoming, axis=0)


def gelu(v):
    return 0.5 * v * (1.0 + lax.erf(v * SQRT_HALF))


def gelu_slope(v):
    return 0.5 * (1.0 + lax.erf(v * SQRT_HALF)) + v * jnp.exp(-0.5 * v * v) * INV_ROOT_TWO_PI


def dot_nn(a, b):
    return jnp.dot(a, b, preferred_element_type=F32)


def dot_tn(a, b):
    return lax.dot_general(a, b, (((0,), (0,)), ((), ())), preferred_element_type=F32)


def dot_nt(a, b):
    return lax.dot_general(a, b, (((1,), (1,)), ((), ())), preferred_element_type=F32)


def gather_weight(shard):
    tensor_size = lax.axis_size("tensor")
    rows, cols = shard.shape
    got = lax.all_gather(shard, BOTH, axis=0, tiled=False)
    got = got.reshape(-1, tensor_size, rows, cols)
    return got.transpose(0, 2, 1, 3).reshape(-1, tensor_size * cols)


def scatter_grad(grad, rows, cols):
    tensor_size = lax.axis_size("tensor")
    parts = grad.reshape(-1, rows, tensor_size, cols).transpose(0, 2, 1, 3)
    parts = parts.reshape(-1, cols).astype(BF16)
    return lax.psum_scatter(parts, BOTH, scatter_dimension=0, tiled=True).astype(F32)


def pick_kernel(order, src, dst, sems):
    def copy(t):
        return pltpu.make_async_copy(src.at[order[t]], dst.at[t], sems.at[t])

    count = dst.shape[0]
    for t in range(count):
        copy(t).start()
    for t in range(count):
        copy(t).wait()


def pick(pieces, order):
    return pl.pallas_call(
        pick_kernel,
        out_shape=jax.ShapeDtypeStruct(pieces.shape, pieces.dtype),
        in_specs=[pl.BlockSpec(memory_space=pltpu.SMEM), pl.BlockSpec(memory_space=pl.ANY)],
        out_specs=pl.BlockSpec(memory_space=pl.ANY),
        scratch_shapes=[pltpu.SemaphoreType.DMA((pieces.shape[0],))],
        name="pick",
    )(order, pieces)


def slots_to_initial(block, inverse):
    micro, half, features = block.shape
    dp, tensor_size = lax.axis_size("dp"), lax.axis_size("tensor")
    piece = half // dp
    spread = lax.all_to_all(
        block.reshape(micro, dp, piece, features), "dp", split_axis=1, concat_axis=0, tiled=True
    ).reshape(micro * dp, piece, features)
    chosen = pick(spread, inverse)
    got = lax.all_to_all(chosen, BOTH, split_axis=0, concat_axis=0, tiled=True)
    return got.reshape(dp, tensor_size, piece, features).transpose(1, 0, 2, 3).reshape(-1, features)


def initial_to_slots(rows, slot_order, micro):
    dp, tensor_size = lax.axis_size("dp"), lax.axis_size("tensor")
    features = rows.shape[-1]
    piece = rows.shape[0] // (dp * tensor_size)
    pieces = rows.reshape(tensor_size, dp, piece, features).transpose(1, 0, 2, 3)
    got = lax.all_to_all(
        pieces.reshape(-1, piece, features), BOTH, split_axis=0, concat_axis=0, tiled=True
    )
    chosen = pick(got, slot_order)
    back = lax.all_to_all(chosen, "dp", split_axis=0, concat_axis=0, tiled=True)
    back = back.reshape(dp, micro, piece, features).transpose(1, 0, 2, 3)
    return back.reshape(micro, dp * piece, features)


def on_device(
    tokens, cotangent, lengths, slot_order,
    query_weight, key_weight, value_weight, out_weight, up_weight, down_weight,
    query_bias, value_bias, out_bias, up_bias, down_bias,
    first_gain, first_offset, second_gain, second_offset,
):
    micro, half, features = tokens.shape
    dp, tensor_size = lax.axis_size("dp"), lax.axis_size("tensor")
    dp_pos, tensor_pos = lax.axis_index("dp"), lax.axis_index("tensor")
    seq_len = half * tensor_size
    heads = features // HEAD
    slot_count = slot_order.shape[0]
    inverse = jnp.zeros_like(slot_order).at[slot_order].set(jnp.arange(slot_count, dtype=jnp.int32))
    live_len = lengths[dp_pos * tensor_size + tensor_pos]
    positions = jnp.arange(seq_len, dtype=jnp.int32)
    live = positions < live_len
    live_col = live.astype(F32)[:, None]

    x = lax.all_to_all(tokens, "tensor", split_axis=0, concat_axis=1, tiled=True)[0]
    wq, wk, wv, wo, wu, wd = (
        gather_weight(w)
        for w in (query_weight, key_weight, value_weight, out_weight, up_weight, down_weight)
    )
    bq = lax.all_gather(query_bias, "tensor", axis=0, tiled=True)
    bv = lax.all_gather(value_bias, "tensor", axis=0, tiled=True)
    bu = lax.all_gather(up_bias, "tensor", axis=0, tiled=True)
    cot = slots_to_initial(cotangent, inverse)

    split = (seq_len, heads, HEAD)
    scale = HEAD**-0.5
    q = (dot_nn(x, wq) + bq).astype(BF16).reshape(split)
    k = dot_nn(x, wk).astype(BF16).reshape(split)
    v = (dot_nn(x, wv) + bv).astype(BF16).reshape(split)
    s = jnp.einsum("qhd,khd->hqk", q, k, preferred_element_type=F32) * scale
    s = jnp.where(live[None, None, :], s, -1e9)
    row_max = jnp.max(s, axis=-1, keepdims=True)
    raised = jnp.exp(s - row_max)
    total = jnp.sum(raised, axis=-1, keepdims=True)
    probs = raised / total
    probs_low = probs.astype(BF16)
    attended = jnp.einsum("hqk,khd->qhd", probs_low, v, preferred_element_type=F32)
    attended = attended.astype(BF16).reshape(seq_len, features)
    attn_out = dot_nt(attended, wo) + out_bias
    normed, n1, r1 = norm_forward(x.astype(F32) + attn_out, first_gain, first_offset)
    normed_low = normed.astype(BF16)
    hidden = dot_nn(normed_low, wu) + bu
    act = gelu(hidden).astype(BF16)
    ffn_out = dot_nt(act, wd) + down_bias
    final, n2, r2 = norm_forward(normed + ffn_out, second_gain, second_offset)
    layer_out = initial_to_slots((final * live_col).astype(BF16), slot_order, micro)

    grad_out = cot.astype(F32) * live_col
    grad_second, gain_two, offset_two = norm_backward(grad_out, n2, r2, second_gain)
    gffn = grad_second.astype(BF16)
    grad_act = dot_nn(gffn, wd)
    ghid = (grad_act * gelu_slope(hidden)).astype(BF16)
    grad_normed = dot_nt(ghid, wu) + grad_second
    d_down = dot_tn(gffn, act)
    d_up = dot_tn(normed_low, ghid)
    grad_first, gain_one, offset_one = norm_backward(grad_normed, n1, r1, first_gain)
    gattn = grad_first.astype(BF16)
    gatt = dot_nn(gattn, wo).astype(BF16)
    d_out = dot_tn(gattn, attended)
    gatt_h = gatt.reshape(split)
    gp = jnp.einsum("qhd,khd->hqk", gatt_h, v, preferred_element_type=F32)
    inner = jnp.sum(gp * probs, axis=-1, keepdims=True)
    gs = (probs * (gp - inner) * scale).astype(BF16)
    gq = jnp.einsum("hqk,khd->qhd", gs, k, preferred_element_type=F32)
    gk = jnp.einsum("hqk,qhd->khd", gs, q, preferred_element_type=F32)
    gv = jnp.einsum("hqk,qhd->khd", probs_low, gatt_h, preferred_element_type=F32)
    gq, gk, gv = (g.astype(BF16).reshape(seq_len, features) for g in (gq, gk, gv))
    grad_tokens = (grad_first + dot_nt(gq, wq) + dot_nt(gk, wk) + dot_nt(gv, wv)).astype(BF16)
    input_grad = lax.all_to_all(
        grad_tokens.reshape(1, seq_len, features), "tensor", split_axis=1, concat_axis=0, tiled=True
    )
    rows, cols = query_weight.shape
    units = up_weight.shape[1]
    grads = (
        scatter_grad(dot_tn(x, gq), rows, cols),
        scatter_grad(dot_tn(x, gk), rows, cols),
        scatter_grad(dot_tn(x, gv), rows, cols),
        scatter_grad(d_out, rows, cols),
        scatter_grad(d_up, rows, units),
        scatter_grad(d_down, rows, units),
    )

    def colsum(a):
        return jnp.sum(a.astype(F32), axis=0)

    sums = lax.psum(
        jnp.concatenate([
            colsum(gq), colsum(gv), colsum(gattn), colsum(ghid), colsum(gffn),
            gain_one, offset_one, gain_two, offset_two,
        ]),
        BOTH,
    )
    pieces = []
    at = 0
    for width in (features, features, features, units * tensor_size, *(features,) * 5):
        pieces.append(sums[at : at + width])
        at += width

    def own(vec, width):
        return lax.dynamic_slice_in_dim(vec, tensor_pos * width, width)

    return (
        layer_out, input_grad, *grads,
        own(pieces[0], cols), own(pieces[1], cols), pieces[2], own(pieces[3], units), *pieces[4:],
    )


def solution(mesh):
    rows = P("dp", "tensor", None)
    weight = P("dp", "tensor")
    cut = P("tensor")
    whole = P()
    return jax.shard_map(
        on_device,
        mesh=mesh,
        in_specs=(rows, rows, whole, whole, *(weight,) * 6, cut, cut, whole, cut, *(whole,) * 5),
        out_specs=(rows, rows, *(weight,) * 6, cut, cut, whole, cut, *(whole,) * 5),
        check_vma=False,
    )
```

```python
import functools

import jax
import jax.numpy as jnp
from jax import lax
from jax.experimental import pallas as pl
from jax.experimental.pallas import tpu as pltpu
from jax.sharding import PartitionSpec as P

HEAD = 64
PAIR = 2 * HEAD
EPSILON = 1e-05
SQRT_HALF = 0.7071067811865476
INV_ROOT_TWO_PI = 0.3989422804014327
BOTH = ("dp", "tensor")
F32 = jnp.float32
BF16 = jnp.bfloat16
TILE = 256
ROWS = 128
HBM = pl.BlockSpec(memory_space=pl.ANY)
VMEM = pl.BlockSpec(memory_space=pltpu.VMEM)
SMEM = pl.BlockSpec(memory_space=pltpu.SMEM)
LEN, AT_Z, AT_X, AT_C, AT_Y = range(5)


def dot_nn(a, b):
    return lax.dot_general(a, b, (((1,), (0,)), ((), ())), preferred_element_type=F32)


def dot_nt(a, b):
    return lax.dot_general(a, b, (((1,), (1,)), ((), ())), preferred_element_type=F32)


def params(mib):
    return pltpu.CompilerParams(vmem_limit_bytes=mib << 20)


def exchange(value, bit):
    count = lax.axis_size("dp") * lax.axis_size("tensor")
    return lax.ppermute(value, BOTH, [(i, i ^ (1 << bit)) for i in range(count)])


def in_order(bit_at, mine, other, axis):
    low = jnp.where(bit_at == 0, mine, other)
    high = jnp.where(bit_at == 0, other, mine)
    return jnp.stack([low, high], axis=axis)


def gather_pieces(first, second, at):
    _, at_x, _, at_y, at_z0, at_z1 = at
    both = jnp.stack([first, second])
    both = in_order(at_z1, both, exchange(both, 4), 1)
    both = in_order(at_z0, both, exchange(both, 3), 2)
    both = both.reshape(2, 4, *first.shape)
    a, b = both[0], both[1]
    a = in_order(at_x, a, exchange(a, 2), 0)
    b = in_order(at_y, b, exchange(b, 0), 0)
    a_far, b_far = exchange(a, 0), exchange(b, 2)
    return [p for near in (a, a_far, b, b_far) for p in (near, exchange(near, 1))]


def load_pieces(scalars, pieces, weight, sems, spans):
    copies = []

    def add(src, dst):
        copies.append(pltpu.make_async_copy(src, dst, sems.at[len(copies)]))

    for number, piece in enumerate(pieces):
        half, far, other = number // 4, (number // 2) % 2, number % 2
        at_c = scalars[AT_C] ^ other
        for inner in range(2):
            if half == 0:
                at_x, at_y = inner, scalars[AT_Y] ^ far
            else:
                at_x, at_y = scalars[AT_X] ^ far, inner
            for start, width, to in spans[half]:
                column = pl.multiple_of(to(at_y), 128)
                add(
                    piece.at[inner, :, :, pl.ds(start, width)],
                    weight.at[:, at_x, at_c, :, pl.ds(column, width)],
                )
    return copies


def load_whole(scalars, pieces, weight, sems, spans):
    return [pltpu.make_async_copy(pieces[0], weight, sems.at[0])]


def normalize(z):
    mean = jnp.mean(z, axis=-1, keepdims=True)
    center = z - mean
    rscale = lax.rsqrt(jnp.mean(center * center, axis=-1, keepdims=True) + EPSILON)
    return center * rscale, rscale


def norm_backward(e, normal, rscale, gain):
    scaled = e * gain
    mean = jnp.mean(scaled, axis=-1, keepdims=True)
    tilt = jnp.mean(scaled * normal, axis=-1, keepdims=True)
    return rscale * (scaled - mean - normal * tilt)


def lane_mask(shape, odd):
    lane = lax.broadcasted_iota(jnp.int32, shape, len(shape) - 1)
    return (lane >= HEAD) if odd else (lane < HEAD)


def flat(weight):
    return weight.reshape(-1, weight.shape[-1])


def run_copies(copies):
    for c in copies:
        c.start()
    for c in copies:
        c.wait()


def attend_kernel(load, scalars, x_ref, vec_ref, *refs):
    pieces, refs = refs[:-11], refs[-11:]
    q_ref, k_ref, v_ref, att_ref, lse_ref, n_ref, r_ref, low_ref, w5, acc, sems = refs
    run_copies(load(scalars, pieces, w5, sems))
    w = flat(w5)
    seq, features = x_ref.shape
    live = lax.broadcasted_iota(jnp.int32, (1, seq), 1) < scalars[LEN]
    scale = HEAD**-0.5

    @pl.loop(0, features // TILE)
    def _(t):
        col = pl.multiple_of(t * TILE, TILE)
        here = pl.ds(col, TILE)
        x = x_ref[...]
        q = dot_nn(x, w[:, here]) + vec_ref[0:1, here]
        q_ref[:, here] = (q.astype(BF16).astype(F32) * scale).astype(BF16)
        k = dot_nn(x, w[:, pl.ds(pl.multiple_of(features + col, TILE), TILE)])
        k_ref[:, here] = k.astype(BF16)
        v = dot_nn(x, w[:, pl.ds(pl.multiple_of(2 * features + col, TILE), TILE)])
        v_ref[:, here] = (v + vec_ref[1:2, here]).astype(BF16)

    lse_ref[...] = jnp.zeros_like(lse_ref)

    @pl.loop(0, features // PAIR)
    def _(pair):
        here = pl.ds(pl.multiple_of(pair * PAIR, PAIR), PAIR)
        k2, v2 = k_ref[:, here], v_ref[:, here]
        keys = [jnp.where(lane_mask(k2.shape, odd), k2, jnp.zeros_like(k2)) for odd in range(2)]
        column = lax.broadcasted_iota(jnp.int32, (ROWS, 128), 1)
        for row in range(0, seq, ROWS):
            rows = pl.ds(row, ROWS)
            q2 = q_ref[rows, here]
            outs = []
            sums = lse_ref[rows, :]
            for odd in range(2):
                s = jnp.where(live, dot_nt(q2, keys[odd]), -1e9)
                top = jnp.max(s, axis=-1, keepdims=True)
                e = jnp.exp(s - top)
                total = jnp.sum(e, axis=-1, keepdims=True)
                outs.append(dot_nn((e * (1.0 / total)).astype(BF16), v2))
                sums = jnp.where(column == 2 * pair + odd, top + jnp.log(total), sums)
            lse_ref[rows, :] = sums
            att_ref[rows, here] = jnp.where(lane_mask(outs[0].shape, 1), outs[1], outs[0]).astype(BF16)

    @pl.loop(0, features // TILE)
    def _(t):
        col = pl.multiple_of(t * TILE, TILE)
        acc[:, pl.ds(col, TILE)] = dot_nt(att_ref[...], w[pl.ds(col, TILE), 3 * features :])

    @pl.loop(0, seq // ROWS)
    def _(t):
        rows = pl.ds(pl.multiple_of(t * ROWS, ROWS), ROWS)
        normal, rscale = normalize(x_ref[rows, :].astype(F32) + acc[rows, :] + vec_ref[2:3, :])
        n_ref[rows, :] = normal
        r_ref[rows, :] = rscale
        low_ref[rows, :] = (normal * vec_ref[3:4, :] + vec_ref[4:5, :]).astype(BF16)


def forward_kernel(load, scalars, low_ref, n_ref, vec_ref, up_bias_ref, *refs):
    pieces, refs = refs[:-10], refs[-10:]
    act_ref, slope_ref, n2_ref, r2_ref, out_ref, w5_up, w5_down, acc, sems, sems_down = refs
    half = len(pieces) // 2
    copies = load(scalars, pieces[:half], w5_up, sems)
    later = load(scalars, pieces[half:], w5_down, sems_down)
    for c in copies + later:
        c.start()
    for c in copies:
        c.wait()
    up, down = flat(w5_up), flat(w5_down)
    seq, features = low_ref.shape
    units = up.shape[1]

    @pl.loop(0, units // TILE)
    def _(t):
        here = pl.ds(pl.multiple_of(t * TILE, TILE), TILE)
        h = dot_nn(low_ref[...], up[:, here]) + up_bias_ref[0:1, here]
        phi = 0.5 + 0.5 * lax.erf(h * SQRT_HALF)
        act_ref[:, here] = (h * phi).astype(BF16)
        slope_ref[:, here] = (phi + h * jnp.exp(-0.5 * h * h) * INV_ROOT_TWO_PI).astype(slope_ref.dtype)

    for c in later:
        c.wait()

    @pl.loop(0, features // TILE)
    def _(t):
        col = pl.multiple_of(t * TILE, TILE)
        acc[:, pl.ds(col, TILE)] = dot_nt(act_ref[...], down[pl.ds(col, TILE), :])

    groups, parts, piece, _ = out_ref.shape
    block = seq // parts

    for part in range(parts):
        rows = pl.ds(part * block, block)
        normed = n_ref[rows, :] * vec_ref[0:1, :] + vec_ref[1:2, :]
        normal, rscale = normalize(normed + acc[rows, :] + vec_ref[2:3, :])
        n2_ref[rows, :] = normal
        r2_ref[rows, :] = rscale
        at = part * block + lax.broadcasted_iota(jnp.int32, (block, 1), 0)
        final = (normal * vec_ref[3:4, :] + vec_ref[4:5, :]) * (at < scalars[LEN]).astype(F32)
        out_ref[:, part] = final.astype(BF16).reshape(groups, piece, features)


def column_sum(value):
    return jnp.sum(value, axis=0, keepdims=True)


def down_kernel(store, scalars, cot_ref, n2_ref, r2_ref, act_ref, vec_ref, *refs):
    outs, (second_ref, low_ref, sums_ref, turned) = refs[:-4], refs[-4:]
    groups, parts, piece, features = cot_ref.shape
    block = groups * piece
    sums = [jnp.zeros((1, features), F32)] * 3
    for part in range(parts):
        rows = pl.ds(part * block, block)
        at = part * block + lax.broadcasted_iota(jnp.int32, (block, 1), 0)
        grad_out = cot_ref[:, part].reshape(block, features).astype(F32)
        grad_out = grad_out * (at < scalars[LEN]).astype(F32)
        normal = n2_ref[rows, :]
        second = norm_backward(grad_out, normal, r2_ref[rows, :], vec_ref[0:1, :])
        low = second.astype(BF16)
        second_ref[rows, :] = second
        low_ref[rows, :] = low
        turned[:, rows] = low.T
        more = [column_sum(low.astype(F32)), column_sum(grad_out * normal), column_sum(grad_out)]
        sums = [a + b for a, b in zip(sums, more)]
    sums_ref[...] = jnp.concatenate(sums, axis=0)
    units = act_ref.shape[1]

    @pl.loop(0, units // TILE)
    def _(t):
        here = pl.ds(pl.multiple_of(t * TILE, TILE), TILE)
        store(scalars, outs, t, dot_nn(turned[...], act_ref[:, here]).astype(BF16))


def up_kernel(load, store, kept, scalars, gffn_ref, second_ref, slope_ref, low_ref, n_ref, r_ref, vec_ref, *refs):
    pieces, refs = refs[:-kept], refs[-kept:]
    first_ref, gattn_ref, sums_ref, unit_sums_ref, *outs = refs[:-7]
    w5_up, w5_down, ghid, turned, acc, sems, sems_down = refs[-7:]
    half = len(pieces) // 2
    copies = load(scalars, pieces[half:], w5_down, sems_down)
    later = load(scalars, pieces[:half], w5_up, sems)
    for c in copies + later:
        c.start()
    up, down = flat(w5_up), flat(w5_down)
    seq, features = low_ref.shape
    units = slope_ref.shape[1]
    turned[...] = low_ref[...].T
    for c in copies:
        c.wait()

    @pl.loop(0, units // TILE)
    def _(t):
        here = pl.ds(pl.multiple_of(t * TILE, TILE), TILE)
        grad_act = dot_nn(gffn_ref[...], down[:, here])
        low = (grad_act * slope_ref[:, here].astype(F32)).astype(BF16)
        ghid[:, here] = low
        unit_sums_ref[0:1, here] = column_sum(low.astype(F32))
        store(scalars, outs, t, dot_nn(turned[...], low).astype(BF16))

    for c in later:
        c.wait()

    @pl.loop(0, features // TILE)
    def _(t):
        col = pl.multiple_of(t * TILE, TILE)
        acc[:, pl.ds(col, TILE)] = dot_nt(ghid[...], up[pl.ds(col, TILE), :])

    sums_ref[...] = jnp.zeros_like(sums_ref)

    @pl.loop(0, seq // ROWS)
    def _(t):
        rows = pl.ds(pl.multiple_of(t * ROWS, ROWS), ROWS)
        normal = n_ref[rows, :]
        e = acc[rows, :] + second_ref[rows, :]
        first = norm_backward(e, normal, r_ref[rows, :], vec_ref[0:1, :])
        low = first.astype(BF16)
        first_ref[rows, :] = first
        gattn_ref[rows, :] = low
        more = [column_sum(low.astype(F32)), column_sum(e * normal), column_sum(e)]
        sums_ref[...] += jnp.concatenate(more, axis=0)


def attend_back_kernel(load, store, kept, scalars, gattn_ref, first_ref, x_ref, q_ref, k_ref, v_ref, att_ref, lse_ref, *refs):
    pieces, refs = refs[:-kept], refs[-kept:]
    grad_ref, sums_ref, *outs = refs[:-11]
    w5, gatt, gq, gk, gv, turned, turned_q, turned_do, gkt, gvt, sems = refs[-11:]
    copies = load(scalars, pieces, w5, sems)
    for c in copies:
        c.start()
    w = flat(w5)
    seq, features = x_ref.shape
    scale = HEAD**-0.5
    live = lax.broadcasted_iota(jnp.int32, (1, seq), 1) < scalars[LEN]
    turned[...] = gattn_ref[...].T
    for c in copies:
        c.wait()

    @pl.loop(0, features // TILE)
    def _(t):
        col = pl.multiple_of(t * TILE, TILE)
        gatt[:, pl.ds(col, TILE)] = dot_nn(
            gattn_ref[...], w[:, pl.ds(pl.multiple_of(3 * features + col, TILE), TILE)]
        ).astype(BF16)

    store(scalars, outs, 3, dot_nn(turned[...], att_ref[...]).astype(BF16))
    turned[...] = x_ref[...].T

    @pl.loop(0, features // PAIR)
    def _(pair):
        here = pl.ds(pl.multiple_of(pair * PAIR, PAIR), PAIR)
        k2, v2 = k_ref[:, here], v_ref[:, here]
        keys = [jnp.where(lane_mask(k2.shape, odd), k2, jnp.zeros_like(k2)) for odd in range(2)]
        values = [jnp.where(lane_mask(v2.shape, odd), v2, jnp.zeros_like(v2)) for odd in range(2)]
        turned_q[...] = q_ref[:, here].T
        turned_do[...] = gatt[:, here].T
        column = lax.broadcasted_iota(jnp.int32, (ROWS, 128), 1)
        for row in range(0, seq, ROWS):
            rows = pl.ds(row, ROWS)
            q2, do2 = q_ref[rows, here], gatt[rows, here]
            both = do2.astype(F32) * att_ref[rows, here].astype(F32)
            sums = lse_ref[rows, :]
            outs_q = []
            for odd in range(2):
                head = pl.ds(odd * HEAD, HEAD)
                lse = jnp.sum(jnp.where(column == 2 * pair + odd, sums, 0.0), axis=-1, keepdims=True)
                inner = jnp.sum(jnp.where(lane_mask(both.shape, odd), both, 0.0), axis=-1, keepdims=True)
                s = jnp.where(live, dot_nt(q2, keys[odd]), -1e9)
                p = jnp.exp(s - lse)
                gs = (p * (dot_nt(do2, values[odd]) - inner)).astype(BF16)
                outs_q.append(dot_nn(gs, k2))
                gkt_part = dot_nn(turned_q[head, rows], gs)
                gvt_part = dot_nn(turned_do[head, rows], p.astype(BF16))
                if row == 0:
                    gkt[head, :] = gkt_part
                    gvt[head, :] = gvt_part
                else:
                    gkt[head, :] += gkt_part
                    gvt[head, :] += gvt_part
            gq[rows, here] = (
                jnp.where(lane_mask(outs_q[0].shape, 1), outs_q[1], outs_q[0]) * scale
            ).astype(BF16)
        gk[:, here] = gkt[...].astype(BF16).T
        gv[:, here] = gvt[...].astype(BF16).T

    store(scalars, outs, 0, dot_nn(turned[...], gq[...]).astype(BF16))
    store(scalars, outs, 1, dot_nn(turned[...], gk[...]).astype(BF16))
    store(scalars, outs, 2, dot_nn(turned[...], gv[...]).astype(BF16))
    sums_ref[...] = jnp.concatenate(
        [column_sum(gq[...].astype(F32)), column_sum(gv[...].astype(F32))], axis=0
    )
    parts, block, _ = grad_ref.shape

    @pl.loop(0, features // TILE)
    def _(t):
        col = pl.multiple_of(t * TILE, TILE)
        here = pl.ds(col, TILE)
        total = (
            first_ref[:, here]
            + dot_nt(gq[...], w[here, 0:features])
            + dot_nt(gk[...], w[here, features : 2 * features])
            + dot_nt(gv[...], w[here, 2 * features : 3 * features])
        ).astype(BF16)
        for part in range(parts):
            grad_ref[part, :, here] = total[part * block : (part + 1) * block]


def each_block(scalars, outs, write):
    keep, send = outs
    for mine in range(2):

        @pl.when(scalars[AT_C] == mine)
        def _():
            for at_z in range(4):
                for at_x in range(2):
                    write(at_z, at_x, mine, keep)
                    write(at_z, at_x, 1 - mine, send)


def store_units(scalars, outs, t, value):
    rows, width = outs[0].shape[-2:]
    tiles = width // TILE
    half, col = (t // tiles) % 2, pl.multiple_of((t % tiles) * TILE, TILE)
    far_y = (t // (2 * tiles)) ^ scalars[AT_Y]

    def write(at_z, at_x, at_c, out):
        far_z, far_x = at_z ^ scalars[AT_Z], at_x ^ scalars[AT_X]
        one = jnp.where(half == 0, far_x, far_y)
        two = jnp.where(half == 0, far_y, far_x)
        start = ((at_z * 2 + at_x) * 2 + at_c) * rows
        out[half, one, two, far_z, :, pl.ds(col, TILE)] = value[start : start + rows]

    each_block(scalars, outs, write)


def store_heads(scalars, outs, number, value):
    rows, width = outs[0].shape[-2:]
    cols = width // 2
    half, col = number // 2, (number % 2) * cols

    def write(at_z, at_x, at_c, out):
        far_z, far_x = at_z ^ scalars[AT_Z], at_x ^ scalars[AT_X]
        start = ((at_z * 2 + at_x) * 2 + at_c) * rows
        for at_y in range(2):
            far_y = at_y ^ scalars[AT_Y]
            one, two = (far_x, far_y) if half == 0 else (far_y, far_x)
            piece = value[start : start + rows, at_y * cols : (at_y + 1) * cols]
            out[half, one, two, far_z, :, col : col + cols] = piece

    each_block(scalars, outs, write)


def store_units_whole(scalars, outs, t, value):
    outs[0][:, pl.ds(pl.multiple_of(t * TILE, TILE), TILE)] = value


def store_heads_whole(scalars, outs, number, value):
    cols = value.shape[1]
    outs[0][:, number * cols : (number + 1) * cols] = value


def pick_kernel(order, src, dst):
    @pl.loop(0, dst.shape[0])
    def _(t):
        dst[t] = src[order[t]]


def pick(pieces, order):
    return pl.pallas_call(
        pick_kernel,
        out_shape=jax.ShapeDtypeStruct(pieces.shape, pieces.dtype),
        in_specs=[SMEM, VMEM],
        out_specs=VMEM,
        compiler_params=params(8),
        name="pick",
    )(order, pieces)


def add_low(a, b):
    return (a.astype(F32) + b.astype(F32)).astype(BF16)


def scatter_pieces(keep, send):
    near = exchange(send, 1)
    a_send = add_low(keep[0, 1], near[0, 1])
    b_send = add_low(keep[1, 1], near[1, 1])
    a_far, b_far = exchange(a_send, 2), exchange(b_send, 0)
    a_keep = add_low(keep[0, 0], near[0, 0])
    b_keep = add_low(keep[1, 0], near[1, 0])
    a_next = exchange(add_low(a_keep[1], a_far[1]), 0)
    b_next = exchange(add_low(b_keep[1], b_far[1]), 2)
    a_keep, b_keep = add_low(a_keep[0], a_far[0]), add_low(b_keep[0], b_far[0])
    rows, width = keep.shape[-2:]
    both = jnp.stack([add_low(a_keep, a_next), add_low(b_keep, b_next)]).reshape(2, 2, 2, rows, width)
    far = exchange(both[:, :, 1], 3)
    both = add_low(both[:, :, 0], far)
    far = exchange(both[:, 1], 4)
    total = both[:, 0].astype(F32) + far.astype(F32)
    return total[0], total[1]


def scatter_whole(grad, rows, cols):
    size = lax.axis_size("tensor")
    parts = grad.reshape(-1, rows, size, cols).transpose(0, 2, 1, 3).reshape(-1, cols)
    return lax.psum_scatter(parts, BOTH, scatter_dimension=0, tiled=True).astype(F32)


def gather_whole(shard):
    size = lax.axis_size("tensor")
    rows, cols = shard.shape
    got = lax.all_gather(shard, BOTH, axis=0, tiled=False).reshape(-1, size, rows, cols)
    return got.transpose(0, 2, 1, 3).reshape(1, 1, 1, -1, size * cols)


def deal(block, order):
    micro, half, features = block.shape
    dp, size = lax.axis_size("dp"), lax.axis_size("tensor")
    piece = half // dp
    pieces = block.reshape(micro, dp, piece, features).transpose(1, 0, 2, 3)
    spread = lax.all_to_all(pieces.reshape(dp, micro * piece, features), "dp", split_axis=0, concat_axis=0, tiled=True)
    chosen = pick(spread.reshape(dp * micro, piece, features), order)
    got = lax.all_to_all(chosen, BOTH, split_axis=0, concat_axis=0, tiled=True)
    return got.reshape(dp, size, piece, features)


def collect(pieces, order, micro):
    dp, size, piece, features = pieces.shape
    got = lax.all_to_all(pieces.reshape(dp * size, piece, features), BOTH, split_axis=0, concat_axis=0, tiled=True)
    chosen = pick(got, order).reshape(dp, micro * piece, features)
    back = lax.all_to_all(chosen, "dp", split_axis=0, concat_axis=0, tiled=True)
    return back.reshape(dp, micro, piece, features).transpose(1, 0, 2, 3).reshape(micro, dp * piece, features)


def on_device(
    tokens, cotangent, lengths, slot_order,
    query_weight, key_weight, value_weight, out_weight, up_weight, down_weight,
    query_bias, value_bias, out_bias, up_bias, down_bias,
    first_gain, first_offset, second_gain, second_offset,
):
    micro, half, features = tokens.shape
    dp, size = lax.axis_size("dp"), lax.axis_size("tensor")
    assert micro == size == 2
    dp_pos, at_y = lax.axis_index("dp"), lax.axis_index("tensor")
    rows, cols = query_weight.shape
    unit_cols = up_weight.shape[1]
    units = unit_cols * size
    seq = half * size
    slots = slot_order.shape[0]
    inverse = jnp.zeros_like(slot_order).at[slot_order].set(jnp.arange(slots, dtype=jnp.int32))
    at_c, at_x, at_z0, at_z1 = dp_pos & 1, (dp_pos >> 1) & 1, (dp_pos >> 2) & 1, dp_pos >> 3
    scalars = jnp.stack([lengths[dp_pos * size + at_y], dp_pos >> 2, at_x, at_c, at_y]).astype(jnp.int32)

    split = dp == 16 and rows % 16 == 0
    if split:
        dims = (4, 2, 2, rows)
        at = (at_c, at_x, None, at_y, at_z0, at_z1)
        heads_in = gather_pieces(
            jnp.concatenate([query_weight, key_weight], axis=1),
            jnp.concatenate([value_weight, out_weight], axis=1), at,
        )
        wide = unit_cols // 2
        up_in = gather_pieces(up_weight[:, :wide], up_weight[:, wide:], at)
        down_in = gather_pieces(down_weight[:, :wide], down_weight[:, wide:], at)
        unit_spans = [[(0, wide, lambda y, h=h: y * unit_cols + h * wide)] for h in range(2)]
        head_spans = [
            [(m * cols, cols, lambda y, n=2 * h + m: n * features + y * cols) for m in range(2)] for h in range(2)
        ]
        load_units = functools.partial(load_pieces, spans=unit_spans)
        load_heads = functools.partial(load_pieces, spans=head_spans)
        put_units, put_heads = store_units, store_heads
        grad_out = [jax.ShapeDtypeStruct((2, 2, 2, 4, rows, wide), BF16)] * 2
        count = 16
    else:
        dims = (1, 1, 1, features)
        heads_in = [jnp.concatenate(
            [gather_whole(w) for w in (query_weight, key_weight, value_weight, out_weight)], axis=-1
        )]
        up_in, down_in = [gather_whole(up_weight)], [gather_whole(down_weight)]
        load_units = load_heads = functools.partial(load_whole, spans=None)
        put_units, put_heads = store_units_whole, store_heads_whole
        grad_out = [jax.ShapeDtypeStruct((features, units), BF16)]
        count = 1

    own_half = lax.dynamic_index_in_dim(tokens, at_y, 0, keepdims=False)
    other_half = exchange(lax.dynamic_index_in_dim(tokens, 1 - at_y, 0, keepdims=False), 0)
    x = in_order(at_y, own_half, other_half, 0).reshape(seq, features)
    biases = jnp.concatenate([query_bias, value_bias, up_bias]).reshape(-1, cols)
    biases = in_order(at_y, biases, exchange(biases, 0), 1)
    biases = biases.reshape(-1, size, cols)
    full_query, full_value = biases[0].reshape(-1), biases[1].reshape(-1)
    full_up = biases[2:].transpose(1, 0, 2).reshape(1, units)

    cot = deal(cotangent, inverse)
    if not split:
        cot = cot.transpose(1, 0, 2, 3).reshape(1, size, half, features)

    def act(shape, dtype=BF16):
        return jax.ShapeDtypeStruct(shape, dtype)

    wide_rows, tall = act((seq, features)), act((seq, features), F32)
    column = act((seq, 1), F32)
    head_vec = jnp.stack([full_query, full_value, out_bias, first_gain, first_offset])
    sem = pltpu.SemaphoreType.DMA

    q, k, v, att, lse, n1, r1, low = pl.pallas_call(
        functools.partial(attend_kernel, load_heads),
        out_shape=(wide_rows, wide_rows, wide_rows, wide_rows, act((seq, 128), F32), tall, column, wide_rows),
        in_specs=[SMEM, VMEM, VMEM] + [HBM] * len(heads_in),
        out_specs=(VMEM,) * 8,
        scratch_shapes=[
            pltpu.VMEM((*dims, 4 * features), BF16), pltpu.VMEM((seq, features), F32), sem((2 * count,)),
        ],
        compiler_params=params(40),
        name="attend",
    )(scalars, x, head_vec, *heads_in)

    forward_vec = jnp.stack([first_gain, first_offset, down_bias, second_gain, second_offset])
    deal_dims = (dp, size, half // dp, features) if split else (1, size, half, features)
    wide_units = act((seq, units))
    active, slope, n2, r2, out = pl.pallas_call(
        functools.partial(forward_kernel, load_units),
        out_shape=(wide_units, wide_units, tall, column, act(deal_dims)),
        in_specs=[SMEM] + [VMEM] * 4 + [HBM] * (2 * len(up_in)),
        out_specs=(VMEM,) * 5,
        scratch_shapes=[
            pltpu.VMEM((*dims, units), BF16), pltpu.VMEM((*dims, units), BF16),
            pltpu.VMEM((seq, features), F32), sem((count,)), sem((count,)),
        ],
        compiler_params=params(40),
        name="forward",
    )(scalars, low, n1, forward_vec, full_up, *up_in, *down_in)
    if not split:
        out = out.reshape(size, dp, half // dp, features).transpose(1, 0, 2, 3)
    layer_out = collect(out, slot_order, micro)

    *down_grad, second, gffn, down_sums = pl.pallas_call(
        functools.partial(down_kernel, put_units),
        out_shape=(*grad_out, tall, wide_rows, act((3, features), F32)),
        in_specs=[SMEM] + [VMEM] * 5,
        out_specs=(VMEM,) * (len(grad_out) + 3),
        scratch_shapes=[pltpu.VMEM((features, seq), BF16)],
        compiler_params=params(40),
        name="down",
    )(scalars, cot, n2, r2, active, second_gain[None])

    first, gattn, up_sums, unit_sums, *up_grad = pl.pallas_call(
        functools.partial(up_kernel, load_units, put_units, 11 + len(grad_out)),
        out_shape=(tall, wide_rows, act((3, features), F32), act((1, units), F32), *grad_out),
        in_specs=[SMEM] + [VMEM] * 7 + [HBM] * (2 * len(up_in)),
        out_specs=(VMEM,) * (4 + len(grad_out)),
        scratch_shapes=[
            pltpu.VMEM((*dims, units), BF16), pltpu.VMEM((*dims, units), BF16),
            pltpu.VMEM((seq, units), BF16), pltpu.VMEM((features, seq), BF16),
            pltpu.VMEM((seq, features), F32), sem((count,)), sem((count,)),
        ],
        compiler_params=params(48),
        name="up",
    )(scalars, gffn, second, slope, low, n1, r1, first_gain[None], *up_in, *down_in)

    grad_rows, head_sums, *head_grad = pl.pallas_call(
        functools.partial(attend_back_kernel, load_heads, put_heads, 13 + len(grad_out)),
        out_shape=(act((size, half, features)), act((2, features), F32), *grad_out),
        in_specs=[SMEM] + [VMEM] * 8 + [HBM] * len(heads_in),
        out_specs=(VMEM,) * (2 + len(grad_out)),
        scratch_shapes=[
            pltpu.VMEM((*dims, 4 * features), BF16),
            *[pltpu.VMEM((seq, features), BF16)] * 4,
            pltpu.VMEM((features, seq), BF16),
            pltpu.VMEM((PAIR, seq), BF16), pltpu.VMEM((PAIR, seq), BF16),
            pltpu.VMEM((PAIR, seq), F32), pltpu.VMEM((PAIR, seq), F32), sem((2 * count,)),
        ],
        compiler_params=params(48),
        name="attend_back",
    )(scalars, gattn, first, x, q, k, v, att, lse, *heads_in)

    own_grad = lax.dynamic_index_in_dim(grad_rows, at_y, 0, keepdims=False)
    other_grad = exchange(lax.dynamic_index_in_dim(grad_rows, 1 - at_y, 0, keepdims=False), 0)
    input_grad = in_order(at_y, own_grad, other_grad, 0)

    if split:
        grads = []
        for pair in (head_grad,):
            a, b = scatter_pieces(*pair)
            grads += [a[:, :cols], a[:, cols:], b[:, :cols], b[:, cols:]]
        grads += [jnp.concatenate(scatter_pieces(*pair), axis=1) for pair in (up_grad, down_grad)]
    else:
        cut = [head_grad[0][:, n * features : (n + 1) * features] for n in range(4)]
        grads = [scatter_whole(g, rows, cols) for g in cut]
        grads += [scatter_whole(g[0], rows, unit_cols) for g in (up_grad, down_grad)]

    sums = jnp.concatenate([down_sums, up_sums, head_sums, unit_sums.reshape(-1, features)])
    if split:
        for bit in range(5):
            sums = sums + exchange(sums, bit)
    else:
        sums = lax.psum(sums, BOTH)

    def own(vec, width):
        return lax.dynamic_slice_in_dim(vec, at_y * width, width)

    return (
        layer_out, input_grad, *grads,
        own(sums[6], cols), own(sums[7], cols), sums[3], own(sums[8:].reshape(-1), unit_cols), sums[0],
        sums[4], sums[5], sums[1], sums[2],
    )


def solution(mesh):
    rows = P("dp", "tensor", None)
    weight = P("dp", "tensor")
    cut = P("tensor")
    whole = P()
    return jax.shard_map(
        on_device,
        mesh=mesh,
        in_specs=(rows, rows, whole, whole, *(weight,) * 6, cut, cut, whole, cut, *(whole,) * 5),
        out_specs=(rows, rows, *(weight,) * 6, cut, cut, whole, cut, *(whole,) * 5),
        check_vma=False,
    )
```

```python
import functools

import jax
import jax.numpy as jnp
from jax import lax
from jax.experimental import pallas as pl
from jax.experimental.pallas import tpu as pltpu
from jax.sharding import PartitionSpec as P

HEAD = 64
PAIR = 2 * HEAD
EPSILON = 1e-05
SQRT_HALF = 0.7071067811865476
INV_ROOT_TWO_PI = 0.3989422804014327
BOTH = ("dp", "tensor")
F32 = jnp.float32
BF16 = jnp.bfloat16
TILE = 768
ROWS = 128
HBM = pl.BlockSpec(memory_space=pltpu.HBM)
VMEM = pl.BlockSpec(memory_space=pltpu.VMEM)
SMEM = pl.BlockSpec(memory_space=pltpu.SMEM)
LEN, AT_Z, AT_X, AT_C, AT_Y = range(5)
Y_BIT, C_BIT, X_BIT, Z_BIT = 1, 2, 4, 8


def dot_nn(a, b):
    return lax.dot_general(a, b, (((1,), (0,)), ((), ())), preferred_element_type=F32)


def dot_nt(a, b):
    return lax.dot_general(a, b, (((1,), (1,)), ((), ())), preferred_element_type=F32)


def dot_tn(a, b):
    return lax.dot_general(a, b, (((0,), (0,)), ((), ())), preferred_element_type=F32)


def params(mib):
    return pltpu.CompilerParams(vmem_limit_bytes=mib << 20)


def cost(us):
    return pl.CostEstimate(flops=int(us * 1e9), bytes_accessed=int(us * 3e6), transcendentals=0)


def tie(*values):
    return lax.optimization_barrier(values)


def exchange(value, mask):
    count = lax.axis_size("dp") * lax.axis_size("tensor")
    return lax.ppermute(value, BOTH, [(i, i ^ mask) for i in range(count)])


def in_order(bit_at, mine, other, axis=0):
    low = jnp.where(bit_at == 0, mine, other)
    high = jnp.where(bit_at == 0, other, mine)
    return jnp.stack([low, high], axis=axis)


class Gather:
    def __init__(self, first, second, places):
        self.places = places
        self.a, self.b = first, second

    def along_z(self):
        both = jnp.stack([self.a, self.b])
        self.both = both
        self.got = [exchange(both, m * Z_BIT) for m in (1, 2, 3)]

    def first_side(self):
        at_z = self.places[0]
        both, (g1, g2, g3) = self.both, self.got
        rows = []
        for z in range(4):
            far = jnp.where(at_z == z ^ 2, g2, g3)
            rows.append(jnp.where(at_z == z, both, jnp.where(at_z == z ^ 1, g1, far)))
        self.a = jnp.stack([r[0] for r in rows])
        self.b = jnp.stack([r[1] for r in rows])
        self.got = exchange(self.a, X_BIT), exchange(self.b, Y_BIT)

    def second_side(self):
        _, at_x, _, at_y = self.places
        self.a = in_order(at_x, self.a, self.got[0])
        self.b = in_order(at_y, self.b, self.got[1])
        self.got = exchange(self.a, Y_BIT), exchange(self.b, X_BIT)
        self.near = exchange(self.a, C_BIT), exchange(self.b, C_BIT)

    def core(self):
        self.far = exchange(self.got[0], C_BIT), exchange(self.got[1], C_BIT)

    def pieces(self):
        return (
            [self.a, self.near[0], self.got[0], self.far[0]],
            [self.b, self.near[1], self.got[1], self.far[1]],
        )


class Mover:
    def __init__(self, sems):
        self.sems, self.used = sems, 0

    def __call__(self, src, dst):
        copy = pltpu.make_async_copy(src, dst, self.sems.at[self.used])
        self.used += 1
        copy.start()
        return copy


def wait(copies):
    for c in copies:
        c.wait()


def load_pieces(move, scalars, pieces, weight, second, spans):
    copies = []
    for number, piece in enumerate(pieces):
        far, other = number // 2, number % 2
        at_c = scalars[AT_C] ^ other
        for inner in range(2):
            if second:
                at_x, at_y = scalars[AT_X] ^ far, inner
            else:
                at_x, at_y = inner, scalars[AT_Y] ^ far
            for start, width, to in spans:
                column = pl.multiple_of(to(at_y), 128)
                copies.append(
                    move(
                        piece.at[inner, :, :, pl.ds(start, width)],
                        weight.at[:, at_x, at_c, :, pl.ds(column, width)],
                    )
                )
    return copies


def load_whole(move, scalars, pieces, weight, second, spans):
    return [
        move(pieces[0].at[:, :, :, :, pl.ds(start, width)], weight.at[:, :, :, :, pl.ds(to, width)])
        for start, width, to in spans
    ]


def flat(weight):
    return weight.reshape(-1, weight.shape[-1])


def normalize(z):
    mean = jnp.mean(z, axis=-1, keepdims=True)
    center = z - mean
    rscale = lax.rsqrt(jnp.mean(center * center, axis=-1, keepdims=True) + EPSILON)
    return center * rscale, rscale


def norm_backward(e, normal, rscale, gain):
    scaled = e * gain
    mean = jnp.mean(scaled, axis=-1, keepdims=True)
    tilt = jnp.mean(scaled * normal, axis=-1, keepdims=True)
    return rscale * (scaled - mean - normal * tilt)


def column_sum(value):
    return jnp.sum(value, axis=0, keepdims=True)


def odd_lanes(shape):
    return lax.broadcasted_iota(jnp.int32, shape, len(shape) - 1) >= HEAD


def of_head(value, odd):
    mask = odd_lanes(value.shape)
    zero = jnp.zeros_like(value)
    return jnp.where(mask, value, zero) if odd else jnp.where(mask, zero, value)


def pair_of(t):
    return pl.ds(pl.multiple_of(t * PAIR, PAIR), PAIR)


def load_tokens(move, scalars, tokens, other, x):
    half = other.shape[0]
    at = scalars[AT_Y]
    return [
        move(tokens.at[at], x.at[pl.ds(pl.multiple_of(at * half, half), half)]),
        move(other, x.at[pl.ds(pl.multiple_of((1 - at) * half, half), half)]),
    ]


def attend_kernel(load, scalars, tokens, other, vec, *refs):
    first, second, outs, scratch = refs
    move = Mover(scratch[-1])
    x, q, k, v, att, lse, normal, rscale, low, acc, w5 = scratch[:-1]
    copies = load_tokens(move, scalars, tokens, other, x)
    for copy_set in (load[0](move, scalars, first, w5), load[1](move, scalars, second, w5)):
        copies += copy_set
    wait(copies)
    w = flat(w5)
    seq, features = x.shape
    live = lax.broadcasted_iota(jnp.int32, (1, seq), 1) < scalars[LEN]
    scale = HEAD**-0.5
    at_q, at_k, at_v, at_o = (pl.ds(n * features, features) for n in range(4))
    q[...] = ((dot_nn(x[...], w[:, at_q]) + vec[0:1, :]).astype(BF16).astype(F32) * scale).astype(BF16)
    k[...] = dot_nn(x[...], w[:, at_k]).astype(BF16)
    v[...] = (dot_nn(x[...], w[:, at_v]) + vec[1:2, :]).astype(BF16)
    sent = [move(s, o) for s, o in zip((q, k, v), outs[:3])]
    lse[...] = jnp.zeros_like(lse)

    @pl.loop(0, features // PAIR)
    def _(pair):
        here = pair_of(pair)
        q2, k2, v2 = q[:, here], k[:, here], v[:, here]
        column = lax.broadcasted_iota(jnp.int32, lse.shape, 1)
        parts = []
        logs = lse[...]
        for odd in range(2):
            s = jnp.where(live, dot_nt(q2, of_head(k2, odd)), -1e9)
            top = jnp.max(s, axis=-1, keepdims=True)
            e = jnp.exp(s - top)
            total = jnp.sum(e, axis=-1, keepdims=True)
            parts.append(dot_nn(e.astype(BF16), v2) * (1.0 / total))
            logs = jnp.where(column == 2 * pair + odd, top + jnp.log(total), logs)
        lse[...] = logs
        att[:, here] = jnp.where(odd_lanes(parts[0].shape), parts[1], parts[0]).astype(BF16)

    sent += [move(att, outs[3]), move(lse, outs[4])]
    acc[...] = dot_nt(att[...], w[:, at_o])

    @pl.loop(0, seq // ROWS)
    def _(t):
        rows = pl.ds(pl.multiple_of(t * ROWS, ROWS), ROWS)
        n, r = normalize(x[rows, :].astype(F32) + acc[rows, :] + vec[2:3, :])
        normal[rows, :] = n
        rscale[rows, :] = r
        low[rows, :] = (n * vec[3:4, :] + vec[4:5, :]).astype(BF16)

    sent += [move(s, o) for s, o in zip((normal, rscale, low), outs[5:])]
    wait(sent)


def forward_kernel(load, scalars, low_in, normal_in, vec, up_bias, *refs):
    first, second, outs, scratch = refs
    move = Mover(scratch[-1])
    low, normal, act, slope, n2, r2, out, acc, w_up, w_down = scratch[:-1]
    early = [move(low_in, low)] + load[0](move, scalars, first, w_up)
    late = [move(normal_in, normal)] + load[1](move, scalars, second, w_down)
    wait(early)
    up, down = flat(w_up), flat(w_down)
    seq, features = low.shape
    sent = []
    for t in range(up.shape[1] // TILE):
        here = pl.ds(t * TILE, TILE)
        h = dot_nn(low[...], up[:, here]) + up_bias[0:1, here]
        phi = 0.5 + 0.5 * lax.erf(h * SQRT_HALF)
        act[:, here] = (h * phi).astype(BF16)
        slope[:, here] = (phi + h * jnp.exp(-0.5 * h * h) * INV_ROOT_TWO_PI).astype(BF16)
        sent += [move(s.at[:, here], o.at[:, here]) for s, o in zip((act, slope), outs[:2])]
    wait(late)
    acc[...] = dot_nt(act[...], down[...])
    groups, parts, piece, _ = out.shape
    block = seq // parts
    for part in range(parts):
        rows = pl.ds(part * block, block)
        normed = normal[rows, :] * vec[0:1, :] + vec[1:2, :]
        n, r = normalize(normed + acc[rows, :] + vec[2:3, :])
        n2[rows, :] = n
        r2[rows, :] = r
        at = part * block + lax.broadcasted_iota(jnp.int32, (block, 1), 0)
        final = (n * vec[3:4, :] + vec[4:5, :]) * (at < scalars[LEN]).astype(F32)
        out[:, part] = final.astype(BF16).reshape(groups, piece, features)
    sent += [move(s, o) for s, o in zip((n2, r2, out), outs[2:])]
    wait(sent)


def back_kernel(load, store, scalars, cot_in, n2_in, r2_in, act_in, slope_in, low_in, gain, *refs):
    weights, outs, (sums, unit_sums), scratch = refs
    second_out, ghid_out, *grad_outs = outs
    move = Mover(scratch[-1])
    cot, n2, r2, act, slope, low, second, gffn, ghid, w5, grads = scratch[:-1]
    early = [move(s, d) for s, d in ((cot_in, cot), (n2_in, n2), (r2_in, r2), (act_in, act))]
    late = load(move, scalars, weights, w5) + [move(slope_in, slope), move(low_in, low)]
    wait(early)
    groups, parts, piece, features = cot.shape
    block = groups * piece
    total = [jnp.zeros((1, features), F32)] * 3
    for part in range(parts):
        rows = pl.ds(part * block, block)
        at = part * block + lax.broadcasted_iota(jnp.int32, (block, 1), 0)
        grad_out = cot[:, part].reshape(block, features).astype(F32)
        grad_out = grad_out * (at < scalars[LEN]).astype(F32)
        normal = n2[rows, :]
        grad = norm_backward(grad_out, normal, r2[rows, :], gain[...])
        g = grad.astype(BF16)
        second[rows, :] = grad
        gffn[rows, :] = g
        more = [column_sum(g.astype(F32)), column_sum(grad_out * normal), column_sum(grad_out)]
        total = [a + b for a, b in zip(total, more)]
    sums[...] = jnp.concatenate(total, axis=0)
    sent = [move(second, second_out)]
    tiles = act.shape[1] // TILE
    for t in range(tiles):
        here = pl.ds(t * TILE, TILE)
        store(scalars, grads, 1, t, dot_tn(gffn[...], act[:, here]).astype(BF16))
    sent += [move(grads.at[n, 1], o.at[1]) for n, o in enumerate(grad_outs)]
    wait(late)
    down = flat(w5)
    for t in range(tiles):
        here = pl.ds(t * TILE, TILE)
        g = (dot_nn(gffn[...], down[:, here]) * slope[:, here].astype(F32)).astype(BF16)
        ghid[:, here] = g
        sent.append(move(ghid.at[:, here], ghid_out.at[:, here]))
        unit_sums[0:1, here] = column_sum(g.astype(F32))
        store(scalars, grads, 0, t, dot_tn(low[...], g).astype(BF16))
    sent += [move(grads.at[n, 0], o.at[0]) for n, o in enumerate(grad_outs)]
    wait(sent)


def normed_kernel(load, load_out, scalars, ghid_in, second_in, normal_in, rscale_in, gain, *refs):
    weights, head_weights, outs, (sums,), scratch = refs
    move = Mover(scratch[-1])
    ghid, second, normal, rscale, first, gattn, gatt, acc, w_up, w_out = scratch[:-1]
    early = [move(ghid_in, ghid)] + load(move, scalars, weights, w_up)
    late = [move(s, d) for s, d in ((second_in, second), (normal_in, normal), (rscale_in, rscale))]
    last = load_out(move, scalars, head_weights, w_out)
    wait(early)
    seq, features = second.shape
    acc[...] = dot_nt(ghid[...], flat(w_up)[...])
    wait(late)
    sums[...] = jnp.zeros_like(sums)

    @pl.loop(0, seq // ROWS)
    def _(t):
        rows = pl.ds(pl.multiple_of(t * ROWS, ROWS), ROWS)
        n = normal[rows, :]
        e = acc[rows, :] + second[rows, :]
        grad = norm_backward(e, n, rscale[rows, :], gain[...])
        g = grad.astype(BF16)
        first[rows, :] = grad
        gattn[rows, :] = g
        more = [column_sum(g.astype(F32)), column_sum(e * n), column_sum(e)]
        sums[...] += jnp.concatenate(more, axis=0)

    sent = [move(first, outs[0]), move(gattn, outs[1])]
    wait(last)
    gatt[...] = dot_nn(gattn[...], flat(w_out)[...]).astype(BF16)
    sent.append(move(gatt, outs[2]))
    wait(sent)


def last_kernel(load, store, scalars, *refs):
    ins, (tokens,), (other,), first_pieces, second_pieces, outs, (sums,), scratch = refs
    own_out, other_out, *grad_outs = outs
    move = Mover(scratch[-1])
    gatt, q, k, v, att, lse, gattn, first, x, gq, gk, gv, rows_grad, w5, grads = scratch[:-1]
    early = [move(s, d) for s, d in zip(ins[:6], (gatt, q, k, v, att, lse))]
    late = [move(ins[6], gattn)] + load_tokens(move, scalars, tokens, other, x)
    later = load[0](move, scalars, first_pieces, w5) + load[1](move, scalars, second_pieces, w5)
    later.append(move(ins[7], first))
    wait(early)
    seq, features = q.shape
    scale = HEAD**-0.5
    live = lax.broadcasted_iota(jnp.int32, (1, seq), 1) < scalars[LEN]

    @pl.loop(0, features // PAIR)
    def _(pair):
        here = pair_of(pair)
        q2, k2, v2, do2 = q[:, here], k[:, here], v[:, here], gatt[:, here]
        both = do2.astype(F32) * att[:, here].astype(F32)
        column = lax.broadcasted_iota(jnp.int32, lse.shape, 1)
        logs = lse[...]
        q_turned, do_turned = q2.T, do2.T
        for_q, for_k, for_v = [], [], []
        for odd in range(2):
            log = jnp.sum(jnp.where(column == 2 * pair + odd, logs, 0.0), axis=-1, keepdims=True)
            inner = jnp.sum(of_head(both, odd), axis=-1, keepdims=True)
            s = jnp.where(live, dot_nt(q2, of_head(k2, odd)), -1e9)
            p = jnp.exp(s - log)
            gs = (p * (dot_nt(do2, of_head(v2, odd)) - inner)).astype(BF16)
            for_q.append(dot_nn(gs, k2))
            head = slice(odd * HEAD, (odd + 1) * HEAD)
            for_k.append(dot_nn(q_turned[head], gs))
            for_v.append(dot_nn(do_turned[head], p.astype(BF16)))
        g = (jnp.where(odd_lanes(for_q[0].shape), for_q[1], for_q[0]) * scale).astype(BF16)
        gq[:, here] = g
        sums[0:1, here] = column_sum(g.astype(F32))
        gk[:, here] = jnp.concatenate(for_k, axis=0).astype(BF16).T
        g = jnp.concatenate(for_v, axis=0).astype(BF16).T
        gv[:, here] = g
        sums[1:2, here] = column_sum(g.astype(F32))

    wait(late)
    store(scalars, grads, 0, dot_tn(x[...], gq[...]).astype(BF16))
    store(scalars, grads, 1, dot_tn(x[...], gk[...]).astype(BF16))
    sent = [move(grads.at[n, 0], o.at[0]) for n, o in enumerate(grad_outs)]
    store(scalars, grads, 2, dot_tn(x[...], gv[...]).astype(BF16))
    store(scalars, grads, 3, dot_tn(gattn[...], att[...]).astype(BF16))
    sent += [move(grads.at[n, 1], o.at[1]) for n, o in enumerate(grad_outs)]
    wait(later)
    w = flat(w5)
    total = first[...]
    for n, g in enumerate((gq, gk, gv)):
        total = total + dot_nt(g[...], w[:, pl.ds(n * features, features)])
    rows_grad[...] = total.astype(BF16)
    half = own_out.shape[0]
    for at, out in ((scalars[AT_Y], own_out), (1 - scalars[AT_Y], other_out)):
        sent.append(move(rows_grad.at[pl.ds(pl.multiple_of(at * half, half), half)], out))
    wait(sent)


def store_units(scalars, out, half, t, value):
    rows, width = out.shape[-2:]
    tiles = width // TILE
    col = (t % tiles) * TILE
    far_y = (t // tiles) ^ scalars[AT_Y]
    for at_z in range(4):
        for at_x in range(2):
            far_z, far_x = at_z ^ scalars[AT_Z], at_x ^ scalars[AT_X]
            one, two = (far_y, far_x) if half else (far_x, far_y)
            for at_c in range(2):
                start = ((at_z * 2 + at_x) * 2 + at_c) * rows
                piece = value[start : start + rows]
                out[at_c ^ scalars[AT_C], half, one, two, far_z, :, col : col + TILE] = piece


def store_heads(scalars, out, number, value):
    rows, width = out.shape[-2:]
    cols = width // 2
    half, col = number // 2, (number % 2) * cols
    for at_z in range(4):
        for at_x in range(2):
            far_z, far_x = at_z ^ scalars[AT_Z], at_x ^ scalars[AT_X]
            for at_c in range(2):
                start = ((at_z * 2 + at_x) * 2 + at_c) * rows
                for at_y in range(2):
                    far_y = at_y ^ scalars[AT_Y]
                    one, two = (far_y, far_x) if half else (far_x, far_y)
                    piece = value[start : start + rows, at_y * cols : (at_y + 1) * cols]
                    out[at_c ^ scalars[AT_C], half, one, two, far_z, :, col : col + cols] = piece


def store_units_whole(scalars, out, half, t, value):
    out[0, half, :, t * TILE : (t + 1) * TILE] = value


def store_heads_whole(scalars, out, number, value):
    cols = value.shape[1]
    out[0, number // 2, :, (number % 2) * cols : (number % 2 + 1) * cols] = value


def pick_kernel(scatter, order, src, dst):
    @pl.loop(0, dst.shape[0])
    def _(t):
        if scatter:
            dst[order[t]] = src[t]
        else:
            dst[t] = src[order[t]]


def pick(pieces, order, scatter):
    return pl.pallas_call(
        functools.partial(pick_kernel, scatter),
        out_shape=jax.ShapeDtypeStruct(pieces.shape, pieces.dtype),
        in_specs=[SMEM, VMEM],
        out_specs=VMEM,
        compiler_params=params(4),
        cost_estimate=cost(1),
        name="pick",
    )(order, pieces)


def in_hbm(value):
    return pltpu.with_memory_space_constraint(value, pltpu.HBM)


def run(kernel, name, us, mib, scalars, ins, lists, outs, sums, scratch, sems):
    arrays = [a if near else in_hbm(a) for a, near in ins] + [in_hbm(a) for some in lists for a in some]
    specs = [VMEM if near else HBM for _, near in ins] + [HBM for some in lists for _ in some]
    groups = [len(some) for some in lists]

    def body(scalars, *refs):
        refs = list(refs)

        def take(n):
            got, refs[:] = refs[:n], refs[n:]
            return got

        singles = take(len(ins))
        grouped = [take(n) for n in groups]
        grouped.append(take(len(outs)))
        if sums:
            grouped.append(take(len(sums)))
        kernel(scalars, *singles, *grouped, refs)

    def buffer(shape):
        return pltpu.VMEM(shape.shape, shape.dtype)

    return pl.pallas_call(
        body,
        out_shape=(*(pltpu.HBM(o.shape, o.dtype) for o in outs), *sums),
        in_specs=[SMEM] + specs,
        out_specs=(HBM,) * len(outs) + (VMEM,) * len(sums),
        scratch_shapes=[*map(buffer, scratch), pltpu.SemaphoreType.DMA((sems,))],
        compiler_params=params(mib),
        cost_estimate=cost(us),
        name=name,
    )(scalars, *arrays)


def add_up(values):
    total = values[0].astype(F32)
    for v in values[1:]:
        total = total + v.astype(F32)
    return total


class Scatter:
    def __init__(self, keep, send):
        self.terms = ([keep[0]], [keep[1]])
        self.send = send

    def core(self):
        self.got = exchange(self.send, C_BIT)

    def _turn(self, masks, first):
        got = []
        for n, mask in enumerate(masks):
            terms = self.terms[n] + [self.got[n]]
            sent = add_up([t[1] for t in terms]).astype(BF16)
            got.append(exchange(sent, mask))
            self.terms[n][:] = [t[0] for t in terms]
        self.got = got

    def first_side(self):
        self._turn((X_BIT, Y_BIT), True)

    def second_side(self):
        self._turn((Y_BIT, X_BIT), False)

    def along_z(self):
        terms = [self.terms[n] + [self.got[n]] for n in range(2)]
        self.got = []
        for m in (1, 2, 3):
            both = jnp.stack([add_up([t[m] for t in terms[n]]).astype(BF16) for n in range(2)])
            self.got.append(exchange(both, m * Z_BIT))
        self.terms = [[t[0] for t in terms[n]] for n in range(2)]

    def total(self):
        return [add_up(self.terms[n] + [g[n] for g in self.got]) for n in range(2)]


def scatter_whole(grad, rows, cols):
    size = lax.axis_size("tensor")
    parts = grad.reshape(-1, rows, size, cols).transpose(0, 2, 1, 3).reshape(-1, cols)
    return lax.psum_scatter(parts, BOTH, scatter_dimension=0, tiled=True).astype(F32)


def gather_whole(shard):
    size = lax.axis_size("tensor")
    rows, cols = shard.shape
    got = lax.all_gather(shard, BOTH, axis=0, tiled=False).reshape(-1, size, rows, cols)
    return got.transpose(0, 2, 1, 3).reshape(1, 1, 1, -1, size * cols)


def deal_start(block):
    micro, half, features = block.shape
    dp = lax.axis_size("dp")
    piece = half // dp
    pieces = block.reshape(micro, dp, piece, features).transpose(1, 0, 2, 3)
    pieces = pieces.reshape(dp, micro * piece, features)
    return lax.all_to_all(pieces, "dp", split_axis=0, concat_axis=0, tiled=True)


def deal_finish(spread, order, micro):
    dp, tall, features = spread.shape
    chosen = pick(spread.reshape(dp * micro, tall // micro, features), order, True)
    got = lax.all_to_all(chosen, BOTH, split_axis=0, concat_axis=0, tiled=True)
    return got.reshape(dp, lax.axis_size("tensor"), tall // micro, features)


def collect_start(pieces):
    dp, size, piece, features = pieces.shape
    pieces = pieces.reshape(dp * size, piece, features)
    return lax.all_to_all(pieces, BOTH, split_axis=0, concat_axis=0, tiled=True)


def collect_finish(got, order, micro):
    dp = lax.axis_size("dp")
    _, piece, features = got.shape
    chosen = pick(got, order, False).reshape(dp, micro * piece, features)
    back = lax.all_to_all(chosen, "dp", split_axis=0, concat_axis=0, tiled=True)
    return back.reshape(dp, micro, piece, features).transpose(1, 0, 2, 3).reshape(micro, dp * piece, features)


def on_device(
    tokens, cotangent, lengths, slot_order,
    query_weight, key_weight, value_weight, out_weight, up_weight, down_weight,
    query_bias, value_bias, out_bias, up_bias, down_bias,
    first_gain, first_offset, second_gain, second_offset,
):
    micro, half, features = tokens.shape
    dp, size = lax.axis_size("dp"), lax.axis_size("tensor")
    assert micro == size == 2
    dp_pos, at_y = lax.axis_index("dp"), lax.axis_index("tensor")
    rows, cols = query_weight.shape
    unit_cols = up_weight.shape[1]
    units = unit_cols * size
    seq = half * size
    at_c, at_x, at_z = dp_pos & 1, (dp_pos >> 1) & 1, dp_pos >> 2
    scalars = jnp.stack([lengths[dp_pos * size + at_y], at_z, at_x, at_c, at_y]).astype(jnp.int32)

    other_half = exchange(lax.dynamic_index_in_dim(tokens, 1 - at_y, 0, keepdims=False), Y_BIT)
    biases = jnp.concatenate([query_bias, value_bias, up_bias]).reshape(-1, cols)
    other_biases = exchange(biases, Y_BIT)

    def act(shape, dtype=BF16):
        return jax.ShapeDtypeStruct(shape, dtype)

    def merged(shapes):
        return act((len(shapes), *shapes[0].shape))

    split = dp == 16 and rows % 16 == 0
    if split:
        dims = (4, 2, 2, rows)
        places = (at_z, at_x, at_c, at_y)
        heads = Gather(
            jnp.concatenate([query_weight, key_weight], axis=1),
            jnp.concatenate([value_weight, out_weight], axis=1), places,
        )
        wide = Gather(up_weight, down_weight, places)
        heads.along_z()
        wide.along_z()
        heads.got, other_half, other_biases = tie(heads.got, other_half, other_biases)
        heads.first_side()
        heads.got, wide.got[0] = tie(heads.got, wide.got[0])
        heads.second_side()
        heads.got, wide.got, cotangent = tie(heads.got, wide.got, cotangent)
        heads.core()
        wide.first_side()
        heads_a, heads_b = heads.pieces()
        heads_a, heads_b, wide.got = tie(heads_a, heads_b, wide.got)
        wide.second_side()
        unit_spans = [(0, unit_cols, lambda y: y * unit_cols)]
        head_spans = [
            [(m * cols, cols, lambda y, n=2 * h + m: n * features + y * cols) for m in range(2)] for h in range(2)
        ]
        out_spans = [(cols, cols, lambda y: y * cols)]
        load_units = [functools.partial(load_pieces, second=h, spans=unit_spans) for h in range(2)]
        load_heads = [functools.partial(load_pieces, second=h, spans=head_spans[h]) for h in range(2)]
        load_out = functools.partial(load_pieces, second=1, spans=out_spans)
        put_units, put_heads = store_units, store_heads
        unit_grads = [act((2, 2, 2, 4, rows, unit_cols))] * 2
        head_grads = [act((2, 2, 2, 4, rows, 2 * cols))] * 2
    else:
        dims = (1, 1, 1, features)
        heads_a, heads_b = (
            [jnp.concatenate([gather_whole(w) for w in pair], axis=-1)]
            for pair in ((query_weight, key_weight), (value_weight, out_weight))
        )
        up_in, down_in = [gather_whole(up_weight)], [gather_whole(down_weight)]
        load_units = [functools.partial(load_whole, second=0, spans=[(0, units, 0)])] * 2
        load_heads = [
            functools.partial(load_whole, second=0, spans=[(0, 2 * features, h * 2 * features)]) for h in range(2)
        ]
        load_out = functools.partial(load_whole, second=0, spans=[(features, features, 0)])
        put_units, put_heads = store_units_whole, store_heads_whole
        unit_grads = [act((2, features, units))]
        head_grads = [act((2, features, 2 * features))]

    biases = in_order(at_y, biases, other_biases, 1)
    full_query, full_value = biases[0].reshape(-1), biases[1].reshape(-1)
    full_up = biases[2:].transpose(1, 0, 2).reshape(1, units)
    spread = deal_start(cotangent)

    low_rows, tall, column = act((seq, features)), act((seq, features), F32), act((seq, 1), F32)
    logs, low_units = act((seq, 128), F32), act((seq, units))
    head_vec = jnp.stack([full_query, full_value, out_bias, first_gain, first_offset])
    head_weights, unit_weights = act((*dims, 4 * features)), act((*dims, units))

    q, k, v, att, lse, n1, r1, low = run(
        functools.partial(attend_kernel, load_heads), "attend", 15, 24, scalars,
        [(tokens, False), (other_half, False), (head_vec, True)], [heads_a, heads_b],
        [low_rows] * 4 + [logs, tall, column, low_rows], [],
        [low_rows] * 5 + [logs, tall, column, low_rows, tall, head_weights], 48,
    )
    if split:
        low, spread = tie(low, spread)
    cot = deal_finish(spread, slot_order, micro)
    if split:
        low, wide.got, wide.near = tie(low, wide.got, wide.near)
        wide.core()
        up_in, down_in = wide.pieces()
    else:
        cot = cot.transpose(1, 0, 2, 3).reshape(1, size, half, features)

    forward_vec = jnp.stack([first_gain, first_offset, down_bias, second_gain, second_offset])
    dealt = act((dp, size, half // dp, features) if split else (1, size, half, features))
    active, slope, n2, r2, out = run(
        functools.partial(forward_kernel, load_units), "forward", 13, 36, scalars,
        [(low, False), (n1, False), (forward_vec, True), (full_up, True)], [up_in, down_in],
        [low_units, low_units, tall, column, dealt], [],
        [low_rows, tall, low_units, low_units, tall, column, dealt, tall, unit_weights, unit_weights], 40,
    )
    if not split:
        out = out.reshape(size, dp, half // dp, features).transpose(1, 0, 2, 3)
    out = collect_start(out)

    second, ghid, *wide_grad, down_sums, unit_sums = run(
        functools.partial(back_kernel, load_units[1], put_units), "back", 16, 48, scalars,
        [(a, False) for a in (cot, n2, r2, active, slope, low)] + [(second_gain[None], True)], [down_in],
        [tall, low_units, *unit_grads], [act((3, features), F32), act((1, units), F32)],
        [dealt, tall, column, low_units, low_units, low_rows, tall, low_rows, low_units, unit_weights, merged(unit_grads)], 32,
    )
    if split:
        ghid, out, wide_grad = tie(ghid, out, wide_grad)
        wide_sum = Scatter(*wide_grad)
        wide_sum.core()
    layer_out = collect_finish(out, slot_order, micro)

    first, gattn, gatt, up_sums = run(
        functools.partial(normed_kernel, load_units[0], load_out), "normed", 8, 28, scalars,
        [(a, False) for a in (ghid, second, n1, r1)] + [(first_gain[None], True)], [up_in, heads_b],
        [tall, low_rows, low_rows], [act((3, features), F32)],
        [low_units, tall, tall, column, tall, low_rows, low_rows, tall, unit_weights, act((*dims, features))], 32,
    )
    if split:
        gatt, wide_sum.got = tie(gatt, wide_sum.got)
        wide_sum.first_side()

    own_grad, other_grad, *head_grad, head_sums = run(
        functools.partial(last_kernel, load_heads, put_heads), "last", 20, 40, scalars,
        [], [[gatt, q, k, v, att, lse, gattn, first], [tokens], [other_half], heads_a, heads_b],
        [act((half, features)), act((half, features)), *head_grads], [act((2, features), F32)],
        [low_rows] * 5 + [logs, low_rows, tall] + [low_rows] * 5 + [head_weights, merged(head_grads)], 60,
    )
    sums = jnp.concatenate([down_sums, up_sums, head_sums, unit_sums.reshape(-1, features)])
    if split:
        head_grad, other_grad, sums, wide_sum.got = tie(head_grad, other_grad, sums, wide_sum.got)
        head_sum = Scatter(*head_grad)
        head_sum.core()
        wide_sum.second_side()
        near = [exchange(sums, m * Z_BIT) for m in (1, 2, 3)]
        near, head_sum.got = tie(near, head_sum.got)
        sums = sums + near[0] + near[1] + near[2]
        near = exchange(sums, C_BIT)
        head_sum.first_side()
        near, wide_sum.got, other_grad = tie(near, wide_sum.got, other_grad)
        sums = sums + near
        near = exchange(sums, X_BIT)
        other_grad = exchange(other_grad, Y_BIT)
        wide_sum.along_z()
        near, head_sum.got = tie(near, head_sum.got)
        sums = sums + near
        near = exchange(sums, Y_BIT)
        head_sum.second_side()
        near, head_sum.got, wide_sum.got = tie(near, head_sum.got, wide_sum.got)
        sums = sums + near
        head_sum.along_z()
        a, b = head_sum.total()
        grads = [a[:, :cols], a[:, cols:], b[:, :cols], b[:, cols:], *wide_sum.total()]
    else:
        other_grad = exchange(other_grad, Y_BIT)
        cut = [head_grad[0][n // 2, :, (n % 2) * features : (n % 2 + 1) * features] for n in range(4)]
        grads = [scatter_whole(g, rows, cols) for g in cut]
        grads += [scatter_whole(wide_grad[0][n], rows, unit_cols) for n in range(2)]
        sums = lax.psum(sums, BOTH)
    input_grad = in_order(at_y, own_grad, other_grad)

    def own(vec, width):
        return lax.dynamic_slice_in_dim(vec, at_y * width, width)

    return (
        layer_out, input_grad, *grads,
        own(sums[6], cols), own(sums[7], cols), sums[3], own(sums[8:].reshape(-1), unit_cols), sums[0],
        sums[4], sums[5], sums[1], sums[2],
    )


def solution(mesh):
    rows = P("dp", "tensor", None)
    weight = P("dp", "tensor")
    cut = P("tensor")
    whole = P()
    return jax.shard_map(
        on_device,
        mesh=mesh,
        in_specs=(rows, rows, whole, whole, *(weight,) * 6, cut, cut, whole, cut, *(whole,) * 5),
        out_specs=(rows, rows, *(weight,) * 6, cut, cut, whole, cut, *(whole,) * 5),
        check_vma=False,
    )
```

```python
import functools

import jax
import jax.numpy as jnp
from jax import lax
from jax.experimental import pallas as pl
from jax.experimental.pallas import tpu as pltpu
from jax.sharding import PartitionSpec as P

HEAD = 64
PAIR = 2 * HEAD
EPSILON = 1e-05
SQRT_HALF = 0.7071067811865476
INV_ROOT_TWO_PI = 0.3989422804014327
BOTH = ("dp", "tensor")
F32 = jnp.float32
BF16 = jnp.bfloat16
TILE = 768
ROWS = 128
HBM = pl.BlockSpec(memory_space=pltpu.HBM)
VMEM = pl.BlockSpec(memory_space=pltpu.VMEM)
SMEM = pl.BlockSpec(memory_space=pltpu.SMEM)
LEN, AT_Z, AT_X, AT_C, AT_Y = range(5)
Y_BIT, C_BIT, X_BIT, Z_BIT = 1, 2, 4, 8


def dot_nn(a, b):
    return lax.dot_general(a, b, (((1,), (0,)), ((), ())), preferred_element_type=F32)


def dot_nt(a, b):
    return lax.dot_general(a, b, (((1,), (1,)), ((), ())), preferred_element_type=F32)


def dot_tn(a, b):
    return lax.dot_general(a, b, (((0,), (0,)), ((), ())), preferred_element_type=F32)


def params(mib):
    return pltpu.CompilerParams(vmem_limit_bytes=mib << 20)


def cost(us):
    return pl.CostEstimate(flops=int(us * 2e7), bytes_accessed=int(us * 6e4), transcendentals=0)


def tie(*values):
    return lax.optimization_barrier(values)


def exchange(value, mask):
    count = lax.axis_size("dp") * lax.axis_size("tensor")
    return lax.ppermute(value, BOTH, [(i, i ^ mask) for i in range(count)])


def in_order(bit_at, mine, other, axis=0):
    low = jnp.where(bit_at == 0, mine, other)
    high = jnp.where(bit_at == 0, other, mine)
    return jnp.stack([low, high], axis=axis)


class Gather:
    def __init__(self, first, second, places):
        self.places = places
        self.a, self.b = first, second

    def along_z(self):
        both = jnp.stack([self.a, self.b])
        self.both = both
        self.got = [exchange(both, m * Z_BIT) for m in (1, 2, 3)]

    def first_side(self):
        at_z = self.places[0]
        both, (g1, g2, g3) = self.both, self.got
        rows = []
        for z in range(4):
            far = jnp.where(at_z == z ^ 2, g2, g3)
            rows.append(jnp.where(at_z == z, both, jnp.where(at_z == z ^ 1, g1, far)))
        self.a = jnp.stack([r[0] for r in rows])
        self.b = jnp.stack([r[1] for r in rows])
        self.got = exchange(self.a, X_BIT), exchange(self.b, Y_BIT)

    def second_side(self):
        _, at_x, _, at_y = self.places
        self.a = in_order(at_x, self.a, self.got[0])
        self.b = in_order(at_y, self.b, self.got[1])
        self.got = exchange(self.a, Y_BIT), exchange(self.b, X_BIT)
        self.near = exchange(self.a, C_BIT), exchange(self.b, C_BIT)

    def core(self):
        self.far = exchange(self.got[0], C_BIT), exchange(self.got[1], C_BIT)

    def pieces(self):
        return (
            [self.a, self.near[0], self.got[0], self.far[0]],
            [self.b, self.near[1], self.got[1], self.far[1]],
        )


class Mover:
    def __init__(self, sems):
        self.sems, self.used = sems, 0

    def __call__(self, src, dst):
        copy = pltpu.make_async_copy(src, dst, self.sems.at[self.used])
        self.used += 1
        copy.start()
        return copy


def wait(copies):
    for c in copies:
        c.wait()


def load_pieces(move, scalars, pieces, weight, second, spans):
    copies = []
    for number, piece in enumerate(pieces):
        far, other = number // 2, number % 2
        at_c = scalars[AT_C] ^ other
        for inner in range(2):
            if second:
                at_x, at_y = scalars[AT_X] ^ far, inner
            else:
                at_x, at_y = inner, scalars[AT_Y] ^ far
            for start, width, to in spans:
                column = pl.multiple_of(to(at_y), 128)
                copies.append(
                    move(
                        piece.at[inner, :, :, pl.ds(start, width)],
                        weight.at[:, at_x, at_c, :, pl.ds(column, width)],
                    )
                )
    return copies


def load_whole(move, scalars, pieces, weight, second, spans):
    return [
        move(pieces[0].at[:, :, :, :, pl.ds(start, width)], weight.at[:, :, :, :, pl.ds(to, width)])
        for start, width, to in spans
    ]


def flat(weight):
    return weight.reshape(-1, weight.shape[-1])


def normalize(z):
    mean = jnp.mean(z, axis=-1, keepdims=True)
    center = z - mean
    rscale = lax.rsqrt(jnp.mean(center * center, axis=-1, keepdims=True) + EPSILON)
    return center * rscale, rscale


def norm_backward(e, normal, rscale, gain):
    scaled = e * gain
    mean = jnp.mean(scaled, axis=-1, keepdims=True)
    tilt = jnp.mean(scaled * normal, axis=-1, keepdims=True)
    return rscale * (scaled - mean - normal * tilt)


def column_sum(value):
    return jnp.sum(value, axis=0, keepdims=True)


def odd_lanes(shape):
    return lax.broadcasted_iota(jnp.int32, shape, len(shape) - 1) >= HEAD


def of_head(value, odd):
    mask = odd_lanes(value.shape)
    zero = jnp.zeros_like(value)
    return jnp.where(mask, value, zero) if odd else jnp.where(mask, zero, value)


def pair_of(t):
    return pl.ds(pl.multiple_of(t * PAIR, PAIR), PAIR)


def load_tokens(move, scalars, tokens, other, x):
    half = other.shape[0]
    at = scalars[AT_Y]
    return [
        move(tokens.at[at], x.at[pl.ds(pl.multiple_of(at * half, half), half)]),
        move(other, x.at[pl.ds(pl.multiple_of((1 - at) * half, half), half)]),
    ]


def attend_kernel(load, scalars, tokens, other, vec, *refs):
    first, second, outs, scratch = refs
    move = Mover(scratch[-1])
    x, q, k, v, att, lse, normal, rscale, low, acc, w5 = scratch[:-1]
    copies = load_tokens(move, scalars, tokens, other, x)
    for copy_set in (load[0](move, scalars, first, w5), load[1](move, scalars, second, w5)):
        copies += copy_set
    wait(copies)
    w = flat(w5)
    seq, features = x.shape
    live = lax.broadcasted_iota(jnp.int32, (1, seq), 1) < scalars[LEN]
    scale = HEAD**-0.5
    at_q, at_k, at_v, at_o = (pl.ds(n * features, features) for n in range(4))
    q[...] = ((dot_nn(x[...], w[:, at_q]) + vec[0:1, :]).astype(BF16).astype(F32) * scale).astype(BF16)
    k[...] = dot_nn(x[...], w[:, at_k]).astype(BF16)
    v[...] = (dot_nn(x[...], w[:, at_v]) + vec[1:2, :]).astype(BF16)
    sent = [move(s, o) for s, o in zip((q, k, v), outs[:3])]
    lse[...] = jnp.zeros_like(lse)

    @pl.loop(0, features // PAIR)
    def _(pair):
        here = pair_of(pair)
        q2, k2, v2 = q[:, here], k[:, here], v[:, here]
        column = lax.broadcasted_iota(jnp.int32, lse.shape, 1)
        parts = []
        logs = lse[...]
        for odd in range(2):
            s = jnp.where(live, dot_nt(q2, of_head(k2, odd)), -1e9)
            top = jnp.max(s, axis=-1, keepdims=True)
            e = jnp.exp(s - top)
            total = jnp.sum(e, axis=-1, keepdims=True)
            parts.append(dot_nn(e.astype(BF16), v2) * (1.0 / total))
            logs = jnp.where(column == 2 * pair + odd, top + jnp.log(total), logs)
        lse[...] = logs
        att[:, here] = jnp.where(odd_lanes(parts[0].shape), parts[1], parts[0]).astype(BF16)

    sent += [move(att, outs[3]), move(lse, outs[4])]
    acc[...] = dot_nt(att[...], w[:, at_o])

    @pl.loop(0, seq // ROWS)
    def _(t):
        rows = pl.ds(pl.multiple_of(t * ROWS, ROWS), ROWS)
        n, r = normalize(x[rows, :].astype(F32) + acc[rows, :] + vec[2:3, :])
        normal[rows, :] = n
        rscale[rows, :] = r
        low[rows, :] = (n * vec[3:4, :] + vec[4:5, :]).astype(BF16)

    sent += [move(s, o) for s, o in zip((normal, rscale, low), outs[5:])]
    wait(sent)


def middle_kernel(load, store, scalars, low_in, normal_in, cot_in, vec, up_bias, *refs):
    first, second, outs, (acc, sums, unit_sums), scratch = refs
    out_out, ghid_out, *grad_outs = outs
    move = Mover(scratch[-1])
    low, normal, cot, act, slope, n2, r2, out, gffn, w_up, w_down, grads = scratch[:-1]
    early = [move(low_in, low)] + load[0](move, scalars, first, w_up)
    late = load[1](move, scalars, second, w_down) + [move(normal_in, normal), move(cot_in, cot)]
    up, down = flat(w_up), flat(w_down)
    seq, features = low.shape
    tiles = up.shape[1] // TILE
    cut = 1 + (len(early) // 2 if len(early) > 2 else 1)
    for n, copies in enumerate((early[:cut], early[cut:])):
        wait(copies)

        @pl.loop(0, tiles // 2)
        def _(t):
            at = (scalars[AT_Y] ^ n) * (tiles // 2) + t
            here = pl.ds(pl.multiple_of(at * TILE, TILE), TILE)
            h = dot_nn(low[...], up[:, here]) + up_bias[0:1, here]
            phi = 0.5 + 0.5 * lax.erf(h * SQRT_HALF)
            act[:, here] = (h * phi).astype(BF16)
            slope[:, here] = (phi + h * jnp.exp(-0.5 * h * h) * INV_ROOT_TWO_PI).astype(BF16)

    wait(late)
    acc[...] = dot_nt(act[...], down[...])
    groups, parts, piece, _ = out.shape
    block = seq // parts
    for part in range(parts):
        rows = pl.ds(part * block, block)
        normed = normal[rows, :] * vec[0:1, :] + vec[1:2, :]
        n, r = normalize(normed + acc[rows, :] + vec[2:3, :])
        n2[rows, :] = n
        r2[rows, :] = r
        at = part * block + lax.broadcasted_iota(jnp.int32, (block, 1), 0)
        final = (n * vec[3:4, :] + vec[4:5, :]) * (at < scalars[LEN]).astype(F32)
        out[:, part] = final.astype(BF16).reshape(groups, piece, features)
    sent = [move(out, out_out)]
    total = [jnp.zeros((1, features), F32)] * 3
    for part in range(parts):
        rows = pl.ds(part * block, block)
        at = part * block + lax.broadcasted_iota(jnp.int32, (block, 1), 0)
        e = cot[:, part].reshape(block, features).astype(F32) * (at < scalars[LEN]).astype(F32)
        n = n2[rows, :]
        grad = norm_backward(e, n, r2[rows, :], vec[3:4, :])
        g = grad.astype(BF16)
        acc[rows, :] = grad
        gffn[rows, :] = g
        more = [column_sum(g.astype(F32)), column_sum(e * n), column_sum(e)]
        total = [a + b for a, b in zip(total, more)]
    sums[...] = jnp.concatenate(total, axis=0)

    for n in range(2):

        @pl.loop(n * tiles // 2, (n + 1) * tiles // 2)
        def _(t):
            here = pl.ds(pl.multiple_of(t * TILE, TILE), TILE)
            store(scalars, grads, 1, t, dot_tn(gffn[...], act[:, here]).astype(BF16))
            g = (dot_nn(gffn[...], down[:, here]) * slope[:, here].astype(F32)).astype(BF16)
            slope[:, here] = g
            unit_sums[0:1, here] = column_sum(g.astype(F32))
            store(scalars, grads, 0, t, dot_tn(low[...], g).astype(BF16))

        done = pl.ds(n * (tiles // 2) * TILE, tiles // 2 * TILE)
        sent.append(move(slope.at[:, done], ghid_out.at[:, done]))
        if len(grad_outs) == 2:
            far = n ^ scalars[AT_Y]
            for c, o in enumerate(grad_outs):
                sent += [move(grads.at[c, 0, :, far], o.at[0, :, far]), move(grads.at[c, 1, far], o.at[1, far])]
    if len(grad_outs) == 1:
        sent.append(move(grads.at[0], grad_outs[0]))
    wait(sent)


def normed_kernel(load, load_out, scalars, ghid_in, second, normal_in, rscale_in, gain, *refs):
    weights, head_weights, _, (first, gattn, gatt, sums), scratch = refs
    move = Mover(scratch[-1])
    ghid, normal, rscale, acc, w_up, w_out = scratch[:-1]
    early = [move(ghid_in, ghid)] + load(move, scalars, weights, w_up)
    late = [move(s, d) for s, d in ((normal_in, normal), (rscale_in, rscale))]
    last = load_out(move, scalars, head_weights, w_out)
    seq, features = second.shape
    wait(early)
    acc[...] = dot_nt(ghid[...], flat(w_up)[...])
    wait(late)
    sums[...] = jnp.zeros_like(sums)

    @pl.loop(0, seq // ROWS)
    def _(t):
        rows = pl.ds(pl.multiple_of(t * ROWS, ROWS), ROWS)
        n = normal[rows, :]
        e = acc[rows, :] + second[rows, :]
        grad = norm_backward(e, n, rscale[rows, :], gain[...])
        g = grad.astype(BF16)
        first[rows, :] = grad
        gattn[rows, :] = g
        more = [column_sum(g.astype(F32)), column_sum(e * n), column_sum(e)]
        sums[...] += jnp.concatenate(more, axis=0)

    wait(last)
    gatt[...] = dot_nn(gattn[...], flat(w_out)[...]).astype(BF16)


def last_kernel(load, store, scalars, gatt, gattn, first, *refs):
    ins, (tokens,), (other,), first_pieces, second_pieces, outs, (sums,), scratch = refs
    own_out, other_out, *grad_outs = outs
    move = Mover(scratch[-1])
    q, k, v, att, lse, x, gq, gk, gv, rows_grad, w5, grads = scratch[:-1]
    early = [move(s, d) for s, d in zip(ins, (q, k, v, att, lse))]
    late = load_tokens(move, scalars, tokens, other, x)
    later = load[0](move, scalars, first_pieces, w5) + load[1](move, scalars, second_pieces, w5)
    wait(early)
    seq, features = q.shape
    scale = HEAD**-0.5
    live = lax.broadcasted_iota(jnp.int32, (1, seq), 1) < scalars[LEN]

    @pl.loop(0, features // PAIR)
    def _(pair):
        here = pair_of(pair)
        q2, k2, v2, do2 = q[:, here], k[:, here], v[:, here], gatt[:, here]
        both = do2.astype(F32) * att[:, here].astype(F32)
        column = lax.broadcasted_iota(jnp.int32, lse.shape, 1)
        logs = lse[...]
        q_turned, do_turned = q2.T, do2.T
        for_q, for_k, for_v = [], [], []
        for odd in range(2):
            log = jnp.sum(jnp.where(column == 2 * pair + odd, logs, 0.0), axis=-1, keepdims=True)
            inner = jnp.sum(of_head(both, odd), axis=-1, keepdims=True)
            s = jnp.where(live, dot_nt(q2, of_head(k2, odd)), -1e9)
            p = jnp.exp(s - log)
            gs = (p * (dot_nt(do2, of_head(v2, odd)) - inner)).astype(BF16)
            for_q.append(dot_nn(gs, k2))
            head = slice(odd * HEAD, (odd + 1) * HEAD)
            for_k.append(dot_nn(q_turned[head], gs))
            for_v.append(dot_nn(do_turned[head], p.astype(BF16)))
        g = (jnp.where(odd_lanes(for_q[0].shape), for_q[1], for_q[0]) * scale).astype(BF16)
        gq[:, here] = g
        sums[0:1, here] = column_sum(g.astype(F32))
        gk[:, here] = jnp.concatenate(for_k, axis=0).astype(BF16).T
        g = jnp.concatenate(for_v, axis=0).astype(BF16).T
        gv[:, here] = g
        sums[1:2, here] = column_sum(g.astype(F32))

    wait(late)
    store(scalars, grads, 0, dot_tn(x[...], gq[...]).astype(BF16))
    store(scalars, grads, 1, dot_tn(x[...], gk[...]).astype(BF16))
    store(scalars, grads, 2, dot_tn(x[...], gv[...]).astype(BF16))
    store(scalars, grads, 3, dot_tn(gattn[...], att[...]).astype(BF16))
    sent = [move(grads.at[n], o) for n, o in enumerate(grad_outs)]
    wait(later)
    w = flat(w5)
    total = first[...]
    for n, g in enumerate((gq, gk, gv)):
        total = total + dot_nt(g[...], w[:, pl.ds(n * features, features)])
    rows_grad[...] = total.astype(BF16)
    half = own_out.shape[0]
    for at, out in ((scalars[AT_Y], own_out), (1 - scalars[AT_Y], other_out)):
        sent.append(move(rows_grad.at[pl.ds(pl.multiple_of(at * half, half), half)], out))
    wait(sent)


def blocks(scalars, rows):
    for at_z in range(4):
        for at_x in range(2):
            for at_c in range(2):
                start = ((at_z * 2 + at_x) * 2 + at_c) * rows
                yield start, at_c ^ scalars[AT_C], at_x ^ scalars[AT_X], at_z ^ scalars[AT_Z]


def store_units(scalars, out, number, t, value):
    rows, width = out.shape[-2:]
    tiles = width // TILE
    col = pl.multiple_of((t % tiles) * TILE, TILE)
    far_y = (t // tiles) ^ scalars[AT_Y]
    for start, far_c, far_x, far_z in blocks(scalars, rows):
        one, two = (far_y, far_x) if number else (far_x, far_y)
        out[far_c, number, one, two, far_z, :, pl.ds(col, TILE)] = value[start : start + rows]


def store_heads(scalars, out, number, value):
    rows, width = out.shape[-2:]
    cols = width // 4
    col = number * cols
    for start, far_c, far_x, far_z in blocks(scalars, rows):
        for at_y in range(2):
            far = far_x * 2 + (at_y ^ scalars[AT_Y])
            piece = value[start : start + rows, at_y * cols : (at_y + 1) * cols]
            out[far_c, far, far_z, :, col : col + cols] = piece


def store_units_whole(scalars, out, number, t, value):
    out[0, number, :, pl.ds(pl.multiple_of(t * TILE, TILE), TILE)] = value


def store_heads_whole(scalars, out, number, value):
    cols = value.shape[1]
    out[0, :, number * cols : (number + 1) * cols] = value


def pick_kernel(scatter, order, src, dst):
    @pl.loop(0, dst.shape[0])
    def _(t):
        if scatter:
            dst[order[t]] = src[t]
        else:
            dst[t] = src[order[t]]


def pick(pieces, order, scatter):
    return pl.pallas_call(
        functools.partial(pick_kernel, scatter),
        out_shape=jax.ShapeDtypeStruct(pieces.shape, pieces.dtype),
        in_specs=[SMEM, VMEM],
        out_specs=VMEM,
        compiler_params=params(4),
        cost_estimate=cost(1),
        name="pick",
    )(order, pieces)


def in_hbm(value):
    return pltpu.with_memory_space_constraint(value, pltpu.HBM)


def in_vmem(value):
    if value.size < 1 << 16:
        return value
    return pltpu.with_memory_space_constraint(value, pltpu.VMEM)


def stays_near(shape):
    return shape if shape.size < 1 << 16 else pltpu.VMEM(shape.shape, shape.dtype)


def run(kernel, name, us, mib, scalars, ins, lists, outs, sums, scratch, sems):
    arrays = [in_vmem(a) if near else in_hbm(a) for a, near in ins] + [in_hbm(a) for some in lists for a in some]
    specs = [VMEM if near else HBM for _, near in ins] + [HBM for some in lists for _ in some]
    groups = [len(some) for some in lists]

    def body(scalars, *refs):
        refs = list(refs)

        def take(n):
            got, refs[:] = refs[:n], refs[n:]
            return got

        singles = take(len(ins))
        grouped = [take(n) for n in groups]
        grouped.append(take(len(outs)))
        if sums:
            grouped.append(take(len(sums)))
        kernel(scalars, *singles, *grouped, refs)

    def buffer(shape):
        return pltpu.VMEM(shape.shape, shape.dtype)

    return pl.pallas_call(
        body,
        out_shape=(*(pltpu.HBM(o.shape, o.dtype) for o in outs), *(stays_near(o) for o in sums)),
        in_specs=[SMEM] + specs,
        out_specs=(HBM,) * len(outs) + (VMEM,) * len(sums),
        scratch_shapes=[*map(buffer, scratch), pltpu.SemaphoreType.DMA((sems,))],
        compiler_params=params(mib),
        cost_estimate=cost(us),
        name=name,
    )(scalars, *arrays)


def add_up(values):
    total = values[0].astype(F32)
    for v in values[1:]:
        total = total + v.astype(F32)
    return total


def pairs(values):
    return (values[0] + values[1]) + (values[2] + values[3])


def split_wide(value):
    high = value.astype(BF16)
    low = (value - high.astype(F32)).astype(BF16)
    both = jnp.concatenate([high, low])
    return jnp.pad(both, ((0, -both.shape[0] % 16), (0, 0)))


def join_wide(rows, count):
    return rows[:count].astype(F32) + rows[count : 2 * count].astype(F32)


class Scatter:
    def __init__(self, keep, send, extra):
        self.keep, self.send, self.extra = keep, send, extra
        self.shape = keep.shape

    def core(self):
        self.got = exchange(self.send, C_BIT), exchange(self.extra, C_BIT)

    def _ready(self, terms):
        self.low = split_wide(self.extra)
        width = self.shape[-1]
        self.sent = [
            jnp.concatenate([add_up([t[m] for t in terms]).astype(BF16).reshape(-1, width), self.low])
            for m in (1, 2, 3)
        ]
        self.terms = [t[0] for t in terms]

    def _go(self, masks):
        self.got = [exchange(s, mask) for s, mask in zip(self.sent, masks)]

    def _came(self):
        rows = self.terms[0].size // self.shape[-1]
        count = self.extra.shape[0]
        self.extra = pairs([join_wide(r, count) for r in (self.low, *(g[rows:] for g in self.got))])
        return [g[:rows].reshape(self.terms[0].shape) for g in self.got]

    def ready_sides(self):
        near, extra = self.got
        self.extra = self.extra + extra
        self._ready([self.keep, near])

    def sides(self):
        self.got = [exchange(self.sent[0], Y_BIT), exchange(self.sent[1], X_BIT)]

    def corner(self):
        self.got.append(exchange(self.sent[2], X_BIT + Y_BIT))

    def along_z(self):
        self._ready(self.terms + self._came())
        self._go((Z_BIT, 2 * Z_BIT, 3 * Z_BIT))

    def total(self):
        return add_up(self.terms + self._came())


def combine_kernel(jobs, tails, *refs):
    refs = list(refs)

    def take(n):
        got, refs[:] = refs[:n], refs[n:]
        return got

    arrays = take(1 + max(n for job in jobs for part in job for n, _ in part))
    rows_in = take(2 if tails else 0)
    outs = take(len(jobs))
    rows_out = take(1 if tails else 0)
    move = Mover(refs.pop())
    into = [take(len(job)) for job in jobs]
    copies = [
        [move(arrays[n].at[at], ref.at[k]) for part, ref in zip(job, some) for k, (n, at) in enumerate(part)]
        for job, some in zip(jobs, into)
    ]
    if tails:
        total = rows_in[0][...] + rows_in[1][...]
        rows_out[0][...] = total
        below = split_wide(total)
    sent = []
    for number, (job, some, made) in enumerate(zip(jobs, into, refs)):
        wait(copies[number])
        at = 0
        for ref in some:
            terms, blocks, high, _ = ref.shape
            for b in range(blocks):
                total = ref[0, b].astype(F32)
                for k in range(1, terms):
                    total = total + ref[k, b].astype(F32)
                made[at : at + high] = total.astype(BF16)
                at += high
        if number in tails:
            made[at:] = below
        sent.append(move(made, outs[number]))
    wait(sent)


def combine(name, us, arrays, jobs, shape, tails=(), rows=()):
    blocks, high, width = shape
    outs = [
        jax.ShapeDtypeStruct((len(job) * blocks * high + (16 if n in tails else 0), width), BF16)
        for n, job in enumerate(jobs)
    ]
    scratch = [pltpu.VMEM((len(part), *shape), BF16) for job in jobs for part in job]
    scratch += [pltpu.VMEM(out.shape, BF16) for out in outs]
    copies = sum(len(part) for job in jobs for part in job) + len(jobs)
    return pl.pallas_call(
        functools.partial(combine_kernel, jobs, tails),
        out_shape=[pltpu.HBM(o.shape, o.dtype) for o in outs]
        + [jax.ShapeDtypeStruct(r.shape, r.dtype) for r in rows[:1]],
        in_specs=[HBM] * len(arrays) + [VMEM] * len(rows),
        out_specs=[HBM] * len(outs) + [VMEM] * len(rows[:1]),
        scratch_shapes=[*scratch, pltpu.SemaphoreType.DMA((copies,))],
        compiler_params=params(12),
        cost_estimate=cost(us),
        name=name,
    )(*map(in_hbm, arrays), *rows)


class ScatterTwo:
    def __init__(self, keep, send):
        self.keep, self.send = keep, send

    def core(self):
        self.got = exchange(self.send, C_BIT)

    def first_side(self):
        rows, width = self.send.shape[-2:]
        keep, near = (a.reshape(2, 2, 8, rows, width) for a in (self.keep, self.got))
        sent = combine("first_side", 3, [keep, near], [[[(n, (h, 1)) for n in range(2)]] for h in range(2)], (8, rows, width))
        self.terms = [[self.keep[h, 0], self.got[h, 0]] for h in range(2)]
        self.got = [exchange(s, m).reshape(2, 4, rows, width) for s, m in zip(sent, (X_BIT, Y_BIT))]

    def side(self, masks):
        got = []
        for n, mask in enumerate(masks):
            terms = self.terms[n] + [self.got[n]]
            got.append(exchange(add_up([t[1] for t in terms]).astype(BF16), mask))
            self.terms[n][:] = [t[0] for t in terms]
        self.got = got

    def along_z(self):
        terms = [self.terms[n] + [self.got[n]] for n in range(2)]
        self.got = []
        for m in (1, 2, 3):
            both = jnp.stack([add_up([t[m] for t in terms[n]]).astype(BF16) for n in range(2)])
            self.got.append(exchange(both, m * Z_BIT))
        self.terms = [[t[0] for t in terms[n]] for n in range(2)]

    def total(self):
        return [add_up(self.terms[n] + [g[n] for g in self.got]) for n in range(2)]


def scatter_whole(grad, rows, cols):
    size = lax.axis_size("tensor")
    parts = grad.reshape(-1, rows, size, cols).transpose(0, 2, 1, 3).reshape(-1, cols)
    return lax.psum_scatter(parts, BOTH, scatter_dimension=0, tiled=True).astype(F32)


def gather_whole(shard):
    size = lax.axis_size("tensor")
    rows, cols = shard.shape
    got = lax.all_gather(shard, BOTH, axis=0, tiled=False).reshape(-1, size, rows, cols)
    return got.transpose(0, 2, 1, 3).reshape(1, 1, 1, -1, size * cols)


def deal_start(block):
    micro, half, features = block.shape
    dp = lax.axis_size("dp")
    piece = half // dp
    pieces = block.reshape(micro, dp, piece, features).transpose(1, 0, 2, 3)
    pieces = pieces.reshape(dp, micro * piece, features)
    return lax.all_to_all(pieces, "dp", split_axis=0, concat_axis=0, tiled=True)


def deal_pick(spread, order, micro):
    dp, tall, features = spread.shape
    return pick(spread.reshape(dp * micro, tall // micro, features), order, True)


def deal_finish(chosen):
    got = lax.all_to_all(chosen, BOTH, split_axis=0, concat_axis=0, tiled=True)
    return got.reshape(lax.axis_size("dp"), lax.axis_size("tensor"), *chosen.shape[1:])


def collect_start(pieces):
    dp, size, piece, features = pieces.shape
    pieces = pieces.reshape(dp * size, piece, features)
    return lax.all_to_all(pieces, BOTH, split_axis=0, concat_axis=0, tiled=True)


def collect_pick(got, order):
    return pick(got, order, False)


def collect_start_back(chosen, micro):
    count, piece, features = chosen.shape
    chosen = chosen.reshape(count // micro, micro * piece, features)
    return lax.all_to_all(chosen, "dp", split_axis=0, concat_axis=0, tiled=True)


def collect_end(back, micro):
    dp, tall, features = back.shape
    back = back.reshape(dp, micro, tall // micro, features).transpose(1, 0, 2, 3)
    return back.reshape(micro, -1, features)


def on_device(
    tokens, cotangent, lengths, slot_order,
    query_weight, key_weight, value_weight, out_weight, up_weight, down_weight,
    query_bias, value_bias, out_bias, up_bias, down_bias,
    first_gain, first_offset, second_gain, second_offset,
):
    micro, half, features = tokens.shape
    dp, size = lax.axis_size("dp"), lax.axis_size("tensor")
    assert micro == size == 2
    dp_pos, at_y = lax.axis_index("dp"), lax.axis_index("tensor")
    rows, cols = query_weight.shape
    unit_cols = up_weight.shape[1]
    units = unit_cols * size
    seq = half * size
    at_c, at_x, at_z = dp_pos & 1, (dp_pos >> 1) & 1, dp_pos >> 2
    scalars = jnp.stack([lengths[dp_pos * size + at_y], at_z, at_x, at_c, at_y]).astype(jnp.int32)

    other_half = exchange(lax.dynamic_index_in_dim(tokens, 1 - at_y, 0, keepdims=False), Y_BIT)
    biases = jnp.concatenate([query_bias, value_bias, up_bias]).reshape(-1, cols)
    other_biases = exchange(biases, Y_BIT)

    def act(shape, dtype=BF16):
        return jax.ShapeDtypeStruct(shape, dtype)

    def merged(shapes):
        return act((len(shapes), *shapes[0].shape))

    split = dp == 16 and rows % 16 == 0
    if split:
        dims = (4, 2, 2, rows)
        places = (at_z, at_x, at_c, at_y)
        heads = Gather(
            jnp.concatenate([query_weight, key_weight], axis=1),
            jnp.concatenate([value_weight, out_weight], axis=1), places,
        )
        wide = Gather(up_weight, down_weight, places)
        heads.along_z()
        wide.along_z()
        heads.got, other_half, other_biases = tie(heads.got, other_half, other_biases)
        heads.first_side()
        heads.got, wide.got[:2] = tie(heads.got, wide.got[:2])
        heads.second_side()
        heads.got, wide.got, cotangent = tie(heads.got, wide.got, cotangent)
        heads.core()
        wide.first_side()
        spread = deal_start(cotangent)
        heads_a, heads_b = heads.pieces()
        heads_a, heads_b, wide.got = tie(heads_a, heads_b, wide.got)
        wide.second_side()
        chosen = deal_pick(spread, slot_order, micro)
        heads_a, heads_b, chosen = tie(heads_a, heads_b, chosen)
        cot = deal_finish(chosen)
        unit_spans = [(0, unit_cols, lambda y: y * unit_cols)]
        head_spans = [
            [(m * cols, cols, lambda y, n=2 * h + m: n * features + y * cols) for m in range(2)] for h in range(2)
        ]
        out_spans = [(cols, cols, lambda y: y * cols)]
        load_units = [functools.partial(load_pieces, second=h, spans=unit_spans) for h in range(2)]
        load_heads = [functools.partial(load_pieces, second=h, spans=head_spans[h]) for h in range(2)]
        load_out = functools.partial(load_pieces, second=1, spans=out_spans)
        put_units, put_heads = store_units, store_heads
        unit_grads = [act((2, 2, 2, 4, rows, unit_cols))] * 2
        head_grads = [act((4, 4, rows, 4 * cols))] * 2
    else:
        dims = (1, 1, 1, features)
        heads_a, heads_b = (
            [jnp.concatenate([gather_whole(w) for w in pair], axis=-1)]
            for pair in ((query_weight, key_weight), (value_weight, out_weight))
        )
        up_in, down_in = [gather_whole(up_weight)], [gather_whole(down_weight)]
        load_units = [functools.partial(load_whole, second=0, spans=[(0, units, 0)])] * 2
        load_heads = [
            functools.partial(load_whole, second=0, spans=[(0, 2 * features, h * 2 * features)]) for h in range(2)
        ]
        load_out = functools.partial(load_whole, second=0, spans=[(features, features, 0)])
        cot = deal_finish(deal_pick(deal_start(cotangent), slot_order, micro))
        put_units, put_heads = store_units_whole, store_heads_whole
        unit_grads = [act((2, features, units))]
        head_grads = [act((features, 4 * features))]

    biases = in_order(at_y, biases, other_biases, 1)
    full_query, full_value = biases[0].reshape(-1), biases[1].reshape(-1)
    full_up = biases[2:].transpose(1, 0, 2).reshape(1, units)

    low_rows, tall, column = act((seq, features)), act((seq, features), F32), act((seq, 1), F32)
    logs, low_units = act((seq, 128), F32), act((seq, units))
    head_vec = jnp.stack([full_query, full_value, out_bias, first_gain, first_offset])
    head_weights, unit_weights = act((*dims, 4 * features)), act((*dims, units))

    q, k, v, att, lse, n1, r1, low = run(
        functools.partial(attend_kernel, load_heads), "attend", 15, 24, scalars,
        [(tokens, False), (other_half, False), (head_vec, True)], [heads_a, heads_b],
        [low_rows] * 4 + [logs, tall, column, low_rows], [],
        [low_rows] * 5 + [logs, tall, column, low_rows, tall, head_weights], 48,
    )
    if split:
        low, wide.got, wide.near = tie(low, wide.got, wide.near)
        wide.core()
        up_in, down_in = wide.pieces()
    else:
        cot = cot.transpose(1, 0, 2, 3).reshape(1, size, half, features)

    middle_vec = jnp.stack([first_gain, first_offset, down_bias, second_gain, second_offset])
    dealt = act((dp, size, half // dp, features) if split else (1, size, half, features))
    out, ghid, *wide_grad, second, down_sums, unit_sums = run(
        functools.partial(middle_kernel, load_units, put_units), "middle", 24, 44, scalars,
        [(low, False), (n1, False), (cot, False), (middle_vec, True), (full_up, True)], [up_in, down_in],
        [dealt, low_units, *unit_grads], [tall, act((3, features), F32), act((1, units), F32)],
        [
            low_rows, tall, dealt, low_units, low_units, tall, column, dealt, low_rows,
            unit_weights, unit_weights, merged(unit_grads),
        ], 44,
    )
    if split:
        wide_sum = ScatterTwo(*wide_grad)
        wide_sum.core()
    else:
        out = out.reshape(size, dp, half // dp, features).transpose(1, 0, 2, 3)
    out = collect_start(out)

    if split:
        ghid, second, wide_sum.got = tie(ghid, second, wide_sum.got)
        wide_sum.first_side()
    first, gattn, gatt, up_sums = run(
        functools.partial(normed_kernel, load_units[0], load_out), "normed", 8, 20, scalars,
        [(ghid, False), (second, True), (n1, False), (r1, False), (first_gain[None], True)], [up_in, heads_b],
        [], [tall, low_rows, low_rows, act((3, features), F32)],
        [low_units, tall, column, tall, unit_weights, act((*dims, features))], 40,
    )
    own_grad, other_grad, *head_grad, head_sums = run(
        functools.partial(last_kernel, load_heads, put_heads), "last", 20, 28, scalars,
        [(gatt, True), (gattn, True), (first, True)], [[q, k, v, att, lse], [tokens], [other_half], heads_a, heads_b],
        [act((half, features)), act((half, features)), *head_grads], [act((2, features), F32)],
        [low_rows] * 4 + [logs] + [low_rows] * 5 + [head_weights, merged(head_grads)], 60,
    )
    sums = jnp.concatenate([down_sums, up_sums, head_sums, unit_sums.reshape(-1, features)])
    if split:
        head_grad, other_grad, sums, wide_sum.got, out = tie(head_grad, other_grad, sums, wide_sum.got, out)
        head_sum = Scatter(*head_grad, sums.reshape(-1, unit_cols))
        head_sum.core()
        wide_sum.side((Y_BIT, X_BIT))
        layer_out = collect_start_back(collect_pick(out, slot_order), micro)
        head_sum.ready_sides()
        head_sum.sent, head_sum.low, wide_sum.got = tie(head_sum.sent, head_sum.low, wide_sum.got)
        head_sum.sides()
        wide_sum.along_z()
        head_sum.sent[2], wide_sum.got[0] = tie(head_sum.sent[2], wide_sum.got[0])
        head_sum.corner()
        head_sum.got, wide_sum.got, layer_out, other_grad = tie(
            head_sum.got, wide_sum.got, layer_out, other_grad
        )
        other_grad = exchange(other_grad, Y_BIT)
        head_sum.along_z()
        layer_out = collect_end(layer_out, micro)
        total = head_sum.total()
        grads = [total[:, n * cols : (n + 1) * cols] for n in range(4)] + wide_sum.total()
        sums = head_sum.extra.reshape(-1, features)
    else:
        layer_out = collect_end(collect_start_back(collect_pick(out, slot_order), micro), micro)
        other_grad = exchange(other_grad, Y_BIT)
        cut = [head_grad[0][:, n * features : (n + 1) * features] for n in range(4)]
        grads = [scatter_whole(g, rows, cols) for g in cut]
        grads += [scatter_whole(wide_grad[0][n], rows, unit_cols) for n in range(2)]
        sums = lax.psum(sums, BOTH)
    input_grad = in_order(at_y, own_grad, other_grad)

    def own(vec, width):
        return lax.dynamic_slice_in_dim(vec, at_y * width, width)

    return (
        layer_out, input_grad, *grads,
        own(sums[6], cols), own(sums[7], cols), sums[3], own(sums[8:].reshape(-1), unit_cols), sums[0],
        sums[4], sums[5], sums[1], sums[2],
    )


def solution(mesh):
    rows = P("dp", "tensor", None)
    weight = P("dp", "tensor")
    cut = P("tensor")
    whole = P()
    return jax.shard_map(
        on_device,
        mesh=mesh,
        in_specs=(rows, rows, whole, whole, *(weight,) * 6, cut, cut, whole, cut, *(whole,) * 5),
        out_specs=(rows, rows, *(weight,) * 6, cut, cut, whole, cut, *(whole,) * 5),
        check_vma=False,
    )
```

```python
import functools

import jax
import jax.numpy as jnp
from jax import lax
from jax.experimental import pallas as pl
from jax.experimental.pallas import tpu as pltpu
from jax.sharding import PartitionSpec as P

HEAD = 64
PAIR = 2 * HEAD
EPSILON = 1e-05
SQRT_HALF = 0.7071067811865476
INV_ROOT_TWO_PI = 0.3989422804014327
BOTH = ("dp", "tensor")
F32 = jnp.float32
BF16 = jnp.bfloat16
TILE = 768
ROWS = 128
HBM = pl.BlockSpec(memory_space=pltpu.HBM)
VMEM = pl.BlockSpec(memory_space=pltpu.VMEM)
SMEM = pl.BlockSpec(memory_space=pltpu.SMEM)
LEN, AT_Z, AT_X, AT_C, AT_Y = range(5)
Y_BIT, C_BIT, X_BIT, Z_BIT = 1, 2, 4, 8


def dot_nn(a, b):
    return lax.dot_general(a, b, (((1,), (0,)), ((), ())), preferred_element_type=F32)


def dot_nt(a, b):
    return lax.dot_general(a, b, (((1,), (1,)), ((), ())), preferred_element_type=F32)


def dot_tn(a, b):
    return lax.dot_general(a, b, (((0,), (0,)), ((), ())), preferred_element_type=F32)


def params(mib):
    return pltpu.CompilerParams(vmem_limit_bytes=mib << 20)


def cost(us):
    return pl.CostEstimate(flops=int(us * 2e7), bytes_accessed=int(us * 6e4), transcendentals=0)


def tie(*values):
    return lax.optimization_barrier(values)


def exchange(value, mask):
    count = lax.axis_size("dp") * lax.axis_size("tensor")
    return lax.ppermute(value, BOTH, [(i, i ^ mask) for i in range(count)])


def in_order(bit_at, mine, other, axis=0):
    low = jnp.where(bit_at == 0, mine, other)
    high = jnp.where(bit_at == 0, other, mine)
    return jnp.stack([low, high], axis=axis)


class Gather:
    def __init__(self, first, second, places):
        self.places = places
        self.a, self.b = first, second

    def along_z(self):
        both = jnp.stack([self.a, self.b])
        self.both = both
        self.got = [exchange(both, m * Z_BIT) for m in (1, 2, 3)]

    def first_side(self):
        at_z = self.places[0]
        both, (g1, g2, g3) = self.both, self.got
        rows = []
        for z in range(4):
            far = jnp.where(at_z == z ^ 2, g2, g3)
            rows.append(jnp.where(at_z == z, both, jnp.where(at_z == z ^ 1, g1, far)))
        self.a = jnp.stack([r[0] for r in rows])
        self.b = jnp.stack([r[1] for r in rows])
        self.got = exchange(self.a, X_BIT), exchange(self.b, Y_BIT)

    def second_side(self):
        self.a = jnp.stack([self.a, self.got[0]])
        self.b = jnp.stack([self.b, self.got[1]])
        self.got = exchange(self.a, Y_BIT), exchange(self.b, X_BIT)
        self.near = exchange(self.a, C_BIT), exchange(self.b, C_BIT)

    def core(self):
        self.far = exchange(self.got[0], C_BIT), exchange(self.got[1], C_BIT)

    def pieces(self):
        return (
            [self.a, self.near[0], self.got[0], self.far[0]],
            [self.b, self.near[1], self.got[1], self.far[1]],
        )


class Mover:
    def __init__(self, sems):
        self.sems, self.used = sems, 0

    def __call__(self, src, dst):
        copy = pltpu.make_async_copy(src, dst, self.sems.at[self.used])
        self.used += 1
        copy.start()
        return copy


def wait(copies):
    for c in copies:
        c.wait()


def load_pieces(move, scalars, pieces, weight, second, spans):
    copies = []
    for number, piece in enumerate(pieces):
        far, other = number // 2, number % 2
        at_c = scalars[AT_C] ^ other
        for inner in range(2):
            if second:
                at_x, at_y = scalars[AT_X] ^ far, scalars[AT_Y] ^ inner
            else:
                at_x, at_y = scalars[AT_X] ^ inner, scalars[AT_Y] ^ far
            for start, width, to in spans:
                column = pl.multiple_of(to(at_y), 128)
                copies.append(
                    move(
                        piece.at[inner, :, :, pl.ds(start, width)],
                        weight.at[:, at_x, at_c, :, pl.ds(column, width)],
                    )
                )
    return copies


def load_whole(move, scalars, pieces, weight, second, spans):
    return [
        move(pieces[0].at[:, :, :, :, pl.ds(start, width)], weight.at[:, :, :, :, pl.ds(to, width)])
        for start, width, to in spans
    ]


def flat(weight):
    return weight.reshape(-1, weight.shape[-1])


def normalize(z):
    mean = jnp.mean(z, axis=-1, keepdims=True)
    center = z - mean
    rscale = lax.rsqrt(jnp.mean(center * center, axis=-1, keepdims=True) + EPSILON)
    return center * rscale, rscale


def norm_backward(e, normal, rscale, gain):
    scaled = e * gain
    mean = jnp.mean(scaled, axis=-1, keepdims=True)
    tilt = jnp.mean(scaled * normal, axis=-1, keepdims=True)
    return rscale * (scaled - mean - normal * tilt)


def column_sum(value):
    return jnp.sum(value, axis=0, keepdims=True)


def odd_lanes(shape):
    return lax.broadcasted_iota(jnp.int32, shape, len(shape) - 1) >= HEAD


def of_head(value, odd):
    mask = odd_lanes(value.shape)
    zero = jnp.zeros_like(value)
    return jnp.where(mask, value, zero) if odd else jnp.where(mask, zero, value)


def pair_of(t):
    return pl.ds(pl.multiple_of(t * PAIR, PAIR), PAIR)


def load_tokens(move, scalars, tokens, other, x):
    half = other.shape[0]
    at = scalars[AT_Y]
    return [
        move(tokens.at[at], x.at[pl.ds(pl.multiple_of(at * half, half), half)]),
        move(other, x.at[pl.ds(pl.multiple_of((1 - at) * half, half), half)]),
    ]


def attend_kernel(load, scalars, tokens, other, vec, *refs):
    first, second, outs, scratch = refs
    move = Mover(scratch[-1])
    x, q, k, v, att, lse, normal, rscale, low, acc, w5 = scratch[:-1]
    copies = load_tokens(move, scalars, tokens, other, x)
    for copy_set in (load[0](move, scalars, first, w5), load[1](move, scalars, second, w5)):
        copies += copy_set
    wait(copies)
    w = flat(w5)
    seq, features = x.shape
    live = lax.broadcasted_iota(jnp.int32, (1, seq), 1) < scalars[LEN]
    scale = HEAD**-0.5
    at_q, at_k, at_v, at_o = (pl.ds(n * features, features) for n in range(4))
    q[...] = ((dot_nn(x[...], w[:, at_q]) + vec[0:1, :]).astype(BF16).astype(F32) * scale).astype(BF16)
    k[...] = dot_nn(x[...], w[:, at_k]).astype(BF16)
    v[...] = (dot_nn(x[...], w[:, at_v]) + vec[1:2, :]).astype(BF16)
    sent = [move(s, o) for s, o in zip((q, k, v), outs[:3])]
    lse[...] = jnp.zeros_like(lse)

    @pl.loop(0, features // PAIR)
    def _(pair):
        here = pair_of(pair)
        q2, k2, v2 = q[:, here], k[:, here], v[:, here]
        column = lax.broadcasted_iota(jnp.int32, lse.shape, 1)
        parts = []
        logs = lse[...]
        for odd in range(2):
            s = jnp.where(live, dot_nt(q2, of_head(k2, odd)), -1e9)
            top = jnp.max(s, axis=-1, keepdims=True)
            e = jnp.exp(s - top)
            total = jnp.sum(e, axis=-1, keepdims=True)
            parts.append(dot_nn(e.astype(BF16), v2) * (1.0 / total))
            logs = jnp.where(column == 2 * pair + odd, top + jnp.log(total), logs)
        lse[...] = logs
        att[:, here] = jnp.where(odd_lanes(parts[0].shape), parts[1], parts[0]).astype(BF16)

    sent += [move(att, outs[3]), move(lse, outs[4])]
    acc[...] = dot_nt(att[...], w[:, at_o])

    @pl.loop(0, seq // ROWS)
    def _(t):
        rows = pl.ds(pl.multiple_of(t * ROWS, ROWS), ROWS)
        n, r = normalize(x[rows, :].astype(F32) + acc[rows, :] + vec[2:3, :])
        normal[rows, :] = n
        rscale[rows, :] = r
        low[rows, :] = (n * vec[3:4, :] + vec[4:5, :]).astype(BF16)

    sent += [move(s, o) for s, o in zip((normal, rscale, low), outs[5:])]
    wait(sent)


def middle_kernel(load, store, scalars, low_in, normal_in, cot_in, vec, up_bias, *refs):
    first, second, outs, (acc, sums, unit_sums), scratch = refs
    out_out, ghid_out, *grad_outs = outs
    move = Mover(scratch[-1])
    low, normal, cot, act, slope, n2, r2, out, gffn, w_up, w_down, grads = scratch[:-1]
    early = [move(low_in, low)] + load[0](move, scalars, first, w_up)
    late = load[1](move, scalars, second, w_down) + [move(normal_in, normal), move(cot_in, cot)]
    up, down = flat(w_up), flat(w_down)
    seq, features = low.shape
    tiles = up.shape[1] // TILE
    cut = 1 + (len(early) // 2 if len(early) > 2 else 1)
    for n, copies in enumerate((early[:cut], early[cut:])):
        wait(copies)

        @pl.loop(0, tiles // 2)
        def _(t):
            at = (scalars[AT_Y] ^ n) * (tiles // 2) + t
            here = pl.ds(pl.multiple_of(at * TILE, TILE), TILE)
            h = dot_nn(low[...], up[:, here]) + up_bias[0:1, here]
            phi = 0.5 + 0.5 * lax.erf(h * SQRT_HALF)
            act[:, here] = (h * phi).astype(BF16)
            slope[:, here] = (phi + h * jnp.exp(-0.5 * h * h) * INV_ROOT_TWO_PI).astype(BF16)

    wait(late)
    acc[...] = dot_nt(act[...], down[...])
    groups, parts, piece, _ = out.shape
    block = seq // parts
    for part in range(parts):
        rows = pl.ds(part * block, block)
        normed = normal[rows, :] * vec[0:1, :] + vec[1:2, :]
        n, r = normalize(normed + acc[rows, :] + vec[2:3, :])
        n2[rows, :] = n
        r2[rows, :] = r
        at = part * block + lax.broadcasted_iota(jnp.int32, (block, 1), 0)
        final = (n * vec[3:4, :] + vec[4:5, :]) * (at < scalars[LEN]).astype(F32)
        out[:, part] = final.astype(BF16).reshape(groups, piece, features)
    sent = [move(out, out_out)]
    total = [jnp.zeros((1, features), F32)] * 3
    for part in range(parts):
        rows = pl.ds(part * block, block)
        at = part * block + lax.broadcasted_iota(jnp.int32, (block, 1), 0)
        e = cot[:, part].reshape(block, features).astype(F32) * (at < scalars[LEN]).astype(F32)
        n = n2[rows, :]
        grad = norm_backward(e, n, r2[rows, :], vec[3:4, :])
        g = grad.astype(BF16)
        acc[rows, :] = grad
        gffn[rows, :] = g
        more = [column_sum(g.astype(F32)), column_sum(e * n), column_sum(e)]
        total = [a + b for a, b in zip(total, more)]
    sums[...] = jnp.concatenate(total, axis=0)

    for n in range(2):

        @pl.loop(n * tiles // 2, (n + 1) * tiles // 2)
        def _(t):
            here = pl.ds(pl.multiple_of(t * TILE, TILE), TILE)
            store(scalars, grads, 1, t, dot_tn(gffn[...], act[:, here]).astype(BF16))
            g = (dot_nn(gffn[...], down[:, here]) * slope[:, here].astype(F32)).astype(BF16)
            slope[:, here] = g
            unit_sums[0:1, here] = column_sum(g.astype(F32))
            store(scalars, grads, 0, t, dot_tn(low[...], g).astype(BF16))

        done = pl.ds(n * (tiles // 2) * TILE, tiles // 2 * TILE)
        sent.append(move(slope.at[:, done], ghid_out.at[:, done]))
        if len(grad_outs) == 2:
            far = n ^ scalars[AT_Y]
            for c, o in enumerate(grad_outs):
                sent += [move(grads.at[c, 0, :, far], o.at[0, :, far]), move(grads.at[c, 1, far], o.at[1, far])]
    if len(grad_outs) == 1:
        sent.append(move(grads.at[0], grad_outs[0]))
    wait(sent)


def normed_kernel(load, load_out, scalars, ghid_in, second, normal_in, rscale_in, gain, *refs):
    weights, head_weights, _, (first, gattn, gatt, sums), scratch = refs
    move = Mover(scratch[-1])
    ghid, normal, rscale, acc, w_up, w_out = scratch[:-1]
    early = [move(ghid_in, ghid)] + load(move, scalars, weights, w_up)
    late = [move(s, d) for s, d in ((normal_in, normal), (rscale_in, rscale))]
    last = load_out(move, scalars, head_weights, w_out)
    seq, features = second.shape
    wait(early)
    acc[...] = dot_nt(ghid[...], flat(w_up)[...])
    wait(late)
    sums[...] = jnp.zeros_like(sums)

    @pl.loop(0, seq // ROWS)
    def _(t):
        rows = pl.ds(pl.multiple_of(t * ROWS, ROWS), ROWS)
        n = normal[rows, :]
        e = acc[rows, :] + second[rows, :]
        grad = norm_backward(e, n, rscale[rows, :], gain[...])
        g = grad.astype(BF16)
        first[rows, :] = grad
        gattn[rows, :] = g
        more = [column_sum(g.astype(F32)), column_sum(e * n), column_sum(e)]
        sums[...] += jnp.concatenate(more, axis=0)

    wait(last)
    gatt[...] = dot_nn(gattn[...], flat(w_out)[...]).astype(BF16)


def last_kernel(load, store, scalars, gatt, gattn, first, *refs):
    ins, (tokens,), (other,), first_pieces, second_pieces, outs, (sums,), scratch = refs
    own_out, other_out, *grad_outs = outs
    move = Mover(scratch[-1])
    q, k, v, att, lse, x, gq, gk, gv, rows_grad, w5, grads = scratch[:-1]
    width = q.shape[1] // 2
    early = [move(ins[4], lse)]
    halves = []
    for at in (pl.ds(0, width), pl.ds(width, width)):
        halves.append([move(s.at[:, at], d.at[:, at]) for s, d in zip(ins, (q, k, v, att))])
    late = load_tokens(move, scalars, tokens, other, x)
    later = load[0](move, scalars, first_pieces, w5) + load[1](move, scalars, second_pieces, w5)
    wait(early)
    seq, features = q.shape
    scale = HEAD**-0.5
    live = lax.broadcasted_iota(jnp.int32, (1, seq), 1) < scalars[LEN]

    def one_pair(pair):
        here = pair_of(pair)
        q2, k2, v2, do2 = q[:, here], k[:, here], v[:, here], gatt[:, here]
        both = do2.astype(F32) * att[:, here].astype(F32)
        column = lax.broadcasted_iota(jnp.int32, lse.shape, 1)
        logs = lse[...]
        q_turned, do_turned = q2.T, do2.T
        for_q, for_k, for_v = [], [], []
        for odd in range(2):
            log = jnp.sum(jnp.where(column == 2 * pair + odd, logs, 0.0), axis=-1, keepdims=True)
            inner = jnp.sum(of_head(both, odd), axis=-1, keepdims=True)
            s = jnp.where(live, dot_nt(q2, of_head(k2, odd)), -1e9)
            p = jnp.exp(s - log)
            gs = (p * (dot_nt(do2, of_head(v2, odd)) - inner)).astype(BF16)
            for_q.append(dot_nn(gs, k2))
            head = slice(odd * HEAD, (odd + 1) * HEAD)
            for_k.append(dot_nn(q_turned[head], gs))
            for_v.append(dot_nn(do_turned[head], p.astype(BF16)))
        g = (jnp.where(odd_lanes(for_q[0].shape), for_q[1], for_q[0]) * scale).astype(BF16)
        gq[:, here] = g
        sums[0:1, here] = column_sum(g.astype(F32))
        gk[:, here] = jnp.concatenate(for_k, axis=0).astype(BF16).T
        g = jnp.concatenate(for_v, axis=0).astype(BF16).T
        gv[:, here] = g
        sums[1:2, here] = column_sum(g.astype(F32))

    pairs_there = features // PAIR // 2
    for n, copies in enumerate(halves):
        wait(copies)
        pl.loop(n * pairs_there, (n + 1) * pairs_there)(one_pair)

    wait(late)
    store(scalars, grads, 0, dot_tn(x[...], gq[...]).astype(BF16))
    store(scalars, grads, 1, dot_tn(x[...], gk[...]).astype(BF16))
    store(scalars, grads, 2, dot_tn(x[...], gv[...]).astype(BF16))
    store(scalars, grads, 3, dot_tn(gattn[...], att[...]).astype(BF16))
    sent = [move(grads.at[n], o) for n, o in enumerate(grad_outs)]
    wait(later)
    w = flat(w5)
    total = first[...]
    for n, g in enumerate((gq, gk, gv)):
        total = total + dot_nt(g[...], w[:, pl.ds(n * features, features)])
    rows_grad[...] = total.astype(BF16)
    half = own_out.shape[0]
    for at, out in ((scalars[AT_Y], own_out), (1 - scalars[AT_Y], other_out)):
        sent.append(move(rows_grad.at[pl.ds(pl.multiple_of(at * half, half), half)], out))
    wait(sent)


def blocks(scalars, rows):
    for at_z in range(4):
        for at_x in range(2):
            for at_c in range(2):
                start = ((at_z * 2 + at_x) * 2 + at_c) * rows
                yield start, at_c ^ scalars[AT_C], at_x ^ scalars[AT_X], at_z ^ scalars[AT_Z]


def store_units(scalars, out, number, t, value):
    rows, width = out.shape[-2:]
    tiles = width // TILE
    col = pl.multiple_of((t % tiles) * TILE, TILE)
    far_y = (t // tiles) ^ scalars[AT_Y]
    for start, far_c, far_x, far_z in blocks(scalars, rows):
        one, two = (far_y, far_x) if number else (far_x, far_y)
        out[far_c, number, one, two, far_z, :, pl.ds(col, TILE)] = value[start : start + rows]


def store_heads(scalars, out, number, value):
    rows, width = out.shape[-2:]
    cols = width // 4
    col = number * cols
    for start, far_c, far_x, far_z in blocks(scalars, rows):
        for at_y in range(2):
            far = far_x * 2 + (at_y ^ scalars[AT_Y])
            piece = value[start : start + rows, at_y * cols : (at_y + 1) * cols]
            out[far_c, far, far_z, :, col : col + cols] = piece


def store_units_whole(scalars, out, number, t, value):
    out[0, number, :, pl.ds(pl.multiple_of(t * TILE, TILE), TILE)] = value


def store_heads_whole(scalars, out, number, value):
    cols = value.shape[1]
    out[0, :, number * cols : (number + 1) * cols] = value


def pick_kernel(scatter, order, src, dst):
    @pl.loop(0, dst.shape[0])
    def _(t):
        if scatter:
            dst[order[t]] = src[t]
        else:
            dst[t] = src[order[t]]


def pick(pieces, order, scatter):
    return pl.pallas_call(
        functools.partial(pick_kernel, scatter),
        out_shape=jax.ShapeDtypeStruct(pieces.shape, pieces.dtype),
        in_specs=[SMEM, VMEM],
        out_specs=VMEM,
        compiler_params=params(4),
        cost_estimate=cost(1),
        name="pick",
    )(order, pieces)


def in_hbm(value):
    return pltpu.with_memory_space_constraint(value, pltpu.HBM)


def in_vmem(value):
    if value.size < 1 << 16:
        return value
    return pltpu.with_memory_space_constraint(value, pltpu.VMEM)


def stays_near(shape):
    return shape if shape.size < 1 << 16 else pltpu.VMEM(shape.shape, shape.dtype)


def run(kernel, name, us, mib, scalars, ins, lists, outs, sums, scratch, sems):
    arrays = [in_vmem(a) if near else in_hbm(a) for a, near in ins] + [in_hbm(a) for some in lists for a in some]
    specs = [VMEM if near else HBM for _, near in ins] + [HBM for some in lists for _ in some]
    groups = [len(some) for some in lists]

    def body(scalars, *refs):
        refs = list(refs)

        def take(n):
            got, refs[:] = refs[:n], refs[n:]
            return got

        singles = take(len(ins))
        grouped = [take(n) for n in groups]
        grouped.append(take(len(outs)))
        if sums:
            grouped.append(take(len(sums)))
        kernel(scalars, *singles, *grouped, refs)

    def buffer(shape):
        return pltpu.VMEM(shape.shape, shape.dtype)

    return pl.pallas_call(
        body,
        out_shape=(*(pltpu.HBM(o.shape, o.dtype) for o in outs), *(stays_near(o) for o in sums)),
        in_specs=[SMEM] + specs,
        out_specs=(HBM,) * len(outs) + (VMEM,) * len(sums),
        scratch_shapes=[*map(buffer, scratch), pltpu.SemaphoreType.DMA((sems,))],
        compiler_params=params(mib),
        cost_estimate=cost(us),
        name=name,
    )(scalars, *arrays)


def add_up(values):
    total = values[0].astype(F32)
    for v in values[1:]:
        total = total + v.astype(F32)
    return total


def pairs(values):
    return (values[0] + values[1]) + (values[2] + values[3])


def split_wide(value):
    high = value.astype(BF16)
    low = (value - high.astype(F32)).astype(BF16)
    space = ((0, 8 - value.shape[0]), (0, 0))
    return jnp.concatenate([jnp.pad(high, space), jnp.pad(low, space)])


def join_wide(rows, count):
    return rows[:count].astype(F32) + rows[8 : 8 + count].astype(F32)


def pairs(values):
    return (values[0] + values[1]) + (values[2] + values[3])


def split_wide(value):
    high = value.astype(BF16)
    low = (value - high.astype(F32)).astype(BF16)
    both = jnp.concatenate([high, low])
    return jnp.pad(both, ((0, -both.shape[0] % 16), (0, 0)))


def join_wide(rows, count):
    return rows[:count].astype(F32) + rows[count : 2 * count].astype(F32)


def finish_kernel(partial, own, first, second, third, *refs):
    outs, extra = refs[:-1], refs[-1]
    rows = partial.shape[0]
    last = [r[...].astype(F32) for r in (first, second, third)]
    total = partial[...] + last[0][:rows] + last[1][:rows] + last[2][:rows]
    cols = outs[0].shape[1]
    for n, out in enumerate(outs):
        out[...] = total[:, n * cols : (n + 1) * cols]
    low = own[...].astype(F32)
    extra[...] = pairs([r[:8] + r[8:] for r in (low, *(v[rows:] for v in last))])


def turn_kernel(keep, near, *refs):
    got, low = refs[:3], refs[3]
    sent, partial, next_low = refs[4:7], refs[7], refs[8]
    a, b, *parts, tails, sems = refs[9:]
    move = Mover(sems)
    blocks, rows, _ = a.shape
    copies = [move(keep.at[0], a), move(near.at[0], b)] + [move(g, p) for g, p in zip(got, parts)]
    wait(copies)
    extra = [low[...]] + [p[blocks * rows :] for p in parts]
    extra = pairs([(lambda v: v[:8] + v[8:])(e.astype(F32)) for e in extra])
    tails[...] = split_wide(extra)
    next_low[...] = tails[...]
    for z in range(blocks):
        at = slice(z * rows, (z + 1) * rows)
        total = a[z].astype(F32) + b[z].astype(F32)
        for p in parts:
            total = total + p[at].astype(F32)
        if z == 0:
            partial[...] = total
        else:
            sent[z - 1][:rows] = total.astype(BF16)
            sent[z - 1][rows:] = tails[...]


class Scatter:
    def __init__(self, keep, send, extra):
        self.keep, self.send, self.extra = keep, send, extra
        self.shape = keep.shape

    def core(self):
        self.got = exchange(self.send, C_BIT), exchange(self.extra, C_BIT)

    def _ready(self, terms):
        self.low = split_wide(self.extra)
        width = self.shape[-1]
        self.sent = [
            jnp.concatenate([add_up([t[m] for t in terms]).astype(BF16).reshape(-1, width), self.low])
            for m in (1, 2, 3)
        ]
        self.terms = [t[0] for t in terms]

    def _go(self, masks):
        self.got = [exchange(s, mask) for s, mask in zip(self.sent, masks)]

    def _came(self):
        rows = self.terms[0].size // self.shape[-1]
        count = self.extra.shape[0]
        self.extra = pairs([join_wide(r, count) for r in (self.low, *(g[rows:] for g in self.got))])
        return [g[:rows].reshape(self.terms[0].shape) for g in self.got]

    def ready_sides(self):
        near, extra = self.got
        self.near = near
        self.extra = self.extra + extra
        self._ready([self.keep, near])

    def sides(self):
        self.got = [exchange(self.sent[0], Y_BIT), exchange(self.sent[1], X_BIT)]

    def corner(self):
        self.got.append(exchange(self.sent[2], X_BIT + Y_BIT))

    def along_z(self):
        blocks, rows, width = self.shape[1:]
        low = jax.ShapeDtypeStruct((16, width), BF16)
        tall = jax.ShapeDtypeStruct((rows + 16, width), BF16)
        part = pltpu.VMEM((blocks, rows, width), BF16)
        *sent, self.partial, self.low = pl.pallas_call(
            turn_kernel,
            out_shape=(*(tall,) * 3, jax.ShapeDtypeStruct((rows, width), F32), low),
            in_specs=[HBM] * 5 + [VMEM],
            out_specs=(VMEM,) * 5,
            scratch_shapes=[
                part, part, *[pltpu.VMEM((blocks * rows + 16, width), BF16)] * 3, pltpu.VMEM((16, width), BF16),
                pltpu.SemaphoreType.DMA((5,)),
            ],
            compiler_params=params(10),
            cost_estimate=cost(2),
            name="turn",
        )(*map(in_hbm, (self.keep, self.near, *self.got)), self.low)
        self.got = [exchange(s, m * Z_BIT) for s, m in zip(sent, (1, 2, 3))]

    def finish(self, count):
        rows, width = self.shape[-2:]
        shapes = [jax.ShapeDtypeStruct((rows, width // count), F32)] * count
        *grads, extra = pl.pallas_call(
            finish_kernel,
            out_shape=(*shapes, jax.ShapeDtypeStruct((8, width), F32)),
            in_specs=[VMEM] * 5,
            out_specs=(VMEM,) * (count + 1),
            compiler_params=params(6),
            cost_estimate=cost(2),
            name="finish",
        )(self.partial, self.low, *self.got)
        return grads, extra[: self.extra.shape[0]]


def combine_kernel(jobs, tails, *refs):
    refs = list(refs)

    def take(n):
        got, refs[:] = refs[:n], refs[n:]
        return got

    arrays = take(1 + max(n for job in jobs for part in job for n, _ in part))
    rows_in = take(2 if tails else 0)
    outs = take(len(jobs))
    rows_out = take(1 if tails else 0)
    move = Mover(refs.pop())
    into = [take(len(job)) for job in jobs]
    copies = [
        [move(arrays[n].at[at], ref.at[k]) for part, ref in zip(job, some) for k, (n, at) in enumerate(part)]
        for job, some in zip(jobs, into)
    ]
    if tails:
        total = rows_in[0][...] + rows_in[1][...]
        rows_out[0][...] = total
        below = split_wide(total)
    sent = []
    for number, (job, some, made) in enumerate(zip(jobs, into, refs)):
        wait(copies[number])
        at = 0
        for ref in some:
            terms, blocks, high, _ = ref.shape
            for b in range(blocks):
                total = ref[0, b].astype(F32)
                for k in range(1, terms):
                    total = total + ref[k, b].astype(F32)
                made[at : at + high] = total.astype(BF16)
                at += high
        if number in tails:
            made[at:] = below
        sent.append(move(made, outs[number]))
    wait(sent)


def combine(name, us, arrays, jobs, shape, tails=(), rows=()):
    blocks, high, width = shape
    outs = [
        jax.ShapeDtypeStruct((len(job) * blocks * high + (16 if n in tails else 0), width), BF16)
        for n, job in enumerate(jobs)
    ]
    scratch = [pltpu.VMEM((len(part), *shape), BF16) for job in jobs for part in job]
    scratch += [pltpu.VMEM(out.shape, BF16) for out in outs]
    copies = sum(len(part) for job in jobs for part in job) + len(jobs)
    return pl.pallas_call(
        functools.partial(combine_kernel, jobs, tails),
        out_shape=[pltpu.HBM(o.shape, o.dtype) for o in outs]
        + [jax.ShapeDtypeStruct(r.shape, r.dtype) for r in rows[:1]],
        in_specs=[HBM] * len(arrays) + [VMEM] * len(rows),
        out_specs=[HBM] * len(outs) + [VMEM] * len(rows[:1]),
        scratch_shapes=[*scratch, pltpu.SemaphoreType.DMA((copies,))],
        compiler_params=params(12),
        cost_estimate=cost(us),
        name=name,
    )(*map(in_hbm, arrays), *rows)


class ScatterTwo:
    def __init__(self, keep, send):
        self.keep, self.send = keep, send

    def core(self):
        self.got = exchange(self.send, C_BIT)

    def first_side(self):
        self.rows, self.width = self.send.shape[-2:]
        self.arrays = [a.reshape(2, 2, 8, self.rows, self.width) for a in (self.keep, self.got)]
        sent = combine(
            "first_side", 3, self.arrays, [[[(n, (h, 1)) for n in range(2)]] for h in range(2)], (8, self.rows, self.width)
        )
        self.got = [exchange(s, m).reshape(8, self.rows, self.width) for s, m in zip(sent, (X_BIT, Y_BIT))]

    def second_side(self):
        self.arrays += self.got
        far = pl.ds(4, 4)
        sent = combine(
            "second_side", 3, self.arrays,
            [[[(0, (h, 0, far)), (1, (h, 0, far)), (2 + h, (far,))]] for h in range(2)],
            (4, self.rows, self.width),
        )
        self.got = [exchange(s, m).reshape(4, self.rows, self.width) for s, m in zip(sent, (Y_BIT, X_BIT))]

    def along_z(self):
        self.arrays += self.got
        jobs = [
            [[(0, (h, 0, at)), (1, (h, 0, at)), (2 + h, (at,)), (4 + h, (at,))] for h in range(2)]
            for at in (pl.ds(m, 1) for m in (1, 2, 3))
        ]
        sent = combine("along_z", 3, self.arrays, jobs, (1, self.rows, self.width))
        self.got = [exchange(s, m * Z_BIT) for s, m in zip(sent, (1, 2, 3))]

    def total(self):
        sums = []
        for h in range(2):
            terms = [self.arrays[n][h, 0, 0] for n in range(2)] + [self.arrays[n + h][0] for n in (2, 4)]
            sums.append(add_up(terms + [g[h * self.rows : (h + 1) * self.rows] for g in self.got]))
        return sums


def scatter_whole(grad, rows, cols):
    size = lax.axis_size("tensor")
    parts = grad.reshape(-1, rows, size, cols).transpose(0, 2, 1, 3).reshape(-1, cols)
    return lax.psum_scatter(parts, BOTH, scatter_dimension=0, tiled=True).astype(F32)


def gather_whole(shard):
    size = lax.axis_size("tensor")
    rows, cols = shard.shape
    got = lax.all_gather(shard, BOTH, axis=0, tiled=False).reshape(-1, size, rows, cols)
    return got.transpose(0, 2, 1, 3).reshape(1, 1, 1, -1, size * cols)


def deal_start(block):
    micro, half, features = block.shape
    dp = lax.axis_size("dp")
    piece = half // dp
    pieces = block.reshape(micro, dp, piece, features).transpose(1, 0, 2, 3)
    pieces = pieces.reshape(dp, micro * piece, features)
    return lax.all_to_all(pieces, "dp", split_axis=0, concat_axis=0, tiled=True)


def deal_pick(spread, order, micro):
    dp, tall, features = spread.shape
    return pick(spread.reshape(dp * micro, tall // micro, features), order, True)


def deal_finish(chosen):
    got = lax.all_to_all(chosen, BOTH, split_axis=0, concat_axis=0, tiled=True)
    return got.reshape(lax.axis_size("dp"), lax.axis_size("tensor"), *chosen.shape[1:])


def collect_start(pieces):
    dp, size, piece, features = pieces.shape
    pieces = pieces.reshape(dp * size, piece, features)
    return lax.all_to_all(pieces, BOTH, split_axis=0, concat_axis=0, tiled=True)


def collect_pick(got, order):
    return pick(got, order, False)


def collect_start_back(chosen, micro):
    count, piece, features = chosen.shape
    chosen = chosen.reshape(count // micro, micro * piece, features)
    return lax.all_to_all(chosen, "dp", split_axis=0, concat_axis=0, tiled=True)


def collect_end(back, micro):
    dp, tall, features = back.shape
    back = back.reshape(dp, micro, tall // micro, features).transpose(1, 0, 2, 3)
    return back.reshape(micro, -1, features)


def on_device(
    tokens, cotangent, lengths, slot_order,
    query_weight, key_weight, value_weight, out_weight, up_weight, down_weight,
    query_bias, value_bias, out_bias, up_bias, down_bias,
    first_gain, first_offset, second_gain, second_offset,
):
    micro, half, features = tokens.shape
    dp, size = lax.axis_size("dp"), lax.axis_size("tensor")
    assert micro == size == 2
    dp_pos, at_y = lax.axis_index("dp"), lax.axis_index("tensor")
    rows, cols = query_weight.shape
    unit_cols = up_weight.shape[1]
    units = unit_cols * size
    seq = half * size
    at_c, at_x, at_z = dp_pos & 1, (dp_pos >> 1) & 1, dp_pos >> 2
    scalars = jnp.stack([lengths[dp_pos * size + at_y], at_z, at_x, at_c, at_y]).astype(jnp.int32)

    other_half = exchange(lax.dynamic_index_in_dim(tokens, 1 - at_y, 0, keepdims=False), Y_BIT)
    biases = jnp.concatenate([query_bias, value_bias, up_bias]).reshape(-1, cols)
    other_biases = exchange(biases, Y_BIT)

    def act(shape, dtype=BF16):
        return jax.ShapeDtypeStruct(shape, dtype)

    def merged(shapes):
        return act((len(shapes), *shapes[0].shape))

    split = dp == 16 and rows % 16 == 0
    if split:
        dims = (4, 2, 2, rows)
        places = (at_z, at_x, at_c, at_y)
        heads = Gather(
            jnp.concatenate([query_weight, key_weight], axis=1),
            jnp.concatenate([value_weight, out_weight], axis=1), places,
        )
        wide = Gather(up_weight, down_weight, places)
        heads.along_z()
        wide.along_z()
        heads.got, other_half, other_biases = tie(heads.got, other_half, other_biases)
        heads.first_side()
        heads.got, wide.got[:2] = tie(heads.got, wide.got[:2])
        heads.second_side()
        heads.got, wide.got, cotangent = tie(heads.got, wide.got, cotangent)
        heads.core()
        wide.first_side()
        spread = deal_start(cotangent)
        heads_a, heads_b = heads.pieces()
        heads_a, heads_b, wide.got = tie(heads_a, heads_b, wide.got)
        wide.second_side()
        chosen = deal_pick(spread, slot_order, micro)
        heads_a, heads_b, chosen = tie(heads_a, heads_b, chosen)
        cot = deal_finish(chosen)
        unit_spans = [(0, unit_cols, lambda y: y * unit_cols)]
        head_spans = [
            [(m * cols, cols, lambda y, n=2 * h + m: n * features + y * cols) for m in range(2)] for h in range(2)
        ]
        out_spans = [(cols, cols, lambda y: y * cols)]
        load_units = [functools.partial(load_pieces, second=h, spans=unit_spans) for h in range(2)]
        load_heads = [functools.partial(load_pieces, second=h, spans=head_spans[h]) for h in range(2)]
        load_out = functools.partial(load_pieces, second=1, spans=out_spans)
        put_units, put_heads = store_units, store_heads
        unit_grads = [act((2, 2, 2, 4, rows, unit_cols))] * 2
        head_grads = [act((4, 4, rows, 4 * cols))] * 2
    else:
        dims = (1, 1, 1, features)
        heads_a, heads_b = (
            [jnp.concatenate([gather_whole(w) for w in pair], axis=-1)]
            for pair in ((query_weight, key_weight), (value_weight, out_weight))
        )
        up_in, down_in = [gather_whole(up_weight)], [gather_whole(down_weight)]
        load_units = [functools.partial(load_whole, second=0, spans=[(0, units, 0)])] * 2
        load_heads = [
            functools.partial(load_whole, second=0, spans=[(0, 2 * features, h * 2 * features)]) for h in range(2)
        ]
        load_out = functools.partial(load_whole, second=0, spans=[(features, features, 0)])
        cot = deal_finish(deal_pick(deal_start(cotangent), slot_order, micro))
        put_units, put_heads = store_units_whole, store_heads_whole
        unit_grads = [act((2, features, units))]
        head_grads = [act((features, 4 * features))]

    biases = in_order(at_y, biases, other_biases, 1)
    full_query, full_value = biases[0].reshape(-1), biases[1].reshape(-1)
    full_up = biases[2:].transpose(1, 0, 2).reshape(1, units)

    low_rows, tall, column = act((seq, features)), act((seq, features), F32), act((seq, 1), F32)
    logs, low_units = act((seq, 128), F32), act((seq, units))
    head_vec = jnp.stack([full_query, full_value, out_bias, first_gain, first_offset])
    head_weights, unit_weights = act((*dims, 4 * features)), act((*dims, units))

    q, k, v, att, lse, n1, r1, low = run(
        functools.partial(attend_kernel, load_heads), "attend", 15, 24, scalars,
        [(tokens, False), (other_half, False), (head_vec, True)], [heads_a, heads_b],
        [low_rows] * 4 + [logs, tall, column, low_rows], [],
        [low_rows] * 5 + [logs, tall, column, low_rows, tall, head_weights], 48,
    )
    if split:
        low, wide.got, wide.near = tie(low, wide.got, wide.near)
        wide.core()
        up_in, down_in = wide.pieces()
    else:
        cot = cot.transpose(1, 0, 2, 3).reshape(1, size, half, features)

    middle_vec = jnp.stack([first_gain, first_offset, down_bias, second_gain, second_offset])
    dealt = act((dp, size, half // dp, features) if split else (1, size, half, features))
    out, ghid, *wide_grad, second, down_sums, unit_sums = run(
        functools.partial(middle_kernel, load_units, put_units), "middle", 24, 44, scalars,
        [(low, False), (n1, False), (cot, False), (middle_vec, True), (full_up, True)], [up_in, down_in],
        [dealt, low_units, *unit_grads], [tall, act((3, features), F32), act((1, units), F32)],
        [
            low_rows, tall, dealt, low_units, low_units, tall, column, dealt, low_rows,
            unit_weights, unit_weights, merged(unit_grads),
        ], 44,
    )
    if split:
        wide_sum = ScatterTwo(*wide_grad)
        wide_sum.core()
    else:
        out = out.reshape(size, dp, half // dp, features).transpose(1, 0, 2, 3)
    out = collect_start(out)

    if split:
        ghid, second, wide_sum.got = tie(ghid, second, wide_sum.got)
        wide_sum.first_side()
    first, gattn, gatt, up_sums = run(
        functools.partial(normed_kernel, load_units[0], load_out), "normed", 8, 20, scalars,
        [(ghid, False), (second, True), (n1, False), (r1, False), (first_gain[None], True)], [up_in, heads_b],
        [], [tall, low_rows, low_rows, act((3, features), F32)],
        [low_units, tall, column, tall, unit_weights, act((*dims, features))], 40,
    )
    own_grad, other_grad, *head_grad, head_sums = run(
        functools.partial(last_kernel, load_heads, put_heads), "last", 20, 28, scalars,
        [(gatt, True), (gattn, True), (first, True)], [[q, k, v, att, lse], [tokens], [other_half], heads_a, heads_b],
        [act((half, features)), act((half, features)), *head_grads], [act((2, features), F32)],
        [low_rows] * 4 + [logs] + [low_rows] * 5 + [head_weights, merged(head_grads)], 60,
    )
    sums = jnp.concatenate([down_sums, up_sums, head_sums, unit_sums.reshape(-1, features)])
    if split:
        head_grad, other_grad, sums, wide_sum.got, out = tie(head_grad, other_grad, sums, wide_sum.got, out)
        head_sum = Scatter(*head_grad, sums.reshape(-1, unit_cols))
        head_sum.core()
        wide_sum.second_side()
        layer_out = collect_start_back(collect_pick(out, slot_order), micro)
        head_sum.ready_sides()
        head_sum.sent, head_sum.low, wide_sum.got = tie(head_sum.sent, head_sum.low, wide_sum.got)
        head_sum.sides()
        wide_sum.along_z()
        head_sum.corner()
        head_sum.got, wide_sum.got, layer_out, other_grad = tie(
            head_sum.got, wide_sum.got, layer_out, other_grad
        )
        input_grad = in_order(at_y, own_grad, exchange(other_grad, Y_BIT))
        head_sum.along_z()
        layer_out = collect_end(layer_out, micro)
        grads, sums = head_sum.finish(4)
        grads += wide_sum.total()
        sums = sums.reshape(-1, features)
    else:
        layer_out = collect_end(collect_start_back(collect_pick(out, slot_order), micro), micro)
        input_grad = in_order(at_y, own_grad, exchange(other_grad, Y_BIT))
        cut = [head_grad[0][:, n * features : (n + 1) * features] for n in range(4)]
        grads = [scatter_whole(g, rows, cols) for g in cut]
        grads += [scatter_whole(wide_grad[0][n], rows, unit_cols) for n in range(2)]
        sums = lax.psum(sums, BOTH)

    def own(vec, width):
        return lax.dynamic_slice_in_dim(vec, at_y * width, width)

    return (
        layer_out, input_grad, *grads,
        own(sums[6], cols), own(sums[7], cols), sums[3], own(sums[8:].reshape(-1), unit_cols), sums[0],
        sums[4], sums[5], sums[1], sums[2],
    )


def solution(mesh):
    rows = P("dp", "tensor", None)
    weight = P("dp", "tensor")
    cut = P("tensor")
    whole = P()
    return jax.shard_map(
        on_device,
        mesh=mesh,
        in_specs=(rows, rows, whole, whole, *(weight,) * 6, cut, cut, whole, cut, *(whole,) * 5),
        out_specs=(rows, rows, *(weight,) * 6, cut, cut, whole, cut, *(whole,) * 5),
        check_vma=False,
    )
```

```python
import functools

import jax
import jax.numpy as jnp
from jax import lax
from jax.experimental import pallas as pl
from jax.experimental.pallas import tpu as pltpu
from jax.sharding import PartitionSpec as P

HEAD = 64
PAIR = 2 * HEAD
EPSILON = 1e-05
SQRT_HALF = 0.7071067811865476
INV_ROOT_TWO_PI = 0.3989422804014327
BOTH = ("dp", "tensor")
F32 = jnp.float32
BF16 = jnp.bfloat16
TILE = 768
ROWS = 128
HBM = pl.BlockSpec(memory_space=pltpu.HBM)
VMEM = pl.BlockSpec(memory_space=pltpu.VMEM)
SMEM = pl.BlockSpec(memory_space=pltpu.SMEM)
LEN, AT_Z, AT_X, AT_C, AT_Y = range(5)
Y_BIT, C_BIT, X_BIT, Z_BIT = 1, 2, 4, 8


def dot_nn(a, b):
    return lax.dot_general(a, b, (((1,), (0,)), ((), ())), preferred_element_type=F32)


def dot_nt(a, b):
    return lax.dot_general(a, b, (((1,), (1,)), ((), ())), preferred_element_type=F32)


def dot_tn(a, b):
    return lax.dot_general(a, b, (((0,), (0,)), ((), ())), preferred_element_type=F32)


def params(mib):
    return pltpu.CompilerParams(vmem_limit_bytes=mib << 20)


def cost(us):
    return pl.CostEstimate(flops=int(us * 2e7), bytes_accessed=int(us * 6e4), transcendentals=0)


def tie(*values):
    return lax.optimization_barrier(values)


def exchange(value, mask):
    count = lax.axis_size("dp") * lax.axis_size("tensor")
    return lax.ppermute(value, BOTH, [(i, i ^ mask) for i in range(count)])


def in_order(bit_at, mine, other, axis=0):
    low = jnp.where(bit_at == 0, mine, other)
    high = jnp.where(bit_at == 0, other, mine)
    return jnp.stack([low, high], axis=axis)


class Gather:
    def __init__(self, first, second, places):
        self.places = places
        self.a, self.b = first, second

    def along_z(self):
        both = jnp.stack([self.a, self.b])
        self.both = both
        self.got = [exchange(both, m * Z_BIT) for m in (1, 2, 3)]

    def first_side(self):
        at_z = self.places[0]
        both, (g1, g2, g3) = self.both, self.got
        rows = []
        for z in range(4):
            far = jnp.where(at_z == z ^ 2, g2, g3)
            rows.append(jnp.where(at_z == z, both, jnp.where(at_z == z ^ 1, g1, far)))
        self.a = jnp.stack([r[0] for r in rows])
        self.b = jnp.stack([r[1] for r in rows])
        self.got = exchange(self.a, X_BIT), exchange(self.b, Y_BIT)

    def second_side(self):
        self.a = jnp.stack([self.a, self.got[0]])
        self.b = jnp.stack([self.b, self.got[1]])
        self.got = exchange(self.a, Y_BIT), exchange(self.b, X_BIT)
        self.near = exchange(self.a, C_BIT), exchange(self.b, C_BIT)

    def core(self):
        self.far = exchange(self.got[0], C_BIT), exchange(self.got[1], C_BIT)

    def pieces(self):
        return (
            [self.a, self.near[0], self.got[0], self.far[0]],
            [self.b, self.near[1], self.got[1], self.far[1]],
        )


class Mover:
    def __init__(self, sems):
        self.sems, self.used = sems, 0

    def __call__(self, src, dst):
        copy = pltpu.make_async_copy(src, dst, self.sems.at[self.used])
        self.used += 1
        copy.start()
        return copy


def wait(copies):
    for c in copies:
        c.wait()


def load_pieces(move, scalars, pieces, weight, second, spans):
    copies = []
    for number, piece in enumerate(pieces):
        far, other = number // 2, number % 2
        at_c = scalars[AT_C] ^ other
        for inner in range(2):
            if second:
                at_x, at_y = scalars[AT_X] ^ far, scalars[AT_Y] ^ inner
            else:
                at_x, at_y = scalars[AT_X] ^ inner, scalars[AT_Y] ^ far
            for start, width, to in spans:
                column = pl.multiple_of(to(at_y), 128)
                copies.append(
                    move(
                        piece.at[inner, :, :, pl.ds(start, width)],
                        weight.at[:, at_x, at_c, :, pl.ds(column, width)],
                    )
                )
    return copies


def load_whole(move, scalars, pieces, weight, second, spans):
    return [
        move(pieces[0].at[:, :, :, :, pl.ds(start, width)], weight.at[:, :, :, :, pl.ds(to, width)])
        for start, width, to in spans
    ]


def flat(weight):
    return weight.reshape(-1, weight.shape[-1])


def normalize(z):
    mean = jnp.mean(z, axis=-1, keepdims=True)
    center = z - mean
    rscale = lax.rsqrt(jnp.mean(center * center, axis=-1, keepdims=True) + EPSILON)
    return center * rscale, rscale


def norm_backward(e, normal, rscale, gain):
    scaled = e * gain
    mean = jnp.mean(scaled, axis=-1, keepdims=True)
    tilt = jnp.mean(scaled * normal, axis=-1, keepdims=True)
    return rscale * (scaled - mean - normal * tilt)


def column_sum(value):
    return jnp.sum(value, axis=0, keepdims=True)


def odd_lanes(shape):
    return lax.broadcasted_iota(jnp.int32, shape, len(shape) - 1) >= HEAD


def of_head(value, odd):
    mask = odd_lanes(value.shape)
    zero = jnp.zeros_like(value)
    return jnp.where(mask, value, zero) if odd else jnp.where(mask, zero, value)


def pair_of(t):
    return pl.ds(pl.multiple_of(t * PAIR, PAIR), PAIR)


def load_tokens(move, scalars, tokens, other, x):
    half = other.shape[0]
    at = scalars[AT_Y]
    return [
        move(tokens.at[at], x.at[pl.ds(pl.multiple_of(at * half, half), half)]),
        move(other, x.at[pl.ds(pl.multiple_of((1 - at) * half, half), half)]),
    ]


def attend_kernel(load, scalars, tokens, other, vec, *refs):
    first, second, outs, scratch = refs
    move = Mover(scratch[-1])
    x, q, k, v, att, lse, normal, rscale, low, acc, w5 = scratch[:-1]
    copies = load_tokens(move, scalars, tokens, other, x)
    for copy_set in (load[0](move, scalars, first, w5), load[1](move, scalars, second, w5)):
        copies += copy_set
    wait(copies)
    w = flat(w5)
    seq, features = x.shape
    live = lax.broadcasted_iota(jnp.int32, (1, seq), 1) < scalars[LEN]
    scale = HEAD**-0.5
    at_q, at_k, at_v, at_o = (pl.ds(n * features, features) for n in range(4))
    q[...] = ((dot_nn(x[...], w[:, at_q]) + vec[0:1, :]).astype(BF16).astype(F32) * scale).astype(BF16)
    k[...] = dot_nn(x[...], w[:, at_k]).astype(BF16)
    v[...] = (dot_nn(x[...], w[:, at_v]) + vec[1:2, :]).astype(BF16)
    sent = [move(s, o) for s, o in zip((q, k, v), outs[:3])]
    lse[...] = jnp.zeros_like(lse)

    @pl.loop(0, features // PAIR)
    def _(pair):
        here = pair_of(pair)
        q2, k2, v2 = q[:, here], k[:, here], v[:, here]
        column = lax.broadcasted_iota(jnp.int32, lse.shape, 1)
        parts = []
        logs = lse[...]
        for odd in range(2):
            s = jnp.where(live, dot_nt(q2, of_head(k2, odd)), -1e9)
            top = jnp.max(s, axis=-1, keepdims=True)
            e = jnp.exp(s - top)
            total = jnp.sum(e, axis=-1, keepdims=True)
            parts.append(dot_nn(e.astype(BF16), v2) * (1.0 / total))
            logs = jnp.where(column == 2 * pair + odd, top + jnp.log(total), logs)
        lse[...] = logs
        att[:, here] = jnp.where(odd_lanes(parts[0].shape), parts[1], parts[0]).astype(BF16)

    sent += [move(att, outs[3]), move(lse, outs[4])]
    acc[...] = dot_nt(att[...], w[:, at_o])

    @pl.loop(0, seq // ROWS)
    def _(t):
        rows = pl.ds(pl.multiple_of(t * ROWS, ROWS), ROWS)
        n, r = normalize(x[rows, :].astype(F32) + acc[rows, :] + vec[2:3, :])
        normal[rows, :] = n
        rscale[rows, :] = r
        low[rows, :] = (n * vec[3:4, :] + vec[4:5, :]).astype(BF16)

    sent += [move(s, o) for s, o in zip((normal, rscale, low), outs[5:])]
    wait(sent)


def middle_kernel(load, store, scalars, low_in, normal_in, cot_in, vec, up_bias, *refs):
    first, second, outs, (acc, sums, unit_sums), scratch = refs
    out_out, ghid_out, *grad_outs = outs
    move = Mover(scratch[-1])
    low, normal, cot, act, slope, n2, r2, out, gffn, w_up, w_down, grads = scratch[:-1]
    early = [move(low_in, low)] + load[0](move, scalars, first, w_up)
    late = load[1](move, scalars, second, w_down) + [move(normal_in, normal), move(cot_in, cot)]
    up, down = flat(w_up), flat(w_down)
    seq, features = low.shape
    tiles = up.shape[1] // TILE
    cut = 1 + (len(early) // 2 if len(early) > 2 else 1)
    for n, copies in enumerate((early[:cut], early[cut:])):
        wait(copies)

        @pl.loop(0, tiles // 2)
        def _(t):
            at = (scalars[AT_Y] ^ n) * (tiles // 2) + t
            here = pl.ds(pl.multiple_of(at * TILE, TILE), TILE)
            h = dot_nn(low[...], up[:, here]) + up_bias[0:1, here]
            phi = 0.5 + 0.5 * lax.erf(h * SQRT_HALF)
            act[:, here] = (h * phi).astype(BF16)
            slope[:, here] = (phi + h * jnp.exp(-0.5 * h * h) * INV_ROOT_TWO_PI).astype(BF16)

    wait(late)
    acc[...] = dot_nt(act[...], down[...])
    groups, parts, piece, _ = out.shape
    block = seq // parts
    for part in range(parts):
        rows = pl.ds(part * block, block)
        normed = normal[rows, :] * vec[0:1, :] + vec[1:2, :]
        n, r = normalize(normed + acc[rows, :] + vec[2:3, :])
        n2[rows, :] = n
        r2[rows, :] = r
        at = part * block + lax.broadcasted_iota(jnp.int32, (block, 1), 0)
        final = (n * vec[3:4, :] + vec[4:5, :]) * (at < scalars[LEN]).astype(F32)
        out[:, part] = final.astype(BF16).reshape(groups, piece, features)
    sent = [move(out, out_out)]
    total = [jnp.zeros((1, features), F32)] * 3
    for part in range(parts):
        rows = pl.ds(part * block, block)
        at = part * block + lax.broadcasted_iota(jnp.int32, (block, 1), 0)
        e = cot[:, part].reshape(block, features).astype(F32) * (at < scalars[LEN]).astype(F32)
        n = n2[rows, :]
        grad = norm_backward(e, n, r2[rows, :], vec[3:4, :])
        g = grad.astype(BF16)
        acc[rows, :] = grad
        gffn[rows, :] = g
        more = [column_sum(g.astype(F32)), column_sum(e * n), column_sum(e)]
        total = [a + b for a, b in zip(total, more)]
    sums[...] = jnp.concatenate(total, axis=0)

    for n in range(2):

        @pl.loop(n * tiles // 2, (n + 1) * tiles // 2)
        def _(t):
            here = pl.ds(pl.multiple_of(t * TILE, TILE), TILE)
            store(scalars, grads, 1, t, dot_tn(gffn[...], act[:, here]).astype(BF16))
            g = (dot_nn(gffn[...], down[:, here]) * slope[:, here].astype(F32)).astype(BF16)
            slope[:, here] = g
            unit_sums[0:1, here] = column_sum(g.astype(F32))
            store(scalars, grads, 0, t, dot_tn(low[...], g).astype(BF16))

        done = pl.ds(n * (tiles // 2) * TILE, tiles // 2 * TILE)
        sent.append(move(slope.at[:, done], ghid_out.at[:, done]))
        if len(grad_outs) == 2:
            far = n ^ scalars[AT_Y]
            for c, o in enumerate(grad_outs):
                sent += [move(grads.at[c, 0, :, far], o.at[0, :, far]), move(grads.at[c, 1, far], o.at[1, far])]
    if len(grad_outs) == 1:
        sent.append(move(grads.at[0], grad_outs[0]))
    wait(sent)


def normed_kernel(load, load_out, scalars, ghid_in, second, normal_in, rscale_in, gain, *refs):
    weights, head_weights, _, (first, gattn, gatt, sums), scratch = refs
    move = Mover(scratch[-1])
    ghid, normal, rscale, acc, w_up, w_out = scratch[:-1]
    early = [move(ghid_in, ghid)] + load(move, scalars, weights, w_up)
    late = [move(s, d) for s, d in ((normal_in, normal), (rscale_in, rscale))]
    last = load_out(move, scalars, head_weights, w_out)
    seq, features = second.shape
    wait(early)
    acc[...] = dot_nt(ghid[...], flat(w_up)[...])
    wait(late)
    sums[...] = jnp.zeros_like(sums)

    @pl.loop(0, seq // ROWS)
    def _(t):
        rows = pl.ds(pl.multiple_of(t * ROWS, ROWS), ROWS)
        n = normal[rows, :]
        e = acc[rows, :] + second[rows, :]
        grad = norm_backward(e, n, rscale[rows, :], gain[...])
        g = grad.astype(BF16)
        first[rows, :] = grad
        gattn[rows, :] = g
        more = [column_sum(g.astype(F32)), column_sum(e * n), column_sum(e)]
        sums[...] += jnp.concatenate(more, axis=0)

    wait(last)
    gatt[...] = dot_nn(gattn[...], flat(w_out)[...]).astype(BF16)


def last_kernel(load, store, scalars, gatt, gattn, first, *refs):
    ins, (tokens,), (other,), first_pieces, second_pieces, outs, (sums,), scratch = refs
    own_out, other_out, *grad_outs = outs
    move = Mover(scratch[-1])
    q, k, v, att, lse, x, gq, gk, gv, rows_grad, w5, grads = scratch[:-1]
    width = q.shape[1] // 2
    early = [move(ins[4], lse)]
    halves = []
    for at in (pl.ds(0, width), pl.ds(width, width)):
        halves.append([move(s.at[:, at], d.at[:, at]) for s, d in zip(ins, (q, k, v, att))])
    late = load_tokens(move, scalars, tokens, other, x)
    later = load[0](move, scalars, first_pieces, w5) + load[1](move, scalars, second_pieces, w5)
    wait(early)
    seq, features = q.shape
    scale = HEAD**-0.5
    live = lax.broadcasted_iota(jnp.int32, (1, seq), 1) < scalars[LEN]

    def one_pair(pair):
        here = pair_of(pair)
        q2, k2, v2, do2 = q[:, here], k[:, here], v[:, here], gatt[:, here]
        both = do2.astype(F32) * att[:, here].astype(F32)
        column = lax.broadcasted_iota(jnp.int32, lse.shape, 1)
        logs = lse[...]
        q_turned, do_turned = q2.T, do2.T
        for_q, for_k, for_v = [], [], []
        for odd in range(2):
            log = jnp.sum(jnp.where(column == 2 * pair + odd, logs, 0.0), axis=-1, keepdims=True)
            inner = jnp.sum(of_head(both, odd), axis=-1, keepdims=True)
            s = jnp.where(live, dot_nt(q2, of_head(k2, odd)), -1e9)
            p = jnp.exp(s - log)
            gs = (p * (dot_nt(do2, of_head(v2, odd)) - inner)).astype(BF16)
            for_q.append(dot_nn(gs, k2))
            head = slice(odd * HEAD, (odd + 1) * HEAD)
            for_k.append(dot_nn(q_turned[head], gs))
            for_v.append(dot_nn(do_turned[head], p.astype(BF16)))
        g = (jnp.where(odd_lanes(for_q[0].shape), for_q[1], for_q[0]) * scale).astype(BF16)
        gq[:, here] = g
        sums[0:1, here] = column_sum(g.astype(F32))
        gk[:, here] = jnp.concatenate(for_k, axis=0).astype(BF16).T
        g = jnp.concatenate(for_v, axis=0).astype(BF16).T
        gv[:, here] = g
        sums[1:2, here] = column_sum(g.astype(F32))

    pairs_there = features // PAIR // 2
    for n, copies in enumerate(halves):
        wait(copies)
        pl.loop(n * pairs_there, (n + 1) * pairs_there)(one_pair)

    wait(late)
    store(scalars, grads, 0, dot_tn(x[...], gq[...]).astype(BF16))
    store(scalars, grads, 1, dot_tn(x[...], gk[...]).astype(BF16))
    store(scalars, grads, 2, dot_tn(x[...], gv[...]).astype(BF16))
    store(scalars, grads, 3, dot_tn(gattn[...], att[...]).astype(BF16))
    sent = [move(grads.at[n], o) for n, o in enumerate(grad_outs)]
    wait(later)
    w = flat(w5)
    total = first[...]
    for n, g in enumerate((gq, gk, gv)):
        total = total + dot_nt(g[...], w[:, pl.ds(n * features, features)])
    rows_grad[...] = total.astype(BF16)
    half = own_out.shape[0]
    for at, out in ((scalars[AT_Y], own_out), (1 - scalars[AT_Y], other_out)):
        sent.append(move(rows_grad.at[pl.ds(pl.multiple_of(at * half, half), half)], out))
    wait(sent)


def blocks(scalars, rows):
    for at_z in range(4):
        for at_x in range(2):
            for at_c in range(2):
                start = ((at_z * 2 + at_x) * 2 + at_c) * rows
                yield start, at_c ^ scalars[AT_C], at_x ^ scalars[AT_X], at_z ^ scalars[AT_Z]


def store_units(scalars, out, number, t, value):
    rows, width = out.shape[-2:]
    tiles = width // TILE
    col = pl.multiple_of((t % tiles) * TILE, TILE)
    far_y = (t // tiles) ^ scalars[AT_Y]
    for start, far_c, far_x, far_z in blocks(scalars, rows):
        one, two = (far_y, far_x) if number else (far_x, far_y)
        out[far_c, number, one, two, far_z, :, pl.ds(col, TILE)] = value[start : start + rows]


def store_heads(scalars, out, number, value):
    rows, width = out.shape[-2:]
    cols = width // 4
    col = number * cols
    for start, far_c, far_x, far_z in blocks(scalars, rows):
        for at_y in range(2):
            far = far_x * 2 + (at_y ^ scalars[AT_Y])
            piece = value[start : start + rows, at_y * cols : (at_y + 1) * cols]
            out[far_c, far, far_z, :, col : col + cols] = piece


def store_units_whole(scalars, out, number, t, value):
    out[0, number, :, pl.ds(pl.multiple_of(t * TILE, TILE), TILE)] = value


def store_heads_whole(scalars, out, number, value):
    cols = value.shape[1]
    out[0, :, number * cols : (number + 1) * cols] = value


def pick_kernel(scatter, order, src, dst):
    @pl.loop(0, dst.shape[0])
    def _(t):
        if scatter:
            dst[order[t]] = src[t]
        else:
            dst[t] = src[order[t]]


def pick(pieces, order, scatter):
    return pl.pallas_call(
        functools.partial(pick_kernel, scatter),
        out_shape=jax.ShapeDtypeStruct(pieces.shape, pieces.dtype),
        in_specs=[SMEM, VMEM],
        out_specs=VMEM,
        compiler_params=params(4),
        cost_estimate=cost(1),
        name="pick",
    )(order, pieces)


def in_hbm(value):
    return pltpu.with_memory_space_constraint(value, pltpu.HBM)


def in_vmem(value):
    if value.size < 1 << 16:
        return value
    return pltpu.with_memory_space_constraint(value, pltpu.VMEM)


def stays_near(shape):
    return shape if shape.size < 1 << 16 else pltpu.VMEM(shape.shape, shape.dtype)


def run(kernel, name, us, mib, scalars, ins, lists, outs, sums, scratch, sems):
    arrays = [in_vmem(a) if near else in_hbm(a) for a, near in ins] + [in_hbm(a) for some in lists for a in some]
    specs = [VMEM if near else HBM for _, near in ins] + [HBM for some in lists for _ in some]
    groups = [len(some) for some in lists]

    def body(scalars, *refs):
        refs = list(refs)

        def take(n):
            got, refs[:] = refs[:n], refs[n:]
            return got

        singles = take(len(ins))
        grouped = [take(n) for n in groups]
        grouped.append(take(len(outs)))
        if sums:
            grouped.append(take(len(sums)))
        kernel(scalars, *singles, *grouped, refs)

    def buffer(shape):
        return pltpu.VMEM(shape.shape, shape.dtype)

    return pl.pallas_call(
        body,
        out_shape=(*(pltpu.HBM(o.shape, o.dtype) for o in outs), *(stays_near(o) for o in sums)),
        in_specs=[SMEM] + specs,
        out_specs=(HBM,) * len(outs) + (VMEM,) * len(sums),
        scratch_shapes=[*map(buffer, scratch), pltpu.SemaphoreType.DMA((sems,))],
        compiler_params=params(mib),
        cost_estimate=cost(us),
        name=name,
    )(scalars, *arrays)


def add_up(values):
    total = values[0].astype(F32)
    for v in values[1:]:
        total = total + v.astype(F32)
    return total


def pairs(values):
    return (values[0] + values[1]) + (values[2] + values[3])


def split_wide(value):
    high = value.astype(BF16)
    low = (value - high.astype(F32)).astype(BF16)
    space = ((0, 8 - value.shape[0]), (0, 0))
    return jnp.concatenate([jnp.pad(high, space), jnp.pad(low, space)])


def join_wide(rows, count):
    return rows[:count].astype(F32) + rows[8 : 8 + count].astype(F32)


def pairs(values):
    return (values[0] + values[1]) + (values[2] + values[3])


def split_wide(value):
    high = value.astype(BF16)
    low = (value - high.astype(F32)).astype(BF16)
    both = jnp.concatenate([high, low])
    return jnp.pad(both, ((0, -both.shape[0] % 16), (0, 0)))


def join_wide(rows, count):
    return rows[:count].astype(F32) + rows[count : 2 * count].astype(F32)


def finish_kernel(scalars, partial, own, first, second, third, *refs):
    grads, vectors, extra = refs[:4], refs[4:13], refs[13]
    rows = partial.shape[0]
    last = [r[...].astype(F32) for r in (first, second, third)]
    total = partial[...] + last[0][:rows] + last[1][:rows] + last[2][:rows]
    cols = grads[0].shape[1]
    for n, out in enumerate(grads):
        out[...] = total[:, n * cols : (n + 1) * cols]
    low = own[...].astype(F32)
    extra[...] = pairs([r[:8] + r[8:] for r in (low, *(v[rows:] for v in last))])
    features = extra.shape[1] // 2
    at_y = scalars[AT_Y]

    def put(out, row, start):
        out[...] = extra[pl.ds(row, 1), pl.ds(pl.multiple_of(start, 128), out.shape[-1])].reshape(out.shape)

    put(vectors[0], 3, at_y * cols)
    put(vectors[1], 3, features + at_y * cols)
    put(vectors[3], 4 + at_y, 0)
    for out, n in zip((vectors[2], *vectors[4:]), (3, 0, 4, 5, 1, 2)):
        put(out, n // 2, n % 2 * features)


def turn_kernel(keep, near, *refs):
    got, low = refs[:3], refs[3]
    sent, partial, next_low = refs[4:7], refs[7], refs[8]
    a, b, *parts, tails, sems = refs[9:]
    move = Mover(sems)
    blocks, rows, _ = a.shape
    copies = [move(keep.at[0], a), move(near.at[0], b)] + [move(g, p) for g, p in zip(got, parts)]
    wait(copies)
    extra = [low[...]] + [p[blocks * rows :] for p in parts]
    extra = pairs([(lambda v: v[:8] + v[8:])(e.astype(F32)) for e in extra])
    tails[...] = split_wide(extra)
    next_low[...] = tails[...]
    for z in range(blocks):
        at = slice(z * rows, (z + 1) * rows)
        total = a[z].astype(F32) + b[z].astype(F32)
        for p in parts:
            total = total + p[at].astype(F32)
        if z == 0:
            partial[...] = total
        else:
            sent[z - 1][:rows] = total.astype(BF16)
            sent[z - 1][rows:] = tails[...]


class Scatter:
    def __init__(self, keep, send, extra):
        self.keep, self.send, self.extra = keep, send, extra
        self.shape = keep.shape

    def core(self):
        self.got = exchange(self.send, C_BIT), exchange(self.extra, C_BIT)

    def _ready(self, terms):
        self.low = split_wide(self.extra)
        width = self.shape[-1]
        self.sent = [
            jnp.concatenate([add_up([t[m] for t in terms]).astype(BF16).reshape(-1, width), self.low])
            for m in (1, 2, 3)
        ]
        self.terms = [t[0] for t in terms]

    def _go(self, masks):
        self.got = [exchange(s, mask) for s, mask in zip(self.sent, masks)]

    def _came(self):
        rows = self.terms[0].size // self.shape[-1]
        count = self.extra.shape[0]
        self.extra = pairs([join_wide(r, count) for r in (self.low, *(g[rows:] for g in self.got))])
        return [g[:rows].reshape(self.terms[0].shape) for g in self.got]

    def ready_sides(self):
        near, extra = self.got
        self.near = near
        self.extra = self.extra + extra
        self._ready([self.keep, near])

    def sides(self):
        self.got = [exchange(self.sent[0], Y_BIT), exchange(self.sent[1], X_BIT)]

    def corner(self):
        self.got.append(exchange(self.sent[2], X_BIT + Y_BIT))

    def along_z(self):
        blocks, rows, width = self.shape[1:]
        low = jax.ShapeDtypeStruct((16, width), BF16)
        tall = jax.ShapeDtypeStruct((rows + 16, width), BF16)
        part = pltpu.VMEM((blocks, rows, width), BF16)
        *sent, self.partial, self.low = pl.pallas_call(
            turn_kernel,
            out_shape=(*(tall,) * 3, jax.ShapeDtypeStruct((rows, width), F32), low),
            in_specs=[HBM] * 5 + [VMEM],
            out_specs=(VMEM,) * 5,
            scratch_shapes=[
                part, part, *[pltpu.VMEM((blocks * rows + 16, width), BF16)] * 3, pltpu.VMEM((16, width), BF16),
                pltpu.SemaphoreType.DMA((5,)),
            ],
            compiler_params=params(10),
            cost_estimate=cost(2),
            name="turn",
        )(*map(in_hbm, (self.keep, self.near, *self.got)), self.low)
        self.got = [exchange(s, m * Z_BIT) for s, m in zip(sent, (1, 2, 3))]

    def finish(self, scalars, unit_cols, features):
        rows, width = self.shape[-2:]
        cols = width // 4

        def out(*shape):
            return jax.ShapeDtypeStruct(shape, F32)

        vectors = [out(n) for n in (cols, cols, features, unit_cols, *(features,) * 5)]
        return pl.pallas_call(
            finish_kernel,
            out_shape=(*[out(rows, cols)] * 4, *vectors),
            in_specs=[SMEM] + [VMEM] * 5,
            out_specs=(VMEM,) * 13,
            scratch_shapes=[pltpu.VMEM((8, width), F32)],
            compiler_params=params(6),
            cost_estimate=cost(2),
            name="finish",
        )(scalars, self.partial, self.low, *self.got)


def combine_kernel(jobs, *refs):
    refs = list(refs)

    def take(n):
        got, refs[:] = refs[:n], refs[n:]
        return got

    arrays = take(1 + max(n for job in jobs for n, _ in job))
    outs = take(len(jobs))
    move = Mover(refs.pop())
    into = take(len(jobs))
    copies = [
        [[move(arrays[n].at[(*at, b)], ref.at[k, b]) for k, (n, at) in enumerate(job)] for b in range(ref.shape[1])]
        for job, ref in zip(jobs, into)
    ]
    sent = []
    for number, (job, ref, made) in enumerate(zip(jobs, into, refs)):
        for b, some in enumerate(copies[number]):
            wait(some)
            for c in range(ref.shape[2]):
                total = ref[0, b, c].astype(F32)
                for k in range(1, len(job)):
                    total = total + ref[k, b, c].astype(F32)
                made[b, c] = total.astype(BF16)
            sent.append(move(made.at[b], outs[number].at[b]))
    wait(sent)


def combine(name, us, arrays, jobs, shape):
    outs = [jax.ShapeDtypeStruct(shape, BF16)] * len(jobs)
    scratch = [pltpu.VMEM((len(job), *shape), BF16) for job in jobs] + [pltpu.VMEM(shape, BF16)] * len(jobs)
    copies = shape[0] * (sum(map(len, jobs)) + len(jobs))
    return pl.pallas_call(
        functools.partial(combine_kernel, jobs),
        out_shape=[pltpu.HBM(o.shape, o.dtype) for o in outs],
        in_specs=[HBM] * len(arrays),
        out_specs=[HBM] * len(outs),
        scratch_shapes=[*scratch, pltpu.SemaphoreType.DMA((copies,))],
        compiler_params=params(12),
        cost_estimate=cost(us),
        name=name,
    )(*map(in_hbm, arrays))


def along_z_kernel(keep, near, *refs):
    got, sent = refs[:4], refs[4:7]
    parts, made = refs[7], refs[8]
    move = Mover(refs[9])
    copies = []
    far = pl.ds(1, 3)
    for h in range(2):
        terms = (keep.at[h, 0, 0], near.at[h, 0, 0], got[h].at[0], got[2 + h])
        copies.append([move(t.at[far], parts.at[h, k]) for k, t in enumerate(terms)])
    moved = []
    for h in range(2):
        wait(copies[h])
        for m in range(3):
            total = parts[h, 0, m].astype(F32)
            for k in range(1, 4):
                total = total + parts[h, k, m].astype(F32)
            made[m, h] = total.astype(BF16)
            if h:
                moved.append(move(made.at[m], sent[m]))
    wait(moved)


class ScatterTwo:
    def __init__(self, keep, send):
        self.keep, self.send = keep, send

    def core(self):
        self.got = exchange(self.send, C_BIT)

    def first_side(self):
        self.arrays = [self.keep, self.got]
        jobs = [[(n, (h, 1)) for n in range(2)] for h in range(2)]
        sent = combine("first_side", 3, self.arrays, jobs, self.keep.shape[2:])
        self.got = [exchange(s, m) for s, m in zip(sent, (X_BIT, Y_BIT))]

    def second_side(self):
        self.arrays += self.got
        blocks = self.keep.shape[3:]
        jobs = [[(0, (h, 0, 1)), (1, (h, 0, 1)), (2 + h, (1,))] for h in range(2)]
        arrays = [a.reshape(*a.shape[:-3], 2, 2, *a.shape[-2:]) for a in self.arrays]
        sent = combine("second_side", 3, arrays, jobs, (2, 2, *blocks[1:]))
        self.got = [exchange(s, m).reshape(blocks) for s, m in zip(sent, (Y_BIT, X_BIT))]

    def along_z(self):
        self.arrays += self.got
        rows, width = self.keep.shape[-2:]
        out = pltpu.HBM((2, rows, width), BF16)
        sent = pl.pallas_call(
            along_z_kernel,
            out_shape=[out] * 3,
            in_specs=[HBM] * 6,
            out_specs=[HBM] * 3,
            scratch_shapes=[
                pltpu.VMEM((2, 4, 3, rows, width), BF16), pltpu.VMEM((3, 2, rows, width), BF16),
                pltpu.SemaphoreType.DMA((11,)),
            ],
            compiler_params=params(8),
            cost_estimate=cost(3),
            name="along_z",
        )(*map(in_hbm, self.arrays))
        self.got = [exchange(s, m * Z_BIT) for s, m in zip(sent, (1, 2, 3))]

    def total(self):
        sums = []
        for h in range(2):
            terms = [self.arrays[n][h, 0, 0, 0] for n in range(2)] + [self.arrays[2 + h][0, 0], self.arrays[4 + h][0]]
            sums.append(add_up(terms + [g[h] for g in self.got]))
        return sums


def scatter_whole(grad, rows, cols):
    size = lax.axis_size("tensor")
    parts = grad.reshape(-1, rows, size, cols).transpose(0, 2, 1, 3).reshape(-1, cols)
    return lax.psum_scatter(parts, BOTH, scatter_dimension=0, tiled=True).astype(F32)


def gather_whole(shard):
    size = lax.axis_size("tensor")
    rows, cols = shard.shape
    got = lax.all_gather(shard, BOTH, axis=0, tiled=False).reshape(-1, size, rows, cols)
    return got.transpose(0, 2, 1, 3).reshape(1, 1, 1, -1, size * cols)


def deal_start(block):
    micro, half, features = block.shape
    dp = lax.axis_size("dp")
    piece = half // dp
    pieces = block.reshape(micro, dp, piece, features).transpose(1, 0, 2, 3)
    pieces = pieces.reshape(dp, micro * piece, features)
    return lax.all_to_all(pieces, "dp", split_axis=0, concat_axis=0, tiled=True)


def deal_pick(spread, order, micro):
    dp, tall, features = spread.shape
    return pick(spread.reshape(dp * micro, tall // micro, features), order, True)


def deal_finish(chosen):
    got = lax.all_to_all(chosen, BOTH, split_axis=0, concat_axis=0, tiled=True)
    return got.reshape(lax.axis_size("dp"), lax.axis_size("tensor"), *chosen.shape[1:])


def collect_start(pieces):
    dp, size, piece, features = pieces.shape
    pieces = pieces.reshape(dp * size, piece, features)
    return lax.all_to_all(pieces, BOTH, split_axis=0, concat_axis=0, tiled=True)


def collect_pick(got, order):
    return pick(got, order, False)


def collect_start_back(chosen, micro):
    count, piece, features = chosen.shape
    chosen = chosen.reshape(count // micro, micro * piece, features)
    return lax.all_to_all(chosen, "dp", split_axis=0, concat_axis=0, tiled=True)


def collect_end(back, micro):
    dp, tall, features = back.shape
    back = back.reshape(dp, micro, tall // micro, features).transpose(1, 0, 2, 3)
    return back.reshape(micro, -1, features)


def on_device(
    tokens, cotangent, lengths, slot_order,
    query_weight, key_weight, value_weight, out_weight, up_weight, down_weight,
    query_bias, value_bias, out_bias, up_bias, down_bias,
    first_gain, first_offset, second_gain, second_offset,
):
    micro, half, features = tokens.shape
    dp, size = lax.axis_size("dp"), lax.axis_size("tensor")
    assert micro == size == 2
    dp_pos, at_y = lax.axis_index("dp"), lax.axis_index("tensor")
    rows, cols = query_weight.shape
    unit_cols = up_weight.shape[1]
    units = unit_cols * size
    seq = half * size
    at_c, at_x, at_z = dp_pos & 1, (dp_pos >> 1) & 1, dp_pos >> 2
    scalars = jnp.stack([lengths[dp_pos * size + at_y], at_z, at_x, at_c, at_y]).astype(jnp.int32)

    other_half = exchange(lax.dynamic_index_in_dim(tokens, 1 - at_y, 0, keepdims=False), Y_BIT)
    biases = jnp.concatenate([query_bias, value_bias, up_bias]).reshape(-1, cols)
    other_biases = exchange(biases, Y_BIT)

    def act(shape, dtype=BF16):
        return jax.ShapeDtypeStruct(shape, dtype)

    def merged(shapes):
        return act((len(shapes), *shapes[0].shape))

    split = dp == 16 and rows % 16 == 0
    if split:
        dims = (4, 2, 2, rows)
        places = (at_z, at_x, at_c, at_y)
        heads = Gather(
            jnp.concatenate([query_weight, key_weight], axis=1),
            jnp.concatenate([value_weight, out_weight], axis=1), places,
        )
        wide = Gather(up_weight, down_weight, places)
        heads.along_z()
        wide.along_z()
        heads.got, other_half, other_biases = tie(heads.got, other_half, other_biases)
        heads.first_side()
        heads.got, wide.got[:2] = tie(heads.got, wide.got[:2])
        heads.second_side()
        heads.got, wide.got, cotangent = tie(heads.got, wide.got, cotangent)
        heads.core()
        wide.first_side()
        spread = deal_start(cotangent)
        heads_a, heads_b = heads.pieces()
        heads_a, heads_b, wide.got = tie(heads_a, heads_b, wide.got)
        wide.second_side()
        chosen = deal_pick(spread, slot_order, micro)
        heads_a, heads_b, chosen = tie(heads_a, heads_b, chosen)
        cot = deal_finish(chosen)
        unit_spans = [(0, unit_cols, lambda y: y * unit_cols)]
        head_spans = [
            [(m * cols, cols, lambda y, n=2 * h + m: n * features + y * cols) for m in range(2)] for h in range(2)
        ]
        out_spans = [(cols, cols, lambda y: y * cols)]
        load_units = [functools.partial(load_pieces, second=h, spans=unit_spans) for h in range(2)]
        load_heads = [functools.partial(load_pieces, second=h, spans=head_spans[h]) for h in range(2)]
        load_out = functools.partial(load_pieces, second=1, spans=out_spans)
        put_units, put_heads = store_units, store_heads
        unit_grads = [act((2, 2, 2, 4, rows, unit_cols))] * 2
        head_grads = [act((4, 4, rows, 4 * cols))] * 2
    else:
        dims = (1, 1, 1, features)
        heads_a, heads_b = (
            [jnp.concatenate([gather_whole(w) for w in pair], axis=-1)]
            for pair in ((query_weight, key_weight), (value_weight, out_weight))
        )
        up_in, down_in = [gather_whole(up_weight)], [gather_whole(down_weight)]
        load_units = [functools.partial(load_whole, second=0, spans=[(0, units, 0)])] * 2
        load_heads = [
            functools.partial(load_whole, second=0, spans=[(0, 2 * features, h * 2 * features)]) for h in range(2)
        ]
        load_out = functools.partial(load_whole, second=0, spans=[(features, features, 0)])
        cot = deal_finish(deal_pick(deal_start(cotangent), slot_order, micro))
        put_units, put_heads = store_units_whole, store_heads_whole
        unit_grads = [act((2, features, units))]
        head_grads = [act((features, 4 * features))]

    biases = in_order(at_y, biases, other_biases, 1)
    full_query, full_value = biases[0].reshape(-1), biases[1].reshape(-1)
    full_up = biases[2:].transpose(1, 0, 2).reshape(1, units)

    low_rows, tall, column = act((seq, features)), act((seq, features), F32), act((seq, 1), F32)
    logs, low_units = act((seq, 128), F32), act((seq, units))
    head_vec = jnp.stack([full_query, full_value, out_bias, first_gain, first_offset])
    head_weights, unit_weights = act((*dims, 4 * features)), act((*dims, units))

    q, k, v, att, lse, n1, r1, low = run(
        functools.partial(attend_kernel, load_heads), "attend", 15, 24, scalars,
        [(tokens, False), (other_half, False), (head_vec, True)], [heads_a, heads_b],
        [low_rows] * 4 + [logs, tall, column, low_rows], [],
        [low_rows] * 5 + [logs, tall, column, low_rows, tall, head_weights], 48,
    )
    if split:
        low, wide.got, wide.near = tie(low, wide.got, wide.near)
        wide.core()
        up_in, down_in = wide.pieces()
    else:
        cot = cot.transpose(1, 0, 2, 3).reshape(1, size, half, features)

    middle_vec = jnp.stack([first_gain, first_offset, down_bias, second_gain, second_offset])
    dealt = act((dp, size, half // dp, features) if split else (1, size, half, features))
    out, ghid, *wide_grad, second, down_sums, unit_sums = run(
        functools.partial(middle_kernel, load_units, put_units), "middle", 24, 44, scalars,
        [(low, False), (n1, False), (cot, False), (middle_vec, True), (full_up, True)], [up_in, down_in],
        [dealt, low_units, *unit_grads], [tall, act((3, features), F32), act((1, units), F32)],
        [
            low_rows, tall, dealt, low_units, low_units, tall, column, dealt, low_rows,
            unit_weights, unit_weights, merged(unit_grads),
        ], 44,
    )
    if split:
        wide_sum = ScatterTwo(*wide_grad)
        wide_sum.core()
    else:
        out = out.reshape(size, dp, half // dp, features).transpose(1, 0, 2, 3)
    out = collect_start(out)

    if split:
        ghid, second, wide_sum.got = tie(ghid, second, wide_sum.got)
        wide_sum.first_side()
    first, gattn, gatt, up_sums = run(
        functools.partial(normed_kernel, load_units[0], load_out), "normed", 8, 20, scalars,
        [(ghid, False), (second, True), (n1, False), (r1, False), (first_gain[None], True)], [up_in, heads_b],
        [], [tall, low_rows, low_rows, act((3, features), F32)],
        [low_units, tall, column, tall, unit_weights, act((*dims, features))], 40,
    )
    own_grad, other_grad, *head_grad, head_sums = run(
        functools.partial(last_kernel, load_heads, put_heads), "last", 20, 28, scalars,
        [(gatt, True), (gattn, True), (first, True)], [[q, k, v, att, lse], [tokens], [other_half], heads_a, heads_b],
        [act((half, features)), act((half, features)), *head_grads], [act((2, features), F32)],
        [low_rows] * 4 + [logs] + [low_rows] * 5 + [head_weights, merged(head_grads)], 60,
    )
    sums = jnp.concatenate([down_sums, up_sums, head_sums, unit_sums.reshape(-1, features)])
    if split:
        head_grad, other_grad, sums, wide_sum.got, out = tie(head_grad, other_grad, sums, wide_sum.got, out)
        head_sum = Scatter(*head_grad, sums.reshape(-1, unit_cols))
        head_sum.core()
        wide_sum.second_side()
        layer_out = collect_start_back(collect_pick(out, slot_order), micro)
        head_sum.ready_sides()
        head_sum.sent, head_sum.low, wide_sum.got = tie(head_sum.sent, head_sum.low, wide_sum.got)
        head_sum.sides()
        wide_sum.along_z()
        head_sum.corner()
        head_sum.got, wide_sum.got, layer_out, other_grad = tie(
            head_sum.got, wide_sum.got, layer_out, other_grad
        )
        input_grad = in_order(at_y, own_grad, exchange(other_grad, Y_BIT))
        head_sum.along_z()
        layer_out = collect_end(layer_out, micro)
        head_sum.got[0], input_grad = tie(head_sum.got[0], input_grad)
        results = head_sum.finish(scalars, unit_cols, features)
        grads = [*results[:4], *wide_sum.total()]
        vectors = results[4:]
    else:
        layer_out = collect_end(collect_start_back(collect_pick(out, slot_order), micro), micro)
        input_grad = in_order(at_y, own_grad, exchange(other_grad, Y_BIT))
        cut = [head_grad[0][:, n * features : (n + 1) * features] for n in range(4)]
        grads = [scatter_whole(g, rows, cols) for g in cut]
        grads += [scatter_whole(wide_grad[0][n], rows, unit_cols) for n in range(2)]
        sums = lax.psum(sums, BOTH)

        def own(vec, width):
            return lax.dynamic_slice_in_dim(vec, at_y * width, width)

        vectors = (
            own(sums[6], cols), own(sums[7], cols), sums[3], own(sums[8:].reshape(-1), unit_cols), sums[0],
            sums[4], sums[5], sums[1], sums[2],
        )

    return layer_out, input_grad, *grads, *vectors


def solution(mesh):
    rows = P("dp", "tensor", None)
    weight = P("dp", "tensor")
    cut = P("tensor")
    whole = P()
    return jax.shard_map(
        on_device,
        mesh=mesh,
        in_specs=(rows, rows, whole, whole, *(weight,) * 6, cut, cut, whole, cut, *(whole,) * 5),
        out_specs=(rows, rows, *(weight,) * 6, cut, cut, whole, cut, *(whole,) * 5),
        check_vma=False,
    )
```

```python
import functools

import jax
import jax.numpy as jnp
from jax import lax
from jax.experimental import pallas as pl
from jax.experimental.pallas import tpu as pltpu
from jax.sharding import PartitionSpec as P

HEAD = 64
PAIR = 2 * HEAD
EPSILON = 1e-05
SQRT_HALF = 0.7071067811865476
INV_ROOT_TWO_PI = 0.3989422804014327
BOTH = ("dp", "tensor")
F32 = jnp.float32
BF16 = jnp.bfloat16
TILE = 768
ROWS = 128
HBM = pl.BlockSpec(memory_space=pltpu.HBM)
VMEM = pl.BlockSpec(memory_space=pltpu.VMEM)
SMEM = pl.BlockSpec(memory_space=pltpu.SMEM)
LEN, AT_Z, AT_X, AT_C, AT_Y = range(5)
Y_BIT, C_BIT, X_BIT, Z_BIT = 1, 2, 4, 8


def dot_nn(a, b):
    return lax.dot_general(a, b, (((1,), (0,)), ((), ())), preferred_element_type=F32)


def dot_nt(a, b):
    return lax.dot_general(a, b, (((1,), (1,)), ((), ())), preferred_element_type=F32)


def dot_tn(a, b):
    return lax.dot_general(a, b, (((0,), (0,)), ((), ())), preferred_element_type=F32)


def params(mib):
    return pltpu.CompilerParams(vmem_limit_bytes=mib << 20)


def cost(us):
    return pl.CostEstimate(flops=int(us * 2e7), bytes_accessed=int(us * 6e4), transcendentals=0)


def tie(*values):
    return lax.optimization_barrier(values)


def exchange(value, mask):
    count = lax.axis_size("dp") * lax.axis_size("tensor")
    return lax.ppermute(value, BOTH, [(i, i ^ mask) for i in range(count)])


def in_order(bit_at, mine, other, axis=0):
    low = jnp.where(bit_at == 0, mine, other)
    high = jnp.where(bit_at == 0, other, mine)
    return jnp.stack([low, high], axis=axis)


class Gather:
    def __init__(self, first, second, places):
        self.places = places
        self.a, self.b = first, second

    def along_z(self):
        both = jnp.stack([self.a, self.b])
        self.both = both
        self.got = [exchange(both, m * Z_BIT) for m in (1, 2, 3)]

    def first_side(self):
        at_z = self.places[0]
        both, (g1, g2, g3) = self.both, self.got
        rows = []
        for z in range(4):
            far = jnp.where(at_z == z ^ 2, g2, g3)
            rows.append(jnp.where(at_z == z, both, jnp.where(at_z == z ^ 1, g1, far)))
        self.a = jnp.stack([r[0] for r in rows])
        self.b = jnp.stack([r[1] for r in rows])
        self.got = exchange(self.a, X_BIT), exchange(self.b, Y_BIT)

    def second_side(self):
        self.a = jnp.stack([self.a, self.got[0]])
        self.b = jnp.stack([self.b, self.got[1]])
        self.got = exchange(self.a, Y_BIT), exchange(self.b, X_BIT)
        self.near = exchange(self.a, C_BIT), exchange(self.b, C_BIT)

    def core(self):
        self.far = exchange(self.got[0], C_BIT), exchange(self.got[1], C_BIT)

    def pieces(self):
        return (
            [self.a, self.near[0], self.got[0], self.far[0]],
            [self.b, self.near[1], self.got[1], self.far[1]],
        )


class Mover:
    def __init__(self, sems):
        self.sems, self.used = sems, 0

    def __call__(self, src, dst):
        copy = pltpu.make_async_copy(src, dst, self.sems.at[self.used])
        self.used += 1
        copy.start()
        return copy


def wait(copies):
    for c in copies:
        c.wait()


def load_pieces(move, scalars, pieces, weight, second, spans):
    copies = []
    for number, piece in enumerate(pieces):
        far, other = number // 2, number % 2
        at_c = scalars[AT_C] ^ other
        for inner in range(2):
            if second:
                at_x, at_y = scalars[AT_X] ^ far, scalars[AT_Y] ^ inner
            else:
                at_x, at_y = scalars[AT_X] ^ inner, scalars[AT_Y] ^ far
            for start, width, to in spans:
                column = pl.multiple_of(to(at_y), 128)
                copies.append(
                    move(
                        piece.at[inner, :, :, pl.ds(start, width)],
                        weight.at[:, at_x, at_c, :, pl.ds(column, width)],
                    )
                )
    return copies


def load_whole(move, scalars, pieces, weight, second, spans):
    return [
        move(pieces[0].at[:, :, :, :, pl.ds(start, width)], weight.at[:, :, :, :, pl.ds(to, width)])
        for start, width, to in spans
    ]


def flat(weight):
    return weight.reshape(-1, weight.shape[-1])


def normalize(z):
    mean = jnp.mean(z, axis=-1, keepdims=True)
    center = z - mean
    rscale = lax.rsqrt(jnp.mean(center * center, axis=-1, keepdims=True) + EPSILON)
    return center * rscale, rscale


def norm_backward(e, normal, rscale, gain):
    scaled = e * gain
    mean = jnp.mean(scaled, axis=-1, keepdims=True)
    tilt = jnp.mean(scaled * normal, axis=-1, keepdims=True)
    return rscale * (scaled - mean - normal * tilt)


def column_sum(value):
    return jnp.sum(value, axis=0, keepdims=True)


def odd_lanes(shape):
    return lax.broadcasted_iota(jnp.int32, shape, len(shape) - 1) >= HEAD


def of_head(value, odd):
    mask = odd_lanes(value.shape)
    zero = jnp.zeros_like(value)
    return jnp.where(mask, value, zero) if odd else jnp.where(mask, zero, value)


def pair_of(t):
    return pl.ds(pl.multiple_of(t * PAIR, PAIR), PAIR)


def load_tokens(move, scalars, tokens, other, x):
    half = other.shape[0]
    at = scalars[AT_Y]
    return [
        move(tokens.at[at], x.at[pl.ds(pl.multiple_of(at * half, half), half)]),
        move(other, x.at[pl.ds(pl.multiple_of((1 - at) * half, half), half)]),
    ]


def attend_kernel(load, scalars, tokens, other, vec, *refs):
    first, second, outs, scratch = refs
    move = Mover(scratch[-1])
    x, q, k, v, att, lse, normal, rscale, low, acc, w5 = scratch[:-1]
    copies = load_tokens(move, scalars, tokens, other, x)
    for copy_set in (load[0](move, scalars, first, w5), load[1](move, scalars, second, w5)):
        copies += copy_set
    wait(copies)
    w = flat(w5)
    seq, features = x.shape
    live = lax.broadcasted_iota(jnp.int32, (1, seq), 1) < scalars[LEN]
    scale = HEAD**-0.5
    at_q, at_k, at_v, at_o = (pl.ds(n * features, features) for n in range(4))
    q[...] = ((dot_nn(x[...], w[:, at_q]) + vec[0:1, :]).astype(BF16).astype(F32) * scale).astype(BF16)
    k[...] = dot_nn(x[...], w[:, at_k]).astype(BF16)
    v[...] = (dot_nn(x[...], w[:, at_v]) + vec[1:2, :]).astype(BF16)
    sent = [move(s, o) for s, o in zip((q, k, v), outs[:3])]
    lse[...] = jnp.zeros_like(lse)

    @pl.loop(0, features // PAIR)
    def _(pair):
        here = pair_of(pair)
        q2, k2, v2 = q[:, here], k[:, here], v[:, here]
        column = lax.broadcasted_iota(jnp.int32, lse.shape, 1)
        parts = []
        logs = lse[...]
        for odd in range(2):
            s = jnp.where(live, dot_nt(q2, of_head(k2, odd)), -1e9)
            top = jnp.max(s, axis=-1, keepdims=True)
            e = jnp.exp(s - top)
            total = jnp.sum(e, axis=-1, keepdims=True)
            parts.append(dot_nn(e.astype(BF16), v2) * (1.0 / total))
            logs = jnp.where(column == 2 * pair + odd, top + jnp.log(total), logs)
        lse[...] = logs
        att[:, here] = jnp.where(odd_lanes(parts[0].shape), parts[1], parts[0]).astype(BF16)

    sent += [move(att, outs[3]), move(lse, outs[4])]
    acc[...] = dot_nt(att[...], w[:, at_o])

    @pl.loop(0, seq // ROWS)
    def _(t):
        rows = pl.ds(pl.multiple_of(t * ROWS, ROWS), ROWS)
        n, r = normalize(x[rows, :].astype(F32) + acc[rows, :] + vec[2:3, :])
        normal[rows, :] = n
        rscale[rows, :] = r
        low[rows, :] = (n * vec[3:4, :] + vec[4:5, :]).astype(BF16)

    sent += [move(s, o) for s, o in zip((normal, rscale, low), outs[5:])]
    wait(sent)


def middle_kernel(load, store, scalars, low_in, normal_in, cot_in, vec, up_bias, *refs):
    first, second, outs, (acc, sums, unit_sums), scratch = refs
    out_out, ghid_out, *grad_outs = outs
    move = Mover(scratch[-1])
    low, normal, cot, act, slope, n2, r2, out, gffn, w_up, w_down, grads = scratch[:-1]
    early = [move(low_in, low)] + load[0](move, scalars, first, w_up)
    late = load[1](move, scalars, second, w_down) + [move(normal_in, normal), move(cot_in, cot)]
    up, down = flat(w_up), flat(w_down)
    seq, features = low.shape
    tiles = up.shape[1] // TILE
    cut = 1 + (len(early) // 2 if len(early) > 2 else 1)
    for n, copies in enumerate((early[:cut], early[cut:])):
        wait(copies)

        @pl.loop(0, tiles // 2)
        def _(t):
            at = (scalars[AT_Y] ^ n) * (tiles // 2) + t
            here = pl.ds(pl.multiple_of(at * TILE, TILE), TILE)
            h = dot_nn(low[...], up[:, here]) + up_bias[0:1, here]
            phi = 0.5 + 0.5 * lax.erf(h * SQRT_HALF)
            act[:, here] = (h * phi).astype(BF16)
            slope[:, here] = (phi + h * jnp.exp(-0.5 * h * h) * INV_ROOT_TWO_PI).astype(BF16)

    wait(late)
    acc[...] = dot_nt(act[...], down[...])
    groups, parts, piece, _ = out.shape
    block = seq // parts
    for part in range(parts):
        rows = pl.ds(part * block, block)
        normed = normal[rows, :] * vec[0:1, :] + vec[1:2, :]
        n, r = normalize(normed + acc[rows, :] + vec[2:3, :])
        n2[rows, :] = n
        r2[rows, :] = r
        at = part * block + lax.broadcasted_iota(jnp.int32, (block, 1), 0)
        final = (n * vec[3:4, :] + vec[4:5, :]) * (at < scalars[LEN]).astype(F32)
        out[:, part] = final.astype(BF16).reshape(groups, piece, features)
    sent = [move(out, out_out)]
    total = [jnp.zeros((1, features), F32)] * 3
    for part in range(parts):
        rows = pl.ds(part * block, block)
        at = part * block + lax.broadcasted_iota(jnp.int32, (block, 1), 0)
        e = cot[:, part].reshape(block, features).astype(F32) * (at < scalars[LEN]).astype(F32)
        n = n2[rows, :]
        grad = norm_backward(e, n, r2[rows, :], vec[3:4, :])
        g = grad.astype(BF16)
        acc[rows, :] = grad
        gffn[rows, :] = g
        more = [column_sum(g.astype(F32)), column_sum(e * n), column_sum(e)]
        total = [a + b for a, b in zip(total, more)]
    sums[...] = jnp.concatenate(total, axis=0)

    for n in range(2):

        @pl.loop(n * tiles // 2, (n + 1) * tiles // 2)
        def _(t):
            here = pl.ds(pl.multiple_of(t * TILE, TILE), TILE)
            store(scalars, grads, 1, t, dot_tn(gffn[...], act[:, here]).astype(BF16))

        if len(grad_outs) == 2:
            far = n ^ scalars[AT_Y]
            sent += [move(grads.at[c, 1, far], o.at[1, far]) for c, o in enumerate(grad_outs)]

    for n in range(2):

        @pl.loop(n * tiles // 2, (n + 1) * tiles // 2)
        def _(t):
            here = pl.ds(pl.multiple_of(t * TILE, TILE), TILE)
            g = (dot_nn(gffn[...], down[:, here]) * slope[:, here].astype(F32)).astype(BF16)
            slope[:, here] = g
            unit_sums[0:1, here] = column_sum(g.astype(F32))
            store(scalars, grads, 0, t, dot_tn(low[...], g).astype(BF16))

        done = pl.ds(n * (tiles // 2) * TILE, tiles // 2 * TILE)
        sent.append(move(slope.at[:, done], ghid_out.at[:, done]))
        if len(grad_outs) == 2:
            far = n ^ scalars[AT_Y]
            sent += [move(grads.at[c, 0, :, far], o.at[0, :, far]) for c, o in enumerate(grad_outs)]
    if len(grad_outs) == 1:
        sent.append(move(grads.at[0], grad_outs[0]))
    wait(sent)


def normed_kernel(load, load_out, scalars, ghid_in, second, normal_in, rscale_in, gain, *refs):
    weights, head_weights, _, (first, gattn, gatt, sums), scratch = refs
    move = Mover(scratch[-1])
    ghid, normal, rscale, acc, w_up, w_out = scratch[:-1]
    half = ghid.shape[1] // 2
    parts = [pl.ds(pl.multiple_of((scalars[AT_Y] ^ n) * half, 128), half) for n in range(2)]
    mine, others = ([move(ghid_in.at[:, at], ghid.at[:, at])] for at in parts)
    copies = load(move, scalars, weights, w_up)
    cut = max(len(copies) // 2, 1)
    mine += copies[:cut]
    others += copies[cut:]
    late = [move(s, d) for s, d in ((normal_in, normal), (rscale_in, rscale))]
    last = load_out(move, scalars, head_weights, w_out)
    seq, features = second.shape
    up = flat(w_up)
    wait(mine)
    acc[...] = dot_nt(ghid[:, parts[0]], up[:, parts[0]])
    wait(others)
    acc[...] += dot_nt(ghid[:, parts[1]], up[:, parts[1]])
    wait(late)
    sums[...] = jnp.zeros_like(sums)

    @pl.loop(0, seq // ROWS)
    def _(t):
        rows = pl.ds(pl.multiple_of(t * ROWS, ROWS), ROWS)
        n = normal[rows, :]
        e = acc[rows, :] + second[rows, :]
        grad = norm_backward(e, n, rscale[rows, :], gain[...])
        g = grad.astype(BF16)
        first[rows, :] = grad
        gattn[rows, :] = g
        more = [column_sum(g.astype(F32)), column_sum(e * n), column_sum(e)]
        sums[...] += jnp.concatenate(more, axis=0)

    wait(last)
    gatt[...] = dot_nn(gattn[...], flat(w_out)[...]).astype(BF16)


def last_kernel(load, store, scalars, gatt, gattn, first, *refs):
    ins, (tokens,), (other,), first_pieces, second_pieces, outs, (sums,), scratch = refs
    own_out, other_out, *grad_outs = outs
    move = Mover(scratch[-1])
    q, k, v, att, lse, x, gq, gk, gv, rows_grad, w5, grads = scratch[:-1]
    width = q.shape[1] // 2
    early = [move(ins[4], lse)]
    halves = []
    for at in (pl.ds(0, width), pl.ds(width, width)):
        halves.append([move(s.at[:, at], d.at[:, at]) for s, d in zip(ins, (q, k, v, att))])
    late = load_tokens(move, scalars, tokens, other, x)
    later = load[0](move, scalars, first_pieces, w5) + load[1](move, scalars, second_pieces, w5)
    wait(early)
    seq, features = q.shape
    scale = HEAD**-0.5
    live = lax.broadcasted_iota(jnp.int32, (1, seq), 1) < scalars[LEN]

    def one_pair(pair):
        here = pair_of(pair)
        q2, k2, v2, do2 = q[:, here], k[:, here], v[:, here], gatt[:, here]
        both = do2.astype(F32) * att[:, here].astype(F32)
        column = lax.broadcasted_iota(jnp.int32, lse.shape, 1)
        logs = lse[...]
        q_turned, do_turned = q2.T, do2.T
        for_q, for_k, for_v = [], [], []
        for odd in range(2):
            log = jnp.sum(jnp.where(column == 2 * pair + odd, logs, 0.0), axis=-1, keepdims=True)
            inner = jnp.sum(of_head(both, odd), axis=-1, keepdims=True)
            s = jnp.where(live, dot_nt(q2, of_head(k2, odd)), -1e9)
            p = jnp.exp(s - log)
            gs = (p * (dot_nt(do2, of_head(v2, odd)) - inner)).astype(BF16)
            for_q.append(dot_nn(gs, k2))
            head = slice(odd * HEAD, (odd + 1) * HEAD)
            for_k.append(dot_nn(q_turned[head], gs))
            for_v.append(dot_nn(do_turned[head], p.astype(BF16)))
        g = (jnp.where(odd_lanes(for_q[0].shape), for_q[1], for_q[0]) * scale).astype(BF16)
        gq[:, here] = g
        sums[0:1, here] = column_sum(g.astype(F32))
        gk[:, here] = jnp.concatenate(for_k, axis=0).astype(BF16).T
        g = jnp.concatenate(for_v, axis=0).astype(BF16).T
        gv[:, here] = g
        sums[1:2, here] = column_sum(g.astype(F32))

    pairs_there = features // PAIR // 2
    for n, copies in enumerate(halves):
        wait(copies)
        pl.loop(n * pairs_there, (n + 1) * pairs_there)(one_pair)

    wait(late)
    store(scalars, grads, 0, dot_tn(x[...], gq[...]).astype(BF16))
    store(scalars, grads, 1, dot_tn(x[...], gk[...]).astype(BF16))
    store(scalars, grads, 2, dot_tn(x[...], gv[...]).astype(BF16))
    store(scalars, grads, 3, dot_tn(gattn[...], att[...]).astype(BF16))
    sent = [move(grads.at[n], o) for n, o in enumerate(grad_outs)]
    wait(later)
    w = flat(w5)
    total = first[...]
    for n, g in enumerate((gq, gk, gv)):
        total = total + dot_nt(g[...], w[:, pl.ds(n * features, features)])
    rows_grad[...] = total.astype(BF16)
    half = own_out.shape[0]
    for at, out in ((scalars[AT_Y], own_out), (1 - scalars[AT_Y], other_out)):
        sent.append(move(rows_grad.at[pl.ds(pl.multiple_of(at * half, half), half)], out))
    wait(sent)


def blocks(scalars, rows):
    for at_z in range(4):
        for at_x in range(2):
            for at_c in range(2):
                start = ((at_z * 2 + at_x) * 2 + at_c) * rows
                yield start, at_c ^ scalars[AT_C], at_x ^ scalars[AT_X], at_z ^ scalars[AT_Z]


def store_units(scalars, out, number, t, value):
    rows, width = out.shape[-2:]
    tiles = width // TILE
    col = pl.multiple_of((t % tiles) * TILE, TILE)
    far_y = (t // tiles) ^ scalars[AT_Y]
    for start, far_c, far_x, far_z in blocks(scalars, rows):
        one, two = (far_y, far_x) if number else (far_x, far_y)
        out[far_c, number, one, two, far_z, :, pl.ds(col, TILE)] = value[start : start + rows]


def store_heads(scalars, out, number, value):
    rows, width = out.shape[-2:]
    cols = width // 4
    col = number * cols
    for start, far_c, far_x, far_z in blocks(scalars, rows):
        for at_y in range(2):
            far = far_x * 2 + (at_y ^ scalars[AT_Y])
            piece = value[start : start + rows, at_y * cols : (at_y + 1) * cols]
            out[far_c, far, far_z, :, col : col + cols] = piece


def store_units_whole(scalars, out, number, t, value):
    out[0, number, :, pl.ds(pl.multiple_of(t * TILE, TILE), TILE)] = value


def store_heads_whole(scalars, out, number, value):
    cols = value.shape[1]
    out[0, :, number * cols : (number + 1) * cols] = value


def pick_kernel(scatter, order, src, dst):
    @pl.loop(0, dst.shape[0])
    def _(t):
        if scatter:
            dst[order[t]] = src[t]
        else:
            dst[t] = src[order[t]]


def pick(pieces, order, scatter):
    return pl.pallas_call(
        functools.partial(pick_kernel, scatter),
        out_shape=jax.ShapeDtypeStruct(pieces.shape, pieces.dtype),
        in_specs=[SMEM, VMEM],
        out_specs=VMEM,
        compiler_params=params(4),
        cost_estimate=cost(1),
        name="pick",
    )(order, pieces)


def in_hbm(value):
    return pltpu.with_memory_space_constraint(value, pltpu.HBM)


def in_vmem(value):
    if value.size < 1 << 16:
        return value
    return pltpu.with_memory_space_constraint(value, pltpu.VMEM)


def stays_near(shape):
    return shape if shape.size < 1 << 16 else pltpu.VMEM(shape.shape, shape.dtype)


def run(kernel, name, us, mib, scalars, ins, lists, outs, sums, scratch, sems):
    arrays = [in_vmem(a) if near else in_hbm(a) for a, near in ins] + [in_hbm(a) for some in lists for a in some]
    specs = [VMEM if near else HBM for _, near in ins] + [HBM for some in lists for _ in some]
    groups = [len(some) for some in lists]

    def body(scalars, *refs):
        refs = list(refs)

        def take(n):
            got, refs[:] = refs[:n], refs[n:]
            return got

        singles = take(len(ins))
        grouped = [take(n) for n in groups]
        grouped.append(take(len(outs)))
        if sums:
            grouped.append(take(len(sums)))
        kernel(scalars, *singles, *grouped, refs)

    def buffer(shape):
        return pltpu.VMEM(shape.shape, shape.dtype)

    return pl.pallas_call(
        body,
        out_shape=(*(pltpu.HBM(o.shape, o.dtype) for o in outs), *(stays_near(o) for o in sums)),
        in_specs=[SMEM] + specs,
        out_specs=(HBM,) * len(outs) + (VMEM,) * len(sums),
        scratch_shapes=[*map(buffer, scratch), pltpu.SemaphoreType.DMA((sems,))],
        compiler_params=params(mib),
        cost_estimate=cost(us),
        name=name,
    )(scalars, *arrays)


def add_up(values):
    total = values[0].astype(F32)
    for v in values[1:]:
        total = total + v.astype(F32)
    return total


def pairs(values):
    return (values[0] + values[1]) + (values[2] + values[3])


def split_wide(value):
    high = value.astype(BF16)
    low = (value - high.astype(F32)).astype(BF16)
    space = ((0, 8 - value.shape[0]), (0, 0))
    return jnp.concatenate([jnp.pad(high, space), jnp.pad(low, space)])


def join_wide(rows, count):
    return rows[:count].astype(F32) + rows[8 : 8 + count].astype(F32)


def pairs(values):
    return (values[0] + values[1]) + (values[2] + values[3])


def split_wide(value):
    high = value.astype(BF16)
    low = (value - high.astype(F32)).astype(BF16)
    both = jnp.concatenate([high, low])
    return jnp.pad(both, ((0, -both.shape[0] % 16), (0, 0)))


def join_wide(rows, count):
    return rows[:count].astype(F32) + rows[count : 2 * count].astype(F32)


def finish_kernel(scalars, partial, own, first, second, third, *refs):
    grads, vectors, extra = refs[:4], refs[4:13], refs[13]
    rows = partial.shape[0]
    last = [r[...].astype(F32) for r in (first, second, third)]
    total = partial[...] + last[0][:rows] + last[1][:rows] + last[2][:rows]
    cols = grads[0].shape[1]
    for n, out in enumerate(grads):
        out[...] = total[:, n * cols : (n + 1) * cols]
    low = own[...].astype(F32)
    extra[...] = pairs([r[:8] + r[8:] for r in (low, *(v[rows:] for v in last))])
    features = extra.shape[1] // 2
    at_y = scalars[AT_Y]

    def put(out, row, start):
        out[...] = extra[pl.ds(row, 1), pl.ds(pl.multiple_of(start, 128), out.shape[-1])].reshape(out.shape)

    put(vectors[0], 3, at_y * cols)
    put(vectors[1], 3, features + at_y * cols)
    put(vectors[3], 4 + at_y, 0)
    for out, n in zip((vectors[2], *vectors[4:]), (3, 0, 4, 5, 1, 2)):
        put(out, n // 2, n % 2 * features)


def turn_kernel(keep, near, *refs):
    got, low = refs[:3], refs[3]
    sent, partial, next_low = refs[4:7], refs[7], refs[8]
    a, b, *parts, tails, sems = refs[9:]
    move = Mover(sems)
    blocks, rows, _ = a.shape
    copies = [move(keep.at[0], a), move(near.at[0], b)] + [move(g, p) for g, p in zip(got, parts)]
    wait(copies)
    extra = [low[...]] + [p[blocks * rows :] for p in parts]
    extra = pairs([(lambda v: v[:8] + v[8:])(e.astype(F32)) for e in extra])
    tails[...] = split_wide(extra)
    next_low[...] = tails[...]
    for z in range(blocks):
        at = slice(z * rows, (z + 1) * rows)
        total = a[z].astype(F32) + b[z].astype(F32)
        for p in parts:
            total = total + p[at].astype(F32)
        if z == 0:
            partial[...] = total
        else:
            sent[z - 1][:rows] = total.astype(BF16)
            sent[z - 1][rows:] = tails[...]


class Scatter:
    def __init__(self, keep, send, extra):
        self.keep, self.send, self.extra = keep, send, extra
        self.shape = keep.shape

    def core(self):
        self.got = exchange(self.send, C_BIT), exchange(self.extra, C_BIT)

    def _ready(self, terms):
        self.low = split_wide(self.extra)
        width = self.shape[-1]
        self.sent = [
            jnp.concatenate([add_up([t[m] for t in terms]).astype(BF16).reshape(-1, width), self.low])
            for m in (1, 2, 3)
        ]
        self.terms = [t[0] for t in terms]

    def _go(self, masks):
        self.got = [exchange(s, mask) for s, mask in zip(self.sent, masks)]

    def _came(self):
        rows = self.terms[0].size // self.shape[-1]
        count = self.extra.shape[0]
        self.extra = pairs([join_wide(r, count) for r in (self.low, *(g[rows:] for g in self.got))])
        return [g[:rows].reshape(self.terms[0].shape) for g in self.got]

    def ready_sides(self):
        near, extra = self.got
        self.near = near
        self.extra = self.extra + extra
        self._ready([self.keep, near])

    def sides(self):
        self.got = [exchange(self.sent[0], Y_BIT), exchange(self.sent[1], X_BIT)]

    def corner(self):
        self.got.append(exchange(self.sent[2], X_BIT + Y_BIT))

    def along_z(self):
        blocks, rows, width = self.shape[1:]
        low = jax.ShapeDtypeStruct((16, width), BF16)
        tall = jax.ShapeDtypeStruct((rows + 16, width), BF16)
        part = pltpu.VMEM((blocks, rows, width), BF16)
        *sent, self.partial, self.low = pl.pallas_call(
            turn_kernel,
            out_shape=(*(tall,) * 3, jax.ShapeDtypeStruct((rows, width), F32), low),
            in_specs=[HBM] * 5 + [VMEM],
            out_specs=(VMEM,) * 5,
            scratch_shapes=[
                part, part, *[pltpu.VMEM((blocks * rows + 16, width), BF16)] * 3, pltpu.VMEM((16, width), BF16),
                pltpu.SemaphoreType.DMA((5,)),
            ],
            compiler_params=params(10),
            cost_estimate=cost(2),
            name="turn",
        )(*map(in_hbm, (self.keep, self.near, *self.got)), self.low)
        self.got = [exchange(s, m * Z_BIT) for s, m in zip(sent, (1, 2, 3))]

    def finish(self, scalars, unit_cols, features):
        rows, width = self.shape[-2:]
        cols = width // 4

        def out(*shape):
            return jax.ShapeDtypeStruct(shape, F32)

        vectors = [out(n) for n in (cols, cols, features, unit_cols, *(features,) * 5)]
        return pl.pallas_call(
            finish_kernel,
            out_shape=(*[out(rows, cols)] * 4, *vectors),
            in_specs=[SMEM] + [VMEM] * 5,
            out_specs=(VMEM,) * 13,
            scratch_shapes=[pltpu.VMEM((8, width), F32)],
            compiler_params=params(6),
            cost_estimate=cost(2),
            name="finish",
        )(scalars, self.partial, self.low, *self.got)


def combine_kernel(jobs, *refs):
    refs = list(refs)

    def take(n):
        got, refs[:] = refs[:n], refs[n:]
        return got

    arrays = take(1 + max(n for job in jobs for n, _ in job))
    outs = take(len(jobs))
    move = Mover(refs.pop())
    into = take(len(jobs))
    copies = [
        [[move(arrays[n].at[(*at, b)], ref.at[k, b]) for k, (n, at) in enumerate(job)] for b in range(ref.shape[1])]
        for job, ref in zip(jobs, into)
    ]
    sent = []
    for number, (job, ref, made) in enumerate(zip(jobs, into, refs)):
        for b, some in enumerate(copies[number]):
            wait(some)
            for c in range(ref.shape[2]):
                total = ref[0, b, c].astype(F32)
                for k in range(1, len(job)):
                    total = total + ref[k, b, c].astype(F32)
                made[b, c] = total.astype(BF16)
            sent.append(move(made.at[b], outs[number].at[b]))
    wait(sent)


def combine(name, us, arrays, jobs, shape):
    outs = [jax.ShapeDtypeStruct(shape, BF16)] * len(jobs)
    scratch = [pltpu.VMEM((len(job), *shape), BF16) for job in jobs] + [pltpu.VMEM(shape, BF16)] * len(jobs)
    copies = shape[0] * (sum(map(len, jobs)) + len(jobs))
    return pl.pallas_call(
        functools.partial(combine_kernel, jobs),
        out_shape=[pltpu.HBM(o.shape, o.dtype) for o in outs],
        in_specs=[HBM] * len(arrays),
        out_specs=[HBM] * len(outs),
        scratch_shapes=[*scratch, pltpu.SemaphoreType.DMA((copies,))],
        compiler_params=params(12),
        cost_estimate=cost(us),
        name=name,
    )(*map(in_hbm, arrays))


def along_z_kernel(keep, near, *refs):
    got, sent = refs[:4], refs[4:7]
    parts, made = refs[7], refs[8]
    move = Mover(refs[9])
    copies = []
    far = pl.ds(1, 3)
    for h in range(2):
        terms = (keep.at[h, 0, 0], near.at[h, 0, 0], got[h].at[0], got[2 + h])
        copies.append([move(t.at[far], parts.at[h, k]) for k, t in enumerate(terms)])
    moved = []
    for h in range(2):
        wait(copies[h])
        for m in range(3):
            total = parts[h, 0, m].astype(F32)
            for k in range(1, 4):
                total = total + parts[h, k, m].astype(F32)
            made[m, h] = total.astype(BF16)
            if h:
                moved.append(move(made.at[m], sent[m]))
    wait(moved)


class ScatterTwo:
    def __init__(self, keep, send):
        self.keep, self.send = keep, send

    def core(self):
        self.got = exchange(self.send, C_BIT)

    def first_side(self):
        self.arrays = [self.keep, self.got]
        jobs = [[(n, (h, 1)) for n in range(2)] for h in range(2)]
        sent = combine("first_side", 3, self.arrays, jobs, self.keep.shape[2:])
        self.got = [exchange(s, m) for s, m in zip(sent, (X_BIT, Y_BIT))]

    def second_side(self):
        self.arrays += self.got
        blocks = self.keep.shape[3:]
        jobs = [[(0, (h, 0, 1)), (1, (h, 0, 1)), (2 + h, (1,))] for h in range(2)]
        arrays = [a.reshape(*a.shape[:-3], 2, 2, *a.shape[-2:]) for a in self.arrays]
        sent = combine("second_side", 3, arrays, jobs, (2, 2, *blocks[1:]))
        self.got = [exchange(s, m).reshape(blocks) for s, m in zip(sent, (Y_BIT, X_BIT))]

    def along_z(self):
        self.arrays += self.got
        rows, width = self.keep.shape[-2:]
        out = pltpu.HBM((2, rows, width), BF16)
        sent = pl.pallas_call(
            along_z_kernel,
            out_shape=[out] * 3,
            in_specs=[HBM] * 6,
            out_specs=[HBM] * 3,
            scratch_shapes=[
                pltpu.VMEM((2, 4, 3, rows, width), BF16), pltpu.VMEM((3, 2, rows, width), BF16),
                pltpu.SemaphoreType.DMA((11,)),
            ],
            compiler_params=params(8),
            cost_estimate=cost(3),
            name="along_z",
        )(*map(in_hbm, self.arrays))
        self.got = [exchange(s, m * Z_BIT) for s, m in zip(sent, (1, 2, 3))]

    def total(self):
        sums = []
        for h in range(2):
            terms = [self.arrays[n][h, 0, 0, 0] for n in range(2)] + [self.arrays[2 + h][0, 0], self.arrays[4 + h][0]]
            sums.append(add_up(terms + [g[h] for g in self.got]))
        return sums


def scatter_whole(grad, rows, cols):
    size = lax.axis_size("tensor")
    parts = grad.reshape(-1, rows, size, cols).transpose(0, 2, 1, 3).reshape(-1, cols)
    return lax.psum_scatter(parts, BOTH, scatter_dimension=0, tiled=True).astype(F32)


def gather_whole(shard):
    size = lax.axis_size("tensor")
    rows, cols = shard.shape
    got = lax.all_gather(shard, BOTH, axis=0, tiled=False).reshape(-1, size, rows, cols)
    return got.transpose(0, 2, 1, 3).reshape(1, 1, 1, -1, size * cols)


def deal_start(block):
    micro, half, features = block.shape
    dp = lax.axis_size("dp")
    piece = half // dp
    pieces = block.reshape(micro, dp, piece, features).transpose(1, 0, 2, 3)
    pieces = pieces.reshape(dp, micro * piece, features)
    return lax.all_to_all(pieces, "dp", split_axis=0, concat_axis=0, tiled=True)


def deal_pick(spread, order, micro):
    dp, tall, features = spread.shape
    return pick(spread.reshape(dp * micro, tall // micro, features), order, True)


def deal_finish(chosen):
    got = lax.all_to_all(chosen, BOTH, split_axis=0, concat_axis=0, tiled=True)
    return got.reshape(lax.axis_size("dp"), lax.axis_size("tensor"), *chosen.shape[1:])


def collect_start(pieces):
    dp, size, piece, features = pieces.shape
    pieces = pieces.reshape(dp * size, piece, features)
    return lax.all_to_all(pieces, BOTH, split_axis=0, concat_axis=0, tiled=True)


def collect_pick(got, order):
    return pick(got, order, False)


def collect_start_back(chosen, micro):
    count, piece, features = chosen.shape
    chosen = chosen.reshape(count // micro, micro * piece, features)
    return lax.all_to_all(chosen, "dp", split_axis=0, concat_axis=0, tiled=True)


def collect_end(back, micro):
    dp, tall, features = back.shape
    back = back.reshape(dp, micro, tall // micro, features).transpose(1, 0, 2, 3)
    return back.reshape(micro, -1, features)


def on_device(
    tokens, cotangent, lengths, slot_order,
    query_weight, key_weight, value_weight, out_weight, up_weight, down_weight,
    query_bias, value_bias, out_bias, up_bias, down_bias,
    first_gain, first_offset, second_gain, second_offset,
):
    micro, half, features = tokens.shape
    dp, size = lax.axis_size("dp"), lax.axis_size("tensor")
    assert micro == size == 2
    dp_pos, at_y = lax.axis_index("dp"), lax.axis_index("tensor")
    rows, cols = query_weight.shape
    unit_cols = up_weight.shape[1]
    units = unit_cols * size
    seq = half * size
    at_c, at_x, at_z = dp_pos & 1, (dp_pos >> 1) & 1, dp_pos >> 2
    scalars = jnp.stack([lengths[dp_pos * size + at_y], at_z, at_x, at_c, at_y]).astype(jnp.int32)

    other_half = exchange(lax.dynamic_index_in_dim(tokens, 1 - at_y, 0, keepdims=False), Y_BIT)
    biases = jnp.concatenate([query_bias, value_bias, up_bias]).reshape(-1, cols)
    other_biases = exchange(biases, Y_BIT)

    def act(shape, dtype=BF16):
        return jax.ShapeDtypeStruct(shape, dtype)

    def merged(shapes):
        return act((len(shapes), *shapes[0].shape))

    split = dp == 16 and rows % 16 == 0
    if split:
        dims = (4, 2, 2, rows)
        places = (at_z, at_x, at_c, at_y)
        heads = Gather(
            jnp.concatenate([query_weight, key_weight], axis=1),
            jnp.concatenate([value_weight, out_weight], axis=1), places,
        )
        wide = Gather(up_weight, down_weight, places)
        heads.along_z()
        wide.along_z()
        heads.got, other_half, other_biases = tie(heads.got, other_half, other_biases)
        heads.first_side()
        heads.got, wide.got[:2] = tie(heads.got, wide.got[:2])
        heads.second_side()
        heads.got, wide.got, cotangent = tie(heads.got, wide.got, cotangent)
        heads.core()
        wide.first_side()
        spread = deal_start(cotangent)
        heads_a, heads_b = heads.pieces()
        heads_a, heads_b, wide.got = tie(heads_a, heads_b, wide.got)
        wide.second_side()
        chosen = deal_pick(spread, slot_order, micro)
        heads_a, heads_b, chosen = tie(heads_a, heads_b, chosen)
        cot = deal_finish(chosen)
        unit_spans = [(0, unit_cols, lambda y: y * unit_cols)]
        head_spans = [
            [(m * cols, cols, lambda y, n=2 * h + m: n * features + y * cols) for m in range(2)] for h in range(2)
        ]
        out_spans = [(cols, cols, lambda y: y * cols)]
        load_units = [functools.partial(load_pieces, second=h, spans=unit_spans) for h in range(2)]
        load_heads = [functools.partial(load_pieces, second=h, spans=head_spans[h]) for h in range(2)]
        load_out = functools.partial(load_pieces, second=1, spans=out_spans)
        put_units, put_heads = store_units, store_heads
        unit_grads = [act((2, 2, 2, 4, rows, unit_cols))] * 2
        head_grads = [act((4, 4, rows, 4 * cols))] * 2
    else:
        dims = (1, 1, 1, features)
        heads_a, heads_b = (
            [jnp.concatenate([gather_whole(w) for w in pair], axis=-1)]
            for pair in ((query_weight, key_weight), (value_weight, out_weight))
        )
        up_in, down_in = [gather_whole(up_weight)], [gather_whole(down_weight)]
        load_units = [functools.partial(load_whole, second=0, spans=[(0, units, 0)])] * 2
        load_heads = [
            functools.partial(load_whole, second=0, spans=[(0, 2 * features, h * 2 * features)]) for h in range(2)
        ]
        load_out = functools.partial(load_whole, second=0, spans=[(features, features, 0)])
        cot = deal_finish(deal_pick(deal_start(cotangent), slot_order, micro))
        put_units, put_heads = store_units_whole, store_heads_whole
        unit_grads = [act((2, features, units))]
        head_grads = [act((features, 4 * features))]

    biases = in_order(at_y, biases, other_biases, 1)
    full_query, full_value = biases[0].reshape(-1), biases[1].reshape(-1)
    full_up = biases[2:].transpose(1, 0, 2).reshape(1, units)

    low_rows, tall, column = act((seq, features)), act((seq, features), F32), act((seq, 1), F32)
    logs, low_units = act((seq, 128), F32), act((seq, units))
    head_vec = jnp.stack([full_query, full_value, out_bias, first_gain, first_offset])
    head_weights, unit_weights = act((*dims, 4 * features)), act((*dims, units))

    q, k, v, att, lse, n1, r1, low = run(
        functools.partial(attend_kernel, load_heads), "attend", 15, 24, scalars,
        [(tokens, False), (other_half, False), (head_vec, True)], [heads_a, heads_b],
        [low_rows] * 4 + [logs, tall, column, low_rows], [],
        [low_rows] * 5 + [logs, tall, column, low_rows, tall, head_weights], 48,
    )
    if split:
        low, wide.got, wide.near = tie(low, wide.got, wide.near)
        wide.core()
        up_in, down_in = wide.pieces()
    else:
        cot = cot.transpose(1, 0, 2, 3).reshape(1, size, half, features)

    middle_vec = jnp.stack([first_gain, first_offset, down_bias, second_gain, second_offset])
    dealt = act((dp, size, half // dp, features) if split else (1, size, half, features))
    out, ghid, *wide_grad, second, down_sums, unit_sums = run(
        functools.partial(middle_kernel, load_units, put_units), "middle", 24, 44, scalars,
        [(low, False), (n1, False), (cot, False), (middle_vec, True), (full_up, True)], [up_in, down_in],
        [dealt, low_units, *unit_grads], [tall, act((3, features), F32), act((1, units), F32)],
        [
            low_rows, tall, dealt, low_units, low_units, tall, column, dealt, low_rows,
            unit_weights, unit_weights, merged(unit_grads),
        ], 44,
    )
    if split:
        wide_sum = ScatterTwo(*wide_grad)
        wide_sum.core()
    else:
        out = out.reshape(size, dp, half // dp, features).transpose(1, 0, 2, 3)
    out = collect_start(out)

    if split:
        ghid, second, wide_sum.got = tie(ghid, second, wide_sum.got)
        wide_sum.first_side()
    first, gattn, gatt, up_sums = run(
        functools.partial(normed_kernel, load_units[0], load_out), "normed", 8, 20, scalars,
        [(ghid, False), (second, True), (n1, False), (r1, False), (first_gain[None], True)], [up_in, heads_b],
        [], [tall, low_rows, low_rows, act((3, features), F32)],
        [low_units, tall, column, tall, unit_weights, act((*dims, features))], 40,
    )
    own_grad, other_grad, *head_grad, head_sums = run(
        functools.partial(last_kernel, load_heads, put_heads), "last", 20, 28, scalars,
        [(gatt, True), (gattn, True), (first, True)], [[q, k, v, att, lse], [tokens], [other_half], heads_a, heads_b],
        [act((half, features)), act((half, features)), *head_grads], [act((2, features), F32)],
        [low_rows] * 4 + [logs] + [low_rows] * 5 + [head_weights, merged(head_grads)], 60,
    )
    sums = jnp.concatenate([down_sums, up_sums, head_sums, unit_sums.reshape(-1, features)])
    if split:
        head_grad, other_grad, sums, wide_sum.got, out = tie(head_grad, other_grad, sums, wide_sum.got, out)
        head_sum = Scatter(*head_grad, sums.reshape(-1, unit_cols))
        head_sum.core()
        wide_sum.second_side()
        layer_out = collect_start_back(collect_pick(out, slot_order), micro)
        head_sum.ready_sides()
        head_sum.sent, head_sum.low, wide_sum.got = tie(head_sum.sent, head_sum.low, wide_sum.got)
        head_sum.sides()
        wide_sum.along_z()
        head_sum.corner()
        head_sum.got, wide_sum.got, layer_out, other_grad = tie(
            head_sum.got, wide_sum.got, layer_out, other_grad
        )
        input_grad = in_order(at_y, own_grad, exchange(other_grad, Y_BIT))
        head_sum.along_z()
        layer_out = collect_end(layer_out, micro)
        head_sum.got[0], input_grad = tie(head_sum.got[0], input_grad)
        results = head_sum.finish(scalars, unit_cols, features)
        grads = [*results[:4], *wide_sum.total()]
        vectors = results[4:]
    else:
        layer_out = collect_end(collect_start_back(collect_pick(out, slot_order), micro), micro)
        input_grad = in_order(at_y, own_grad, exchange(other_grad, Y_BIT))
        cut = [head_grad[0][:, n * features : (n + 1) * features] for n in range(4)]
        grads = [scatter_whole(g, rows, cols) for g in cut]
        grads += [scatter_whole(wide_grad[0][n], rows, unit_cols) for n in range(2)]
        sums = lax.psum(sums, BOTH)

        def own(vec, width):
            return lax.dynamic_slice_in_dim(vec, at_y * width, width)

        vectors = (
            own(sums[6], cols), own(sums[7], cols), sums[3], own(sums[8:].reshape(-1), unit_cols), sums[0],
            sums[4], sums[5], sums[1], sums[2],
        )

    return layer_out, input_grad, *grads, *vectors


def solution(mesh):
    rows = P("dp", "tensor", None)
    weight = P("dp", "tensor")
    cut = P("tensor")
    whole = P()
    return jax.shard_map(
        on_device,
        mesh=mesh,
        in_specs=(rows, rows, whole, whole, *(weight,) * 6, cut, cut, whole, cut, *(whole,) * 5),
        out_specs=(rows, rows, *(weight,) * 6, cut, cut, whole, cut, *(whole,) * 5),
        check_vma=False,
    )
```
